128 devices in a mesh: gx: 4 (over y), gy: 4 (over x_lo, core), gz: 8 (over z, x_hi).
Axes of the slice: x: 4 (x_hi: 2, x_lo: 2; x = x_hi * 2 + x_lo), y: 4, z: 4, core: 2. Of those that a mesh axis runs over, the one named last changes fastest.
Arguments:
- forcing: float32 [128, 128, 1024], P('gx', 'gy', 'gz'), may hold values from -6 to 6
- kappa_base: float32 [128, 128, 1024], P('gx', 'gy', 'gz'), may hold values from 0.5 to 2
- labels: int32 [128, 128, 1024], P('gx', 'gy', 'gz'), may hold values from 0 to 3
- contrast: float32 [4], replicated, may hold values from 1 to 100
- channel_weight: float32 [4], replicated, may hold values from 0.25 to 2
- coarse_coef: float32 [4, 4, 8, 64, 8], P('gx', 'gy', 'gz'), may hold values from -6 to 6
- source_link: int32 [4, 4, 8, 40, 4], P('gx', 'gy', 'gz'), may hold values from 0 to 63, as said below
- offsets: int32 [4, 4, 8, 40, 3], P('gx', 'gy', 'gz'), may hold values from 0 to 120, as said below
- live_pieces: int32 [4, 4, 8], P('gx', 'gy', 'gz'), may hold values from 5 to 40, as said below
- resident_bases: float32 [4, 4, 8, 40, 8, 4096], P('gx', 'gy', 'gz'), may hold values from -5 to 5
Outputs:
- update: float32 [128, 128, 1024], P('gx', 'gy', 'gz')
- new_basis: float32 [4, 4, 8, 40, 2, 4096], P('gx', 'gy', 'gz')
The draws below stay inside these ranges and needn't reach their ends.
Inputs may be any that keep to these rules, and one draw needn't show every extreme that they name: `source_link`: each of the three brick offsets of a slot, minus one, leads to a brick inside the mesh; a coefficient slot may be named by several pieces. `offsets`: every piece lies inside its brick's padded frame of (40) x (40) x (136) cells. `live_pieces`: some brick has all 40 slots live in every draw.
All inputs are finite; a program needn't handle non-finite values.
Results may differ from the reference program's by a relative error of at most 0.0003.
Values sent between devices are 32-bit elements; how exact they have to be, the bound alone decides.
A program may use at most 128 MiB of HBM per device.

```python
import math
import jax
import jax.numpy as jnp
from jax import lax

BX = 32
BY = 32
BZ = 128
MARGIN = 4
PIECE = 16
NB = 8
NP = 40
ND = 64
NCH = 4
SWEEPS = 20
NX = 128
NY = 128
NZ = 1024
N_GX = 4
N_GY = 4
N_GZ = 8


def draw_labels(key, part):
    table = jax.random.randint(key, (NX // 2, NY // 2, NZ // 16), 0, NCH)
    spread = jnp.repeat(jnp.repeat(jnp.repeat(table, 2, 0), 2, 1), 16, 2)
    return spread.astype(jnp.int32)


def draw_source_link(key, part):
    key_steps = jax.random.fold_in(key, 11)
    key_slots = jax.random.fold_in(key, 12)
    steps_drawn = jax.random.randint(key_steps, (N_GX, N_GY, N_GZ, NP, 3), -1, 2)
    along_x = jnp.arange(N_GX)[:, None, None, None]
    along_y = jnp.arange(N_GY)[None, :, None, None]
    along_z = jnp.arange(N_GZ)[None, None, :, None]
    columns = []
    for position, extent, column in ((along_x, N_GX, 0), (along_y, N_GY, 1), (along_z, N_GZ, 2)):
        target = jnp.clip(position + steps_drawn[..., column], 0, extent - 1)
        columns.append(target - position + 1)
    slot_column = jax.random.randint(key_slots, (N_GX, N_GY, N_GZ, NP), 0, ND)
    columns.append(slot_column)
    return jnp.stack(columns, -1).astype(jnp.int32)


def draw_offsets(key, part):
    upper = jnp.array([BX + 2 * MARGIN - PIECE + 1, BY + 2 * MARGIN - PIECE + 1, BZ + 2 * MARGIN - PIECE + 1], jnp.int32)
    return jax.random.randint(key, (N_GX, N_GY, N_GZ, NP, 3), 0, upper).astype(jnp.int32)


def draw_live_pieces(key, part):
    key_base = jax.random.fold_in(key, 21)
    key_pick = jax.random.fold_in(key, 22)
    base_counts = jax.random.randint(key_base, (N_GX * N_GY * N_GZ,), NP // 8, NP // 2 + 1)
    chosen = jax.random.randint(key_pick, (), 0, N_GX * N_GY * N_GZ)
    filled = base_counts.at[chosen].set(NP)
    return filled.reshape(N_GX, N_GY, N_GZ).astype(jnp.int32)


def shard_levels(rng, shape, shards, least, largest):
    factor_of, own = 1.0, jax.random.fold_in(rng, 6)
    for dim, parts in shards:
        draws = jnp.exp(jax.random.uniform(jax.random.fold_in(own, dim), (parts,), jnp.float32, least / len(shards), largest / len(shards)))
        factor_of = factor_of * jnp.repeat(draws, shape[dim] // parts).reshape([-1 if axis == dim else 1 for axis in range(len(shape))])
    return factor_of


def normal_values(key, dims, scale, bound, shards=(), held_as=jnp.bfloat16):
    loudness = shard_levels(key, dims, shards, -0.22, 0.18) if shards else 1.0
    result = jax.random.normal(key, dims, jnp.float32) * scale * loudness
    return jnp.minimum(jnp.maximum(result, -bound), bound).astype(held_as)


def setup_inputs(seed: int = 0) -> dict:
    arg_keys = jax.random.split(jax.random.key(seed), 11)
    forcing = normal_values(arg_keys[0], (NX, NY, NZ), 1.0, 6.0, ((0, 4), (1, 4), (2, 8)), jnp.float32)
    kappa_base = jnp.clip(jnp.exp(math.log(2.0) - 1.3862944 * jax.random.uniform(arg_keys[1], (NX, NY, NZ), jnp.float32) ** shard_levels(arg_keys[1], (NX, NY, NZ), ((0, 4), (1, 4), (2, 8)), -0.2, 0.2)), 0.5, 2.0)
    labels = draw_labels(jax.random.fold_in(arg_keys[10], 71), 0)
    contrast = jnp.clip(jnp.exp(jax.random.uniform(arg_keys[3], (NCH,), jnp.float32, math.log(1.0), math.log(100.0))), 1.0, 100.0)
    channel_weight = jnp.clip(jax.random.uniform(arg_keys[4], (NCH,), jnp.float32, 0.25, 2.0), 0.25, 2.0)
    coarse_coef = normal_values(arg_keys[5], (N_GX, N_GY, N_GZ, ND, NB), 1.0, 6.0, ((0, 4), (1, 4), (2, 8)), jnp.float32)
    source_link = draw_source_link(jax.random.fold_in(arg_keys[10], 71), 0)
    offsets = draw_offsets(jax.random.fold_in(arg_keys[10], 71), 0)
    live_pieces = draw_live_pieces(jax.random.fold_in(arg_keys[10], 71), 0)
    resident_bases = normal_values(arg_keys[9], (N_GX, N_GY, N_GZ, NP, NB, PIECE * PIECE * PIECE), 0.35, 5.0, ((0, 4), (1, 4), (2, 8)), jnp.float32)
    return dict(forcing=forcing, kappa_base=kappa_base, labels=labels, contrast=contrast, channel_weight=channel_weight, coarse_coef=coarse_coef, source_link=source_link, offsets=offsets, live_pieces=live_pieces, resident_bases=resident_bases)


damping = 2.0 / 3.0


def lookup(labels, values):
    accumulated = jnp.zeros(labels.shape, values.dtype)
    for channel in range(values.shape[0]):
        accumulated = accumulated + jnp.where(labels == channel, values[channel], 0.0)
    return accumulated


def neighbour(array, axis_number, offset_step):
    selection = [slice(1, -1), slice(1, -1), slice(1, -1)]
    extent = array.shape[axis_number]
    selection[axis_number] = slice(1 + offset_step, extent - 1 + offset_step)
    return array[tuple(selection)]


def apply_operator(values, conductivity, inside):
    centre = values[1:-1, 1:-1, 1:-1]
    centre_kappa = conductivity[1:-1, 1:-1, 1:-1]
    accumulated = jnp.zeros_like(centre)
    for axis_number in range(3):
        for offset_step in (-1, 1):
            beside_values = neighbour(values, axis_number, offset_step)
            beside_kappa = neighbour(conductivity, axis_number, offset_step)
            beside_inside = neighbour(inside, axis_number, offset_step)
            face_value = jnp.where(beside_inside > 0, 0.5 * (centre_kappa + beside_kappa), centre_kappa)
            accumulated = accumulated + face_value * (centre - beside_values)
    return accumulated


def shift_flat(values, stride, upward):
    filler = jnp.zeros(values.shape[:-1] + (stride,), values.dtype)
    if upward:
        return jnp.concatenate([values[..., stride:], filler], -1)
    return jnp.concatenate([filler, values[..., :-stride]], -1)


def local_solve(sources, conductivity, inside):
    flat_index = jnp.arange(PIECE ** 3)
    couplings = []
    diagonal = jnp.zeros_like(conductivity)
    for stride in (PIECE * PIECE, PIECE, 1):
        grid_position = (flat_index // stride) % PIECE
        for upward, allowed in ((True, grid_position < PIECE - 1), (False, grid_position > 0)):
            beside_kappa = shift_flat(conductivity, stride, upward)
            beside_inside = shift_flat(inside, stride, upward) * allowed.astype(inside.dtype)
            face_value = jnp.where(beside_inside > 0, 0.5 * (conductivity + beside_kappa), conductivity)
            diagonal = diagonal + face_value
            couplings.append((stride, upward, jnp.where(beside_inside > 0, face_value, 0.0)))
    divisor = jnp.where(inside > 0, diagonal, 1.0)

    def sweep(sweep_index, solution):
        gathered_terms = jnp.zeros_like(solution)
        for stride, upward, coupling in couplings:
            gathered_terms = gathered_terms + coupling[:, None, :] * shift_flat(solution, stride, upward)
        update_term = sources - (diagonal[:, None, :] * solution - gathered_terms)
        return solution + damping * inside[:, None, :] * update_term / divisor[:, None, :]

    return lax.fori_loop(0, SWEEPS, sweep, jnp.zeros_like(sources))


def tent_weights():
    flat_index = jnp.arange(PIECE ** 3)
    product = jnp.ones((PIECE ** 3,), jnp.float32)
    for stride in (PIECE * PIECE, PIECE, 1):
        grid_position = ((flat_index // stride) % PIECE).astype(jnp.float32)
        product = product * (grid_position + 0.5) * (PIECE - grid_position - 0.5) * (4.0 / (PIECE * PIECE))
    return product


def piece_place(number, live_pieces, offsets):
    device_number = number // NP
    slot_number = number % NP
    brick_x = device_number // (N_GY * N_GZ)
    brick_y = (device_number // N_GZ) % N_GY
    brick_z = device_number % N_GZ
    active = (slot_number < live_pieces[brick_x, brick_y, brick_z]).astype(jnp.float32)
    corner = offsets[brick_x, brick_y, brick_z, slot_number]
    start_cell = ((brick_x * BX + corner[0]).astype(jnp.int32), (brick_y * BY + corner[1]).astype(jnp.int32), (brick_z * BZ + corner[2]).astype(jnp.int32))
    return brick_x, brick_y, brick_z, slot_number, active, start_cell


def reference(forcing, kappa_base, labels, contrast, channel_weight, coarse_coef, source_link, offsets, live_pieces, resident_bases):
    kappa = kappa_base * lookup(labels, contrast)
    weight = lookup(labels, channel_weight)
    cube_shape = (PIECE, PIECE, PIECE)
    total_pieces = N_GX * N_GY * N_GZ * NP
    numbers = jnp.arange(total_pieces, dtype=jnp.int32)
    flat_coef = coarse_coef.reshape(N_GX * N_GY * N_GZ, ND, NB)

    def place_coarse(field_with_halo, number):
        brick_x, brick_y, brick_z, slot_number, active, start_cell = piece_place(number, live_pieces, offsets)
        link_row = source_link[brick_x, brick_y, brick_z, slot_number]
        source_number = ((brick_x + link_row[0] - 1) * N_GY + brick_y + link_row[1] - 1) * N_GZ + brick_z + link_row[2] - 1
        coef_row = flat_coef[source_number, link_row[3]]
        values = jnp.dot(coef_row, resident_bases[brick_x, brick_y, brick_z, slot_number], precision=lax.Precision.HIGHEST) * active
        existing = lax.dynamic_slice(field_with_halo, start_cell, cube_shape)
        return lax.dynamic_update_slice(field_with_halo, existing + values.reshape(cube_shape), start_cell), None

    padded_zero = jnp.zeros((NX + 2 * MARGIN, NY + 2 * MARGIN, NZ + 2 * MARGIN), jnp.float32)
    padded_coarse, _ = lax.scan(place_coarse, padded_zero, numbers)
    coarse_field = padded_coarse[MARGIN:-MARGIN, MARGIN:-MARGIN, MARGIN:-MARGIN]

    ones_field = jnp.ones_like(kappa)
    residual = forcing - apply_operator(jnp.pad(coarse_field, 1), jnp.pad(kappa, 1), jnp.pad(ones_field, 1))

    residual_pad = jnp.pad(residual, MARGIN)
    kappa_pad = jnp.pad(kappa, MARGIN)
    weight_pad = jnp.pad(weight, MARGIN)
    inside_pad = jnp.pad(ones_field, MARGIN)
    tent = tent_weights()

    def enrich(correction, number):
        brick_x, brick_y, brick_z, slot_number, active, start_cell = piece_place(number, live_pieces, offsets)
        residual_piece = lax.dynamic_slice(residual_pad, start_cell, cube_shape).reshape(1, PIECE ** 3)
        kappa_piece = lax.dynamic_slice(kappa_pad, start_cell, cube_shape).reshape(1, PIECE ** 3)
        weight_piece = lax.dynamic_slice(weight_pad, start_cell, cube_shape).reshape(1, PIECE ** 3)
        inside_piece = lax.dynamic_slice(inside_pad, start_cell, cube_shape).reshape(1, PIECE ** 3)
        sources = jnp.stack([residual_piece, residual_piece * weight_piece], 1)
        solved = local_solve(sources, kappa_piece, inside_piece)[0] * active
        spread = (tent * (solved[0] + solved[1])).reshape(cube_shape)
        existing = lax.dynamic_slice(correction, start_cell, cube_shape)
        return lax.dynamic_update_slice(correction, existing + spread, start_cell), solved

    correction, solved_all = lax.scan(enrich, padded_zero, numbers)
    update = coarse_field + correction[MARGIN:-MARGIN, MARGIN:-MARGIN, MARGIN:-MARGIN]
    new_basis = solved_all.reshape(N_GX, N_GY, N_GZ, NP, 2, PIECE ** 3)
    return update, new_basis
```

```python
import jax
import jax.numpy as jnp
from jax import lax
from jax.experimental import pallas as pl
from jax.experimental.pallas import tpu as pltpu
from jax.sharding import PartitionSpec as P

BX = 32
BY = 32
BZ = 128
MARGIN = 4
ND = 64
PIECE=16; NB=8; NP=40; SWEEPS=20
OMEGA = 2.0/3.0
PAIR = 2
VM = pl.BlockSpec(memory_space=pltpu.VMEM)
SM = pl.BlockSpec(memory_space=pltpu.SMEM)
ANY = pl.BlockSpec(memory_space=pl.ANY)

def corner(off, p):
    ox = jnp.clip(off[p, 0], 0, 24)
    oy = jnp.clip(off[p, 1], 0, 24)
    oz = jnp.clip(off[p, 2], 0, 120)
    tile = (oz > 112).astype(jnp.int32)
    return ox, oy, tile, oz - 8 * tile

def rot(v, shift, axis=1):
    return pltpu.roll(v, shift, axis)

def lanes_sub():
    return lax.broadcasted_iota(jnp.int32, (8, 128), 1), lax.broadcasted_iota(jnp.int32, (8, 128), 0)

def prolong_kernel(live_ref, off, coef, basis, acc, buf, sems):
    live = jnp.minimum(live_ref[0], NP)
    def start(p, c):
        pltpu.make_async_copy(basis.at[pl.ds(p*256,256)], buf.at[pl.ds(p*256,256)], sems.at[p]).start()
        return c
    lax.fori_loop(0, live, start, 0)
    acc[...] = jnp.zeros_like(acc)
    lane, sub = lanes_sub()
    def body(p, c):
        ox, oy, tile, lo = corner(off, p)
        pltpu.make_async_copy(basis.at[pl.ds(p*256,256)], buf.at[pl.ds(p*256,256)], sems.at[p]).wait()
        inwin = (lane >= lo) & (lane < lo + 16)
        for yh in range(2):
            for xo in range(2):
                v = None
                for k in range(NB):
                    t = coef[p, k] * buf[pl.ds(p*256 + 128*xo + 8*yh + k, 8, stride=16), :]
                    v = t if v is None else v + t
                for yl in range(8):
                    r = rot(v, lax.rem(lo - 16*yl + 128, 128))
                    acc[tile, oy + 8*yh + yl, pl.ds(ox + 8*xo, 8), :] += jnp.where(inwin, r, 0.0)
        return c
    lax.fori_loop(0, live, body, 0)

def enrich_kernel(live_ref, off, R, K, W, out, corr, cbuf, vbuf, sbuf):
    live = jnp.minimum(live_ref[0], NP)
    corr[...] = jnp.zeros_like(corr)
    lane, sub = lanes_sub()
    group = lane // 16
    zpos = lane % 16
    zw = zpos < 15
    zg = zpos > 0
    yup = lane < 112
    ydn = lane >= 16
    xup = sub < 7
    xdn = sub > 0
    fz = zpos.astype(jnp.float32)
    def tentf(t):
        return (t + 0.5) * (PIECE - t - 0.5) * (4.0 / (PIECE * PIECE))
    tents = {}
    for xp in range(2):
        for yp in range(2):
            tents[xp, yp] = tentf((2*sub + xp).astype(jnp.float32)) * tentf((2*group + yp).astype(jnp.float32)) * tentf(fz)
    par = [(0,0),(0,1),(1,0),(1,1)]

    def prep(p, slot):
        ox, oy, tile, lo = corner(off, p)
        active = jnp.where(p < live, 1.0, 0.0)
        got = []
        for F in (R, K, W):
            d = {}
            for xp, yp in par:
                a = None
                for yh in range(8):
                    row = F[tile, oy + 2*yh + yp, pl.ds(ox + xp, 8, stride=2), :]
                    r = rot(row, lax.rem(16*yh - lo + 128, 128))
                    a = r if a is None else jnp.where(group == yh, r, a)
                d[xp, yp] = a
            got.append(d)
        r, k, w = got
        for i, (xp, yp) in enumerate(par):
            kc = k[xp, yp]
            nbs = [
                (rot(kc, 127), zw), (rot(kc, 1), zg),
                (k[xp, 1-yp], None),
                (rot(k[xp, 1-yp], 16 if yp == 0 else 112), ydn if yp == 0 else yup),
                (k[1-xp, yp], None),
                (rot(k[1-xp, yp], 1 if xp == 0 else 7, 0), xdn if xp == 0 else xup),
            ]
            diag = None
            cs = []
            inside = kc > 0.0
            for nb, m in nbs:
                ok = nb > 0.0
                if m is not None:
                    ok = ok & m
                face = jnp.where(ok, 0.5 * (kc + nb), kc)
                cs.append(jnp.where(ok & inside, face, 0.0))
                diag = face if diag is None else diag + face
            inv = jnp.where(inside, OMEGA / jnp.where(inside, diag, 1.0), 0.0)
            for j, cj in enumerate(cs):
                cbuf[slot, pl.ds((i*6 + j)*8, 8), :] = cj * inv
            b1 = r[xp, yp] * inv * active
            vbuf[slot, pl.ds(i*8, 8), :] = b1
            vbuf[slot, pl.ds((4+i)*8, 8), :] = b1 * w[xp, yp]

    def sweep_piece(vs, slot):
        res = []
        for s in range(2):
            v = {par[i]: vs[s*4+i] for i in range(4)}
            for i, (xp, yp) in enumerate(par):
                c = [cbuf[slot, pl.ds((i*6 + j)*8, 8), :] for j in range(6)]
                vc = v[xp, yp]
                t0 = vbuf[slot, pl.ds((4*s+i)*8, 8), :] + (1.0 - OMEGA) * vc
                t1 = c[0] * rot(vc, 127) + c[1] * rot(vc, 1)
                t2 = c[2] * v[xp, 1-yp] + c[3] * rot(v[xp, 1-yp], 16 if yp == 0 else 112)
                t3 = c[4] * v[1-xp, yp] + c[5] * rot(v[1-xp, yp], 1 if xp == 0 else 7, 0)
                res.append((t0 + t1) + (t2 + t3))
        return res

    idxs = [16*(4*yh2 + group//2) + zpos for yh2 in range(2)]
    gpar = (group % 2) == 0

    def body(g, c):
        for slot in range(PAIR):
            prep(g*PAIR + slot, slot)
        init = tuple(vbuf[slot, pl.ds(n*8, 8), :] for slot in range(PAIR) for n in range(8))
        def sweep(_, vs):
            o = []
            for slot in range(PAIR):
                o += sweep_piece(vs[slot*8:slot*8+8], slot)
            return tuple(o)
        vs = lax.fori_loop(0, SWEEPS - 1, sweep, init)
        for slot in range(PAIR):
            p = g*PAIR + slot
            ox, oy, tile, lo = corner(off, p)
            inwin = (lane >= lo) & (lane < lo + 16)
            v = vs[slot*8:slot*8+8]
            for s in range(2):
                for xp in range(2):
                    for yh2 in range(2):
                        e = jnp.take_along_axis(v[s*4 + 2*xp], idxs[yh2], axis=1)
                        o = jnp.take_along_axis(v[s*4 + 2*xp + 1], idxs[yh2], axis=1)
                        out[pl.ds(p*64 + 4*xp + 2*yh2 + s, 8, stride=8), :] = jnp.where(gpar, e, o)
            for i, (xp, yp) in enumerate(par):
                sp = tents[xp, yp] * (v[i] + v[4+i])
                for yh in range(8):
                    rr = jnp.where(inwin, rot(sp, lax.rem(lo - 16*yh + 128, 128)), 0.0)
                    corr[tile, oy + 2*yh + yp, pl.ds(ox + xp, 8, stride=2), :] += rr
        return c
    ng = (live + PAIR - 1) // PAIR
    lax.fori_loop(0, ng, body, 0)
    def zero(p, c):
        out[pl.ds(p*64, 64), :] = jnp.zeros((64, 128), jnp.float32)
        return c
    lax.fori_loop(ng*PAIR, NP, zero, 0)

def prolong(live, off, coef, basis):
    return pl.pallas_call(prolong_kernel, out_shape=jax.ShapeDtypeStruct((2,40,40,128), jnp.float32),
        in_specs=[SM, SM, SM, ANY], out_specs=VM,
        scratch_shapes=[pltpu.VMEM((NP*256,128), jnp.float32), pltpu.SemaphoreType.DMA((NP,))],
        name="prolong")(live, off, coef, basis)

def enrich(live, off, R, K, W):
    return pl.pallas_call(enrich_kernel,
        out_shape=(jax.ShapeDtypeStruct((NP*64,128), jnp.float32), jax.ShapeDtypeStruct((2,40,40,128), jnp.float32)),
        in_specs=[SM, SM, VM, VM, VM], out_specs=(VM, VM),
        scratch_shapes=[pltpu.VMEM((PAIR,192,128), jnp.float32), pltpu.VMEM((PAIR,64,128), jnp.float32), pltpu.VMEM((8,128), jnp.float32)],
        name="enrich")(live, off, R, K, W)

def basis_rows(rb):
    return rb.reshape(NP,NB,32,128).transpose(0,2,1,3).reshape(NP*256,128)
def out_basis(o):
    return o.reshape(NP,32,2,128).transpose(0,2,1,3).reshape(1,1,1,NP,2,4096)
def extended(array, sides, width):
    for axis, dim in sides:
        count, length = (lax.axis_size(axis), array.shape[dim])
        up = [(i, (i + 1) % count) for i in range(count - 1)]
        down = [(j, i) for i, j in up]
        last = lax.slice_in_dim(array, length - width, length, axis=dim)
        leading = lax.slice_in_dim(array, 0, width, axis=dim)
        before = lax.ppermute(last, axis, up)
        after = lax.ppermute(leading, axis, down)
        array = jnp.concatenate([before, array, after], axis=dim)
    return array


def lookup(labels, values):
    accumulated = jnp.zeros(labels.shape, values.dtype)
    for channel in range(values.shape[0]):
        accumulated = accumulated + jnp.where(labels == channel, values[channel], 0.0)
    return accumulated


def neighbour(array, axis_number, offset_step):
    selection = [slice(1, -1), slice(1, -1), slice(1, -1)]
    extent = array.shape[axis_number]
    selection[axis_number] = slice(1 + offset_step, extent - 1 + offset_step)
    return array[tuple(selection)]


def apply_operator(values, conductivity, inside):
    centre = values[1:-1, 1:-1, 1:-1]
    centre_kappa = conductivity[1:-1, 1:-1, 1:-1]
    accumulated = jnp.zeros_like(centre)
    for axis_number in range(3):
        for offset_step in (-1, 1):
            beside_values = neighbour(values, axis_number, offset_step)
            beside_kappa = neighbour(conductivity, axis_number, offset_step)
            beside_inside = neighbour(inside, axis_number, offset_step)
            face_value = jnp.where(
                beside_inside > 0, 0.5 * (centre_kappa + beside_kappa), centre_kappa
            )
            accumulated = accumulated + face_value * (centre - beside_values)
    return accumulated


def axis_mask(position, extent, depth, whole_extent):
    cells = position * extent - depth + jnp.arange(extent + 2 * depth)
    return ((cells >= 0) & (cells < whole_extent)).astype(jnp.float32)


def domain_mask(depth):
    along_x = axis_mask(lax.axis_index("gx"), BX, depth, BX * lax.axis_size("gx"))
    along_y = axis_mask(lax.axis_index("gy"), BY, depth, BY * lax.axis_size("gy"))
    along_z = axis_mask(lax.axis_index("gz"), BZ, depth, BZ * lax.axis_size("gz"))
    return along_x[:, None, None] * along_y[None, :, None] * along_z[None, None, :]


def fold_margins(field_with_halo):
    halo_width = MARGIN
    holder_array = jnp.concatenate([field_with_halo[:halo_width], field_with_halo[-halo_width:]], 0)
    widened_region = extended(holder_array, (("gx", 0),), halo_width)
    inner_region = field_with_halo[halo_width:-halo_width]
    inner_region = (
        inner_region.at[:halo_width]
        .add(widened_region[:halo_width])
        .at[-halo_width:]
        .add(widened_region[-halo_width:])
    )
    holder_array = jnp.concatenate([inner_region[:, :halo_width], inner_region[:, -halo_width:]], 1)
    widened_region = extended(holder_array, (("gy", 1),), halo_width)
    central_part = inner_region[:, halo_width:-halo_width]
    central_part = (
        central_part.at[:, :halo_width]
        .add(widened_region[:, :halo_width])
        .at[:, -halo_width:]
        .add(widened_region[:, -halo_width:])
    )
    holder_array = jnp.concatenate(
        [central_part[:, :, :halo_width], central_part[:, :, -halo_width:]], 2
    )
    widened_region = extended(holder_array, (("gz", 2),), halo_width)
    inner = central_part[:, :, halo_width:-halo_width]
    inner = (
        inner.at[:, :, :halo_width]
        .add(widened_region[:, :, :halo_width])
        .at[:, :, -halo_width:]
        .add(widened_region[:, :, -halo_width:])
    )
    return inner


def tiles(f):
    t = f.transpose(1, 0, 2)
    return jnp.stack([t[:, :, :128], t[:, :, 8:]])


def untile(t):
    s = jnp.pad(t[0], ((0, 0), (0, 0), (0, 8))) + jnp.pad(t[1], ((0, 0), (0, 0), (8, 0)))
    return s.transpose(1, 0, 2)


def local(forcing, kappa_base, labels, contrast, channel_weight, coarse_coef, source_link, offsets, live_pieces, resident_bases):
    kappa = kappa_base * lookup(labels, contrast)
    weight = lookup(labels, channel_weight)
    link_table = source_link[0, 0, 0]
    everything = lax.all_gather(coarse_coef.reshape(1, ND, NB), ("gx", "gy", "gz"), axis=0, tiled=True)
    source_number = (
        (lax.axis_index("gx") + link_table[:, 0] - 1) * lax.axis_size("gy") + lax.axis_index("gy") + link_table[:, 1] - 1
    ) * lax.axis_size("gz") + lax.axis_index("gz") + link_table[:, 2] - 1
    coef_rows = everything[source_number, link_table[:, 3]]
    live = live_pieces.reshape(1)
    off = offsets[0, 0, 0]
    partial_field = untile(prolong(live, off, coef_rows, basis_rows(resident_bases)))
    coarse_field = fold_margins(partial_field)
    axes = (("gx", 0), ("gy", 1), ("gz", 2))
    field_ext, kappa_ext = extended(coarse_field, axes, 1), extended(kappa, axes, 1)
    residual = forcing - apply_operator(field_ext, kappa_ext, domain_mask(1))
    residual_pad, kappa_pad, weight_pad = (extended(f, axes, MARGIN) for f in (residual, kappa, weight))
    out, corr = enrich(live, off, tiles(residual_pad), tiles(kappa_pad), tiles(weight_pad))
    update = coarse_field + fold_margins(untile(corr))
    return update, out_basis(out)


def solution(mesh):
    return jax.shard_map(
        local,
        mesh=mesh,
        in_specs=(
            P("gx", "gy", "gz"),
            P("gx", "gy", "gz"),
            P("gx", "gy", "gz"),
            P(),
            P(),
            P("gx", "gy", "gz", None, None),
            P("gx", "gy", "gz", None, None),
            P("gx", "gy", "gz", None, None),
            P("gx", "gy", "gz"),
            P("gx", "gy", "gz", None, None, None),
        ),
        out_specs=(P("gx", "gy", "gz"), P("gx", "gy", "gz", None, None, None)),
        check_vma=False,
    )
```

```python
import jax
import jax.numpy as jnp
from jax import lax
from jax.experimental import pallas as pl
from jax.experimental.pallas import tpu as pltpu
from jax.sharding import PartitionSpec as P

ND = 64
PIECE=16; NB=8; NP=40; SWEEPS=20
OMEGA = 2.0/3.0
PAIR = 2
VM = pl.BlockSpec(memory_space=pltpu.VMEM)
SM = pl.BlockSpec(memory_space=pltpu.SMEM)
ANY = pl.BlockSpec(memory_space=pl.ANY)

def corner(off, p):
    ox = jnp.clip(off[p, 0], 0, 24)
    oy = jnp.clip(off[p, 1], 0, 24)
    oz = jnp.clip(off[p, 2], 0, 120)
    tile = (oz > 112).astype(jnp.int32)
    return ox, oy, tile, oz - 8 * tile

def rot(v, shift, axis=1):
    return pltpu.roll(v, shift, axis)

def lanes_sub():
    return lax.broadcasted_iota(jnp.int32, (8, 128), 1), lax.broadcasted_iota(jnp.int32, (8, 128), 0)

MESH = pl.DeviceIdType.MESH
SIZE = {"gx": 4, "gy": 4, "gz": 8}
BIG = 56 * 1024 * 1024


def ring(axis, step):
    n = SIZE[axis]
    return lax.rem(lax.axis_index(axis) + (step + n), n)


def greet(pairs):
    barrier = pltpu.get_barrier_semaphore()
    for axis, step in pairs:
        pl.semaphore_signal(barrier, inc=1, device_id={axis: ring(axis, step)}, device_id_type=MESH)
    pl.semaphore_wait(barrier, len(pairs))


def remote(src, dst, send, recv, i, axis, step):
    copy = pltpu.make_async_remote_copy(
        src_ref=src, dst_ref=dst, send_sem=send.at[i], recv_sem=recv.at[i],
        device_id={axis: ring(axis, step)}, device_id_type=MESH,
    )
    copy.start()
    return copy


def edges(axis):
    i = lax.axis_index(axis)
    return (jnp.where(i > 0, 1.0, 0.0), jnp.where(i < SIZE[axis] - 1, 1.0, 0.0))


def group_row(g, pos):
    return 8 * g - 4 + pos


def share_kernel(coef, forcing, base, labels, con, chw, gat, E, G, zs, zr, yr, yg, xs, xr, xgs, xgr, send, recv):
    ix, iy, iz = lax.axis_index("gx"), lax.axis_index("gy"), lax.axis_index("gz")
    gather = [("gz", s) for s in range(1, 8)] + [("gy", s) for s in range(1, 4)] + [("gx", s) for s in range(1, 4)]
    greet(gather)
    me = (ix * 4 + iy) * 8 + iz
    g1 = [remote(coef.at[0], gat.at[me], send, recv, s - 1, "gz", s) for s in range(1, 8)]
    gat[me] = coef[0]
    lane, sub = lanes_sub()
    E[...] = jnp.zeros_like(E)
    G[...] = jnp.zeros_like(G)

    def fill(y, c):
        for xo in range(4):
            rows = pl.ds(xo * 256 + y, 8, stride=32)
            lab = labels[rows, :]
            kappa = jnp.zeros((8, 128), jnp.float32)
            weight = jnp.zeros((8, 128), jnp.float32)
            for ch in range(4):
                kappa = jnp.where(lab == ch, con[ch], kappa)
                weight = jnp.where(lab == ch, chw[ch], weight)
            E[0, y + 8, pl.ds(8 + 8 * xo, 8), :] = forcing[rows, :]
            E[1, y + 8, pl.ds(8 + 8 * xo, 8), :] = base[rows, :] * kappa
            E[2, y + 8, pl.ds(8 + 8 * xo, 8), :] = weight
        return c

    lax.fori_loop(0, 32, fill, 0)
    yc = [remote(E.at[:, pl.ds(35, 5), pl.ds(8, 32)], yr.at[0], send, recv, 7, "gy", 1),
          remote(E.at[:, pl.ds(8, 5), pl.ds(8, 32)], yr.at[1], send, recv, 8, "gy", -1)]
    lane8 = lane // 8

    def packz(n, c):
        f, q, xo = n // 8, lax.rem(n // 4, 2), lax.rem(n, 4)
        top, bottom = None, None
        for i in range(16):
            v = E[f, 8 + 16 * q + i, pl.ds(pl.multiple_of(8 + 8 * xo, 8), 8), :]
            hi = rot(v, (8 * i + 8) % 128)
            lo = rot(v, (8 * i) % 128) if i else v
            top = hi if i == 0 else jnp.where(lane8 == i, hi, top)
            bottom = lo if i == 0 else jnp.where(lane8 == i, lo, bottom)
        zs[0, f, q, pl.ds(pl.multiple_of(8 * xo, 8), 8), :] = top
        zs[1, f, q, pl.ds(pl.multiple_of(8 * xo, 8), 8), :] = bottom
        return c

    lax.fori_loop(0, 24, packz, 0)
    zc = [remote(zs.at[0], zr.at[0], send, recv, 9, "gz", 1), remote(zs.at[1], zr.at[1], send, recv, 10, "gz", -1)]
    for c in g1:
        c.wait()
    mine = pl.ds((ix * 4 + iy) * 8, 8)
    g2 = [remote(gat.at[mine], gat.at[mine], send, recv, 10 + s, "gy", s) for s in range(1, 4)]

    my, py = edges("gy")
    for c in yc:
        c.wait()

    def addy(n, c):
        f, k = n // 5, lax.rem(n, 5)
        E[f, 3 + k, pl.ds(8, 32), :] = yr[0, f, k] * my
        E[f, 40 + k, pl.ds(8, 32), :] = yr[1, f, k] * py
        return c

    lax.fori_loop(0, 15, addy, 0)

    def stage5(n, c):
        f, y = n // 42, lax.rem(n, 42)
        xs[0, pl.ds(n * 5, 5), :] = E[f, 3 + y, pl.ds(35, 5), :]
        xs[1, pl.ds(n * 5, 5), :] = E[f, 3 + y, pl.ds(8, 5), :]
        return c

    lax.fori_loop(0, 126, stage5, 0)
    xc = [remote(xs.at[0], xr.at[0], send, recv, 14, "gx", 1), remote(xs.at[1], xr.at[1], send, recv, 15, "gx", -1)]
    for c in g2:
        c.wait()
    plane = pl.ds(ix * 32, 32)
    g3 = [remote(gat.at[plane], gat.at[plane], send, recv, 15 + s, "gx", s) for s in range(1, 4)]

    mz, pz = edges("gz")
    for c in zc:
        c.wait()
    lane16 = lane // 16
    low = lax.rem(lane, 16) < 8

    def windows(n, c):
        f, xo = n // 4, lax.rem(n, 4)
        rows = pl.ds(pl.multiple_of(8 * xo, 8), 8)
        src = [[zr[d, f, q, rows, :] * m for q in range(2)] for d, m in ((0, mz), (1, pz))]
        for g in range(1, 6):
            acc = jnp.zeros((8, 128), jnp.float32)
            for pos in range(8):
                y = group_row(g, pos) - 8
                if y < 0 or y > 31:
                    continue
                a = rot(src[0][y // 16], (16 * pos - 8 * (y % 16)) % 128)
                b = rot(src[1][y // 16], (16 * pos + 8 - 8 * (y % 16)) % 128)
                acc = jnp.where(lane16 == pos, jnp.where(low, a, b), acc)
            G[f, g, pl.ds(pl.multiple_of(8 + 8 * xo, 8), 8), :] = acc
        return c

    lax.fori_loop(0, 12, windows, 0)
    wc = [remote(G.at[:, pl.ds(4, 2), pl.ds(8, 32)], yg.at[0], send, recv, 19, "gy", 1),
          remote(G.at[:, pl.ds(1, 2), pl.ds(8, 32)], yg.at[1], send, recv, 20, "gy", -1)]
    mx, px = edges("gx")
    for c in xc:
        c.wait()

    def unstage5(n, c):
        f, y = n // 42, lax.rem(n, 42)
        E[f, 3 + y, pl.ds(3, 5), :] = xr[0, pl.ds(n * 5, 5), :] * mx
        E[f, 3 + y, pl.ds(40, 5), :] = xr[1, pl.ds(n * 5, 5), :] * px
        return c

    lax.fori_loop(0, 126, unstage5, 0)
    for c in wc:
        c.wait()
    for f in range(3):
        for k in range(2):
            G[f, k, pl.ds(8, 32), :] += yg[0, f, k] * my
            G[f, 5 + k, pl.ds(8, 32), :] += yg[1, f, k] * py
    def stageg(n, c):
        f, g = n // 7, lax.rem(n, 7)
        xgs[0, pl.ds(n * 5, 5), :] = G[f, g, pl.ds(35, 5), :]
        xgs[1, pl.ds(n * 5, 5), :] = G[f, g, pl.ds(8, 5), :]
        return c
    lax.fori_loop(0, 21, stageg, 0)
    vc = [remote(xgs.at[0], xgr.at[0], send, recv, 21, "gx", 1), remote(xgs.at[1], xgr.at[1], send, recv, 22, "gx", -1)]
    for c in g3 + vc:
        c.wait()
    def unstageg(n, c):
        f, g = n // 7, lax.rem(n, 7)
        G[f, g, pl.ds(3, 5), :] = xgr[0, pl.ds(n * 5, 5), :] * mx
        G[f, g, pl.ds(40, 5), :] = xgr[1, pl.ds(n * 5, 5), :] * px
        return c
    lax.fori_loop(0, 21, unstageg, 0)


HALO = [("gy", 1), ("gy", -1), ("gx", 1), ("gx", -1), ("gz", 1), ("gz", -1)]


def split_rows(T, ey, rows):
    lane, _ = lanes_sub()
    t0 = rot(T[0, ey, rows, :], 124)
    t1 = rot(T[1, ey, rows, :], 4)
    a = jnp.where(lane < 124, t0, 0.0) + jnp.where(lane >= 4, t1, 0.0)
    m = jnp.where(lane >= 124, t0, jnp.where(lane < 4, t1, 0.0))
    return a, m


def merge_kernel(T, E, W, zs, zr, yr, yw, xs, xr, xws, xwr, send, recv):
    greet(HALO)
    lane, sub = lanes_sub()
    lane16 = lane // 16
    low = lax.rem(lane, 16) < 8
    E[...] = jnp.zeros_like(E)
    W[...] = jnp.zeros_like(W)

    def build(n, c):
        g, xo = 1 + n // 6, lax.rem(n, 6)
        rows = pl.ds(pl.multiple_of(8 * xo, 8), 8)
        nxt, prv, own = None, None, None
        for pos in range(8):
            ey = 8 * g - 4 + pos
            a, m = split_rows(T, ey, rows)
            E[ey, rows, :] = a
            ra = rot(a, (16 * pos + 8) % 128)
            rm = rot(m, (16 * pos + 8) % 128)
            s0, s1 = jnp.where(low, ra, rm), jnp.where(low, rm, ra)
            if pos == 0:
                nxt, prv, own = s0, s1, rm
            else:
                hit = lane16 == pos
                nxt, prv, own = jnp.where(hit, s0, nxt), jnp.where(hit, s1, prv), jnp.where(hit, rm, own)
        zs[0, g - 1, rows, :] = nxt
        zs[1, g - 1, rows, :] = prv
        W[0, g, rows, :] = own
        return c

    lax.fori_loop(0, 30, build, 0)
    yc = [remote(E.at[pl.ds(35, 9)], yr.at[0], send, recv, 0, "gy", 1), remote(E.at[pl.ds(4, 9)], yr.at[1], send, recv, 1, "gy", -1)]
    zc = [remote(zs.at[0], zr.at[0], send, recv, 2, "gz", 1), remote(zs.at[1], zr.at[1], send, recv, 3, "gz", -1)]
    my, py = edges("gy")
    mz, pz = edges("gz")
    mx, px = edges("gx")
    for c in yc:
        c.wait()
    def addy(k, c):
        E[3 + k] += yr[0, k] * my
        E[36 + k] += yr[1, k] * py
        return c
    lax.fori_loop(0, 9, addy, 0)
    def stage(y, c):
        xs[0, pl.ds(y * 9, 9), :] = E[3 + y, pl.ds(35, 9), :]
        xs[1, pl.ds(y * 9, 9), :] = E[3 + y, pl.ds(4, 9), :]
        return c
    lax.fori_loop(0, 42, stage, 0)
    xc = [remote(xs.at[0], xr.at[0], send, recv, 4, "gx", 1), remote(xs.at[1], xr.at[1], send, recv, 5, "gx", -1)]
    for c in zc:
        c.wait()
    def windows(n, c):
        g, xo = n // 6, lax.rem(n, 6)
        rows = pl.ds(pl.multiple_of(8 * xo, 8), 8)
        x, y = zr[0, g, rows, :] * mz, zr[1, g, rows, :] * pz
        W[0, g + 1, rows, :] += jnp.where(low, x, y)
        W[1, g + 1, rows, :] = jnp.where(low, y, x)
        return c
    lax.fori_loop(0, 30, windows, 0)
    wc = [remote(W.at[:, pl.ds(4, 2)], yw.at[0], send, recv, 6, "gy", 1), remote(W.at[:, pl.ds(1, 2)], yw.at[1], send, recv, 7, "gy", -1)]
    for c in wc:
        c.wait()
    for w in range(2):
        for k in range(2):
            W[w, k] += yw[0, w, k] * my
            W[w, 5 + k] += yw[1, w, k] * py
    def stagew(n, c):
        w, g = n // 7, lax.rem(n, 7)
        xws[0, pl.ds(n * 9, 9), :] = W[w, g, pl.ds(35, 9), :]
        xws[1, pl.ds(n * 9, 9), :] = W[w, g, pl.ds(4, 9), :]
        return c
    lax.fori_loop(0, 14, stagew, 0)
    vc = [remote(xws.at[0], xwr.at[0], send, recv, 8, "gx", 1), remote(xws.at[1], xwr.at[1], send, recv, 9, "gx", -1)]
    for c in xc:
        c.wait()
    def unstage(y, c):
        E[3 + y, pl.ds(3, 9), :] += xr[0, pl.ds(y * 9, 9), :] * mx
        E[3 + y, pl.ds(36, 9), :] += xr[1, pl.ds(y * 9, 9), :] * px
        return c
    lax.fori_loop(0, 42, unstage, 0)
    for c in vc:
        c.wait()
    def unstagew(n, c):
        w, g = n // 7, lax.rem(n, 7)
        W[w, g, pl.ds(3, 9), :] += xwr[0, pl.ds(n * 9, 9), :] * mx
        W[w, g, pl.ds(36, 9), :] += xwr[1, pl.ds(n * 9, 9), :] * px
        return c
    lax.fori_loop(0, 14, unstagew, 0)


def fold_kernel(T, C, upd, E, zs, zr, yr, xs, xr, send, recv):
    greet(HALO)
    lane, sub = lanes_sub()
    lane8 = lane // 8

    def build(n, c):
        q, xo = n // 6, lax.rem(n, 6)
        rows = pl.ds(pl.multiple_of(8 * xo, 8), 8)
        nxt, prv = None, None
        for i in range(16):
            ey = 4 + 16 * q + i
            a, m = split_rows(T, ey, rows)
            E[ey, rows, :] = a
            hi = rot(m, (8 * i) % 128) if i else m
            lo = rot(m, (8 * i + 8) % 128)
            nxt = hi if i == 0 else jnp.where(lane8 == i, hi, nxt)
            prv = lo if i == 0 else jnp.where(lane8 == i, lo, prv)
        zs[0, q, rows, :] = nxt
        zs[1, q, rows, :] = prv
        return c

    lax.fori_loop(0, 18, build, 0)
    zc = [remote(zs.at[0], zr.at[0], send, recv, 0, "gz", 1), remote(zs.at[1], zr.at[1], send, recv, 1, "gz", -1)]
    my, py = edges("gy")
    mz, pz = edges("gz")
    mx, px = edges("gx")
    for c in zc:
        c.wait()
    def addz(n, c):
        q, xo = n // 6, lax.rem(n, 6)
        rows = pl.ds(pl.multiple_of(8 * xo, 8), 8)
        x, y = zr[0, q, rows, :] * mz, zr[1, q, rows, :] * pz
        for i in range(16):
            a = rot(x, (128 - 8 * i) % 128) if i else x
            b = rot(y, (120 - 8 * i) % 128)
            E[4 + 16 * q + i, rows, :] += jnp.where(lane < 8, a, jnp.where(lane >= 120, b, 0.0))
        return c
    lax.fori_loop(0, 18, addz, 0)
    yc = [remote(E.at[pl.ds(40, 4)], yr.at[0], send, recv, 2, "gy", 1), remote(E.at[pl.ds(4, 4)], yr.at[1], send, recv, 3, "gy", -1)]
    for c in yc:
        c.wait()
    for k in range(4):
        E[8 + k] += yr[0, k] * my
        E[36 + k] += yr[1, k] * py
    def stage(y, c):
        xs[0, pl.ds(y * 4, 4), :] = E[8 + y, pl.ds(40, 4), :]
        xs[1, pl.ds(y * 4, 4), :] = E[8 + y, pl.ds(4, 4), :]
        return c
    lax.fori_loop(0, 32, stage, 0)
    xc = [remote(xs.at[0], xr.at[0], send, recv, 4, "gx", 1), remote(xs.at[1], xr.at[1], send, recv, 5, "gx", -1)]
    for c in xc:
        c.wait()
    def finish(y, c):
        E[8 + y, pl.ds(8, 4), :] += xr[0, pl.ds(y * 4, 4), :] * mx
        E[8 + y, pl.ds(36, 4), :] += xr[1, pl.ds(y * 4, 4), :] * px
        for xo in range(4):
            upd[pl.ds(xo * 256 + y, 8, stride=32), :] = C[y, pl.ds(8 * xo, 8), :] + E[8 + y, pl.ds(8 + 8 * xo, 8), :]
        return c
    lax.fori_loop(0, 32, finish, 0)


def f32(*shape):
    return jax.ShapeDtypeStruct(shape, jnp.float32)


def vmem(*shape):
    return pltpu.VMEM(shape, jnp.float32)


def params(cid):
    return pltpu.CompilerParams(collective_id=cid, has_side_effects=True, vmem_limit_bytes=BIG)


def share(coef, forcing, base, labels, con, chw):
    return pl.pallas_call(
        share_kernel, out_shape=(f32(128, 4, 128), f32(3, 48, 48, 128), f32(3, 7, 48, 128)),
        in_specs=[VM, VM, VM, VM, SM, SM], out_specs=(VM, VM, VM),
        scratch_shapes=[vmem(2, 3, 2, 32, 128), vmem(2, 3, 2, 32, 128), vmem(2, 3, 5, 32, 128), vmem(2, 3, 2, 32, 128),
                        vmem(2, 632, 128), vmem(2, 632, 128), vmem(2, 112, 128), vmem(2, 112, 128),
                        pltpu.SemaphoreType.DMA((23,)), pltpu.SemaphoreType.DMA((23,))],
        compiler_params=params(0), name="share")(coef, forcing, base, labels, con, chw)


def merge(T):
    return pl.pallas_call(
        merge_kernel, out_shape=(f32(48, 48, 128), f32(2, 7, 48, 128)), in_specs=[VM], out_specs=(VM, VM),
        scratch_shapes=[vmem(2, 5, 48, 128), vmem(2, 5, 48, 128), vmem(2, 9, 48, 128), vmem(2, 2, 2, 48, 128),
                        vmem(2, 384, 128), vmem(2, 384, 128), vmem(2, 128, 128), vmem(2, 128, 128),
                        pltpu.SemaphoreType.DMA((10,)), pltpu.SemaphoreType.DMA((10,))],
        compiler_params=params(1), name="merge")(T)


def fold(T, C):
    return pl.pallas_call(
        fold_kernel, out_shape=f32(1024, 128), in_specs=[VM, VM], out_specs=VM,
        scratch_shapes=[vmem(52, 48, 128), vmem(2, 3, 48, 128), vmem(2, 3, 48, 128), vmem(2, 4, 48, 128),
                        vmem(2, 128, 128), vmem(2, 128, 128),
                        pltpu.SemaphoreType.DMA((6,)), pltpu.SemaphoreType.DMA((6,))],
        compiler_params=params(2), name="fold")(T, C)


def prolong_kernel(live_ref, off, link, gat, basis, acc, buf, sems):
    live = jnp.clip(live_ref[0], 0, NP)

    def fetch(p):
        return pltpu.make_async_copy(basis.at[pl.ds(p * 256, 256)], buf.at[pl.ds(p * 256, 256)], sems.at[p])

    def start(p, c):
        fetch(p).start()
        return c

    lax.fori_loop(0, live, start, 0)
    acc[...] = jnp.zeros_like(acc)
    lane, sub = lanes_sub()
    ix, iy, iz = lax.axis_index("gx"), lax.axis_index("gy"), lax.axis_index("gz")

    def body(p, c):
        ox, oy, tile, lo = corner(off, p)
        owner = ((ix + link[p, 0] - 1) * 4 + iy + link[p, 1] - 1) * 8 + iz + link[p, 2] - 1
        owner = jnp.clip(owner, 0, 127)
        slot = jnp.clip(link[p, 3], 0, ND - 1)
        row = jnp.broadcast_to(gat[owner, pl.ds(slot // 16, 1), :], (8, 128))
        row = rot(row, lax.rem(128 - 8 * lax.rem(slot, 16), 128))
        ck = [jnp.broadcast_to(row[:, k : k + 1], (8, 128)) for k in range(NB)]
        fetch(p).wait()
        inwin = (lane >= lo) & (lane < lo + 16)
        for yh in range(2):
            for xo in range(2):
                v = None
                for k in range(NB):
                    t = ck[k] * buf[pl.ds(p * 256 + 128 * xo + 8 * yh + k, 8, stride=16), :]
                    v = t if v is None else v + t
                for yl in range(8):
                    r = rot(v, lax.rem(lo - 16 * yl + 128, 128))
                    acc[tile, oy + 4 + 8 * yh + yl, pl.ds(ox + 4 + 8 * xo, 8), :] += jnp.where(inwin, r, 0.0)
        return c

    lax.fori_loop(0, live, body, 0)


def residual_stage(E, G, Ec, Wc, R, K, W, gk, C, gc, inner):
    lane, sub = lanes_sub()
    near = (lane < 8) | (lane >= 120)

    def unpack(n, c):
        g, xo = n // 6, lax.rem(n, 6)
        rows = pl.ds(pl.multiple_of(8 * xo, 8), 8)
        gs, cs, ks = Wc[0, g, rows, :], Wc[1, g, rows, :], G[1, g, rows, :]
        for pos in range(8):
            ey = group_row(g, pos) + 4
            s = (120 - 16 * pos) % 128
            gc[ey, rows, :] = rot(gs, s)
            gk[ey, rows, :] = rot(ks, s)
            C[ey, rows, :] = Ec[jnp.clip(ey - 4, 0, 47), rows, :] + jnp.where(near, rot(cs, s), 0.0)
        return c

    lax.fori_loop(0, 42, unpack, 0)

    def pair(cv, kv, nc, nk):
        inside = nk > 0.0
        return jnp.where(inside, 0.5 * (kv + nk) * (cv - nc), kv * cv)

    def build(n, c):
        g, xo = 1 + n // 5, lax.rem(n, 5)
        x0 = 4 + 8 * xo
        rows, before, after = pl.ds(x0, 8), pl.ds(x0 - 1, 8), pl.ds(x0 + 1, 8)
        gf, gw = G[0, g, rows, :], G[2, g, rows, :]
        for pos in range(8):
            ey = group_row(g, pos) + 4
            s = (120 - 16 * pos) % 128
            cv, gv = C[ey, rows, :], gc[ey, rows, :]
            kv, hv = E[1, ey - 4, rows, :], gk[ey, rows, :]
            cu, cd, gu, gd = rot(cv, 127), rot(cv, 1), rot(gv, 127), rot(gv, 1)
            ku, kd, hu, hd = rot(kv, 127), rot(kv, 1), rot(hv, 127), rot(hv, 1)
            last, first = lane == 127, lane == 0
            r = E[0, ey - 4, rows, :]
            r = r - pair(cv, kv, jnp.where(last, gu, cu), jnp.where(last, hu, ku))
            r = r - pair(cv, kv, jnp.where(first, gd, cd), jnp.where(first, hd, kd))
            q = rot(gf, s)
            q = q - pair(gv, hv, jnp.where(last, cu, gu), jnp.where(last, ku, hu))
            q = q - pair(gv, hv, jnp.where(first, cd, gd), jnp.where(first, kd, hd))
            for dy, rr in ((-1, rows), (1, rows), (0, before), (0, after)):
                r = r - pair(cv, kv, C[ey + dy, rr, :], E[1, ey - 4 + dy, rr, :])
                q = q - pair(gv, hv, gc[ey + dy, rr, :], gk[ey + dy, rr, :])
            head, tail = lane < 4, lane >= 124
            py, px = ey - 8, pl.ds(pl.multiple_of(8 * xo, 8), 8)
            wv = E[2, ey - 4, rows, :]
            R[0, py, px, :] = jnp.where(head, rot(q, 4), rot(r, 4))
            R[1, py, px, :] = jnp.where(tail, rot(q, 124), rot(r, 124))
            K[0, py, px, :] = jnp.where(head, rot(hv, 4), rot(kv, 4))
            K[1, py, px, :] = jnp.where(tail, rot(hv, 124), rot(kv, 124))
            W[0, py, px, :] = jnp.where(head, rot(gw, (s + 4) % 128), rot(wv, 4))
            W[1, py, px, :] = jnp.where(tail, rot(gw, (s + 124) % 128), rot(wv, 124))
        return c

    lax.fori_loop(0, 25, build, 0)

    def keep(y, c):
        inner[y] = C[y + 12, pl.ds(8, 32), :]
        return c

    lax.fori_loop(0, 32, keep, 0)


def enrich_kernel(live_ref, off, E, G, Ec, Wc, out, corr, inner, R, K, W, gk, C, gc, cbuf, vbuf):
    residual_stage(E, G, Ec, Wc, R, K, W, gk, C, gc, inner)
    live = jnp.clip(live_ref[0], 0, NP)
    corr[...] = jnp.zeros_like(corr)
    lane, sub = lanes_sub()
    group = lane // 16
    zpos = lane % 16
    zw = zpos < 15
    zg = zpos > 0
    yup = lane < 112
    ydn = lane >= 16
    xup = sub < 7
    xdn = sub > 0
    fz = zpos.astype(jnp.float32)
    def tentf(t):
        return (t + 0.5) * (PIECE - t - 0.5) * (4.0 / (PIECE * PIECE))
    tents = {}
    for xp in range(2):
        for yp in range(2):
            tents[xp, yp] = tentf((2*sub + xp).astype(jnp.float32)) * tentf((2*group + yp).astype(jnp.float32)) * tentf(fz)
    par = [(0,0),(0,1),(1,0),(1,1)]

    def prep(p, slot):
        ox, oy, tile, lo = corner(off, p)
        active = jnp.where(p < live, 1.0, 0.0)
        got = []
        for F in (R, K, W):
            d = {}
            for xp, yp in par:
                a = None
                for yh in range(8):
                    row = F[tile, oy + 2*yh + yp, pl.ds(ox + xp, 8, stride=2), :]
                    r = rot(row, lax.rem(16*yh - lo + 128, 128))
                    a = r if a is None else jnp.where(group == yh, r, a)
                d[xp, yp] = a
            got.append(d)
        r, k, w = got
        for i, (xp, yp) in enumerate(par):
            kc = k[xp, yp]
            nbs = [
                (rot(kc, 127), zw), (rot(kc, 1), zg),
                (k[xp, 1-yp], None),
                (rot(k[xp, 1-yp], 16 if yp == 0 else 112), ydn if yp == 0 else yup),
                (k[1-xp, yp], None),
                (rot(k[1-xp, yp], 1 if xp == 0 else 7, 0), xdn if xp == 0 else xup),
            ]
            diag = None
            cs = []
            inside = kc > 0.0
            for nb, m in nbs:
                ok = nb > 0.0
                if m is not None:
                    ok = ok & m
                face = jnp.where(ok, 0.5 * (kc + nb), kc)
                cs.append(jnp.where(ok & inside, face, 0.0))
                diag = face if diag is None else diag + face
            inv = jnp.where(inside, OMEGA / jnp.where(inside, diag, 1.0), 0.0)
            for j, cj in enumerate(cs):
                cbuf[slot, pl.ds((i*6 + j)*8, 8), :] = cj * inv
            b1 = r[xp, yp] * inv * active
            vbuf[slot, pl.ds(i*8, 8), :] = b1
            vbuf[slot, pl.ds((4+i)*8, 8), :] = b1 * w[xp, yp]

    def sweep_piece(vs, slot):
        res = []
        for s in range(2):
            v = {par[i]: vs[s*4+i] for i in range(4)}
            for i, (xp, yp) in enumerate(par):
                c = [cbuf[slot, pl.ds((i*6 + j)*8, 8), :] for j in range(6)]
                vc = v[xp, yp]
                t0 = vbuf[slot, pl.ds((4*s+i)*8, 8), :] + (1.0 - OMEGA) * vc
                t1 = c[0] * rot(vc, 127) + c[1] * rot(vc, 1)
                t2 = c[2] * v[xp, 1-yp] + c[3] * rot(v[xp, 1-yp], 16 if yp == 0 else 112)
                t3 = c[4] * v[1-xp, yp] + c[5] * rot(v[1-xp, yp], 1 if xp == 0 else 7, 0)
                res.append((t0 + t1) + (t2 + t3))
        return res

    idxs = [16*(4*yh2 + group//2) + zpos for yh2 in range(2)]
    gpar = (group % 2) == 0

    def body(g, c):
        for slot in range(PAIR):
            prep(g*PAIR + slot, slot)
        init = tuple(vbuf[slot, pl.ds(n*8, 8), :] for slot in range(PAIR) for n in range(8))
        def sweep(_, vs):
            o = []
            for slot in range(PAIR):
                o += sweep_piece(vs[slot*8:slot*8+8], slot)
            return tuple(o)
        vs = lax.fori_loop(0, SWEEPS - 1, sweep, init)
        for slot in range(PAIR):
            p = g*PAIR + slot
            ox, oy, tile, lo = corner(off, p)
            inwin = (lane >= lo) & (lane < lo + 16)
            v = vs[slot*8:slot*8+8]
            for s in range(2):
                for xp in range(2):
                    for yh2 in range(2):
                        e = jnp.take_along_axis(v[s*4 + 2*xp], idxs[yh2], axis=1)
                        o = jnp.take_along_axis(v[s*4 + 2*xp + 1], idxs[yh2], axis=1)
                        out[pl.ds(p*64 + 4*xp + 2*yh2 + s, 8, stride=8), :] = jnp.where(gpar, e, o)
            for i, (xp, yp) in enumerate(par):
                sp = tents[xp, yp] * (v[i] + v[4+i])
                for yh in range(8):
                    rr = jnp.where(inwin, rot(sp, lax.rem(lo - 16*yh + 128, 128)), 0.0)
                    corr[tile, oy + 4 + 2*yh + yp, pl.ds(ox + 4 + xp, 8, stride=2), :] += rr
        return c
    ng = (live + PAIR - 1) // PAIR
    lax.fori_loop(0, ng, body, 0)
    def zero(p, c):
        out[pl.ds(p*64, 64), :] = jnp.zeros((64, 128), jnp.float32)
        return c
    lax.fori_loop(ng*PAIR, NP, zero, 0)


def prolong(live, off, link, gat, basis):
    return pl.pallas_call(
        prolong_kernel, out_shape=f32(2, 52, 48, 128), in_specs=[SM, SM, SM, VM, ANY], out_specs=VM,
        scratch_shapes=[vmem(NP * 256, 128), pltpu.SemaphoreType.DMA((NP,))],
        compiler_params=pltpu.CompilerParams(vmem_limit_bytes=BIG), name="prolong")(live, off, link, gat, basis)


def enrich(live, off, E, G, Ec, Wc):
    return pl.pallas_call(
        enrich_kernel, out_shape=(f32(NP * 64, 128), f32(2, 52, 48, 128), f32(32, 32, 128)),
        in_specs=[SM, SM, VM, VM, VM, VM], out_specs=(VM, VM, VM),
        scratch_shapes=[vmem(2, 40, 40, 128), vmem(2, 40, 40, 128), vmem(2, 40, 40, 128),
                        vmem(56, 48, 128), vmem(56, 48, 128), vmem(56, 48, 128), vmem(PAIR, 192, 128), vmem(PAIR, 64, 128)],
        compiler_params=pltpu.CompilerParams(vmem_limit_bytes=BIG), name="enrich")(live, off, E, G, Ec, Wc)


def basis_rows(rb):
    return rb.reshape(NP, NB, 32, 128).transpose(0, 2, 1, 3).reshape(NP * 256, 128)


def out_basis(o):
    return o.reshape(NP, 32, 2, 128).transpose(0, 2, 1, 3).reshape(1, 1, 1, NP, 2, 4096)


def local(forcing, kappa_base, labels, contrast, channel_weight, coarse_coef, source_link, offsets, live_pieces, resident_bases):
    live = live_pieces.reshape(1)
    off = offsets[0, 0, 0]
    link = source_link[0, 0, 0]
    gat, E, G = share(
        coarse_coef.reshape(1, 4, 128), forcing.reshape(1024, 128), kappa_base.reshape(1024, 128), labels.reshape(1024, 128),
        contrast, channel_weight)
    T = prolong(live, off, link, gat, basis_rows(resident_bases))
    Ec, Wc = merge(T)
    out, corr, inner = enrich(live, off, E, G, Ec, Wc)
    return fold(corr, inner).reshape(32, 32, 128), out_basis(out)


def solution(mesh):
    return jax.shard_map(
        local,
        mesh=mesh,
        in_specs=(
            P("gx", "gy", "gz"),
            P("gx", "gy", "gz"),
            P("gx", "gy", "gz"),
            P(),
            P(),
            P("gx", "gy", "gz", None, None),
            P("gx", "gy", "gz", None, None),
            P("gx", "gy", "gz", None, None),
            P("gx", "gy", "gz"),
            P("gx", "gy", "gz", None, None, None),
        ),
        out_specs=(P("gx", "gy", "gz"), P("gx", "gy", "gz", None, None, None)),
        check_vma=False,
    )
```

```python
import jax
import jax.numpy as jnp
from jax import lax
from jax.experimental import pallas as pl
from jax.experimental.pallas import tpu as pltpu
from jax.sharding import PartitionSpec as P

ND = 64
PIECE=16; NB=8; NP=40; SWEEPS=20
OMEGA = 2.0/3.0
PAIR = 8
VM = pl.BlockSpec(memory_space=pltpu.VMEM)
SM = pl.BlockSpec(memory_space=pltpu.SMEM)
ANY = pl.BlockSpec(memory_space=pl.ANY)

def corner(off, p):
    ox = jnp.clip(off[0, 0, p], 0, 24)
    oy = jnp.clip(off[1, 0, p], 0, 24)
    oz = jnp.clip(off[2, 0, p], 0, 120)
    tile = (oz > 112).astype(jnp.int32)
    return ox, oy, tile, oz - 8 * tile

def rot(v, shift, axis=1):
    return pltpu.roll(v, shift, axis)

def lanes_sub():
    return lax.broadcasted_iota(jnp.int32, (8, 128), 1), lax.broadcasted_iota(jnp.int32, (8, 128), 0)

MESH = pl.DeviceIdType.MESH
SIZE = {"gx": 4, "gy": 4, "gz": 8}
BIG = 56 * 1024 * 1024


def ring(axis, step):
    n = SIZE[axis]
    return lax.rem(lax.axis_index(axis) + (step + n), n)


def greet(pairs):
    barrier = pltpu.get_barrier_semaphore()
    for axis, step in pairs:
        pl.semaphore_signal(barrier, inc=1, device_id={axis: ring(axis, step)}, device_id_type=MESH)
    pl.semaphore_wait(barrier, len(pairs))


def remote(src, dst, send, recv, i, axis, step):
    copy = pltpu.make_async_remote_copy(
        src_ref=src, dst_ref=dst, send_sem=send.at[i], recv_sem=recv.at[i],
        device_id={axis: ring(axis, step)}, device_id_type=MESH,
    )
    copy.start()
    return copy


def edges(axis):
    i = lax.axis_index(axis)
    return (jnp.where(i > 0, 1.0, 0.0), jnp.where(i < SIZE[axis] - 1, 1.0, 0.0))


def group_row(g, pos):
    return 8 * g - 4 + pos


def share_kernel(coef, forcing, base, labels, con, chw, gat, E, G, tile, col, zs, zr, yr, yg, xs, xr, xc, xg, send, recv):
    ix, iy, iz = lax.axis_index("gx"), lax.axis_index("gy"), lax.axis_index("gz")
    lane, sub = lanes_sub()
    tile[...] = jnp.zeros_like(tile)
    tile[0:8, 0:64] = coef[...]
    greet([("gz", s) for s in range(1, 8)] + [("gy", s) for s in range(1, 4)] + [("gx", s) for s in range(1, 4)])
    g1 = [remote(tile, col.at[iz], send, recv, s - 1, "gz", s) for s in range(1, 8)]
    col[iz] = tile[...]

    def fill(x, c):
        for yo in range(4):
            rows = pl.ds(pl.multiple_of(x * 32 + 8 * yo, 8), 8)
            lab = labels[rows, :]
            kappa = jnp.zeros((8, 128), jnp.float32)
            weight = jnp.zeros((8, 128), jnp.float32)
            for ch in range(4):
                kappa = jnp.where(lab == ch, con[ch], kappa)
                weight = jnp.where(lab == ch, chw[ch], weight)
            for f, v in enumerate((forcing[rows, :], base[rows, :] * kappa, weight)):
                E[pl.ds((48 * f + 8 + 8 * yo) * 48 + 8 + x, 8, stride=48), :] = v
                @pl.when(x >= 27)
                def _():
                    xs[0, f, x - 27, pl.ds(8 * yo, 8), :] = v
                @pl.when(x < 5)
                def _():
                    xs[1, f, x, pl.ds(8 * yo, 8), :] = v
        return c

    lax.fori_loop(0, 32, fill, 0, unroll=2)
    xm = [remote(xs.at[0], xr.at[0], send, recv, 7, "gx", 1), remote(xs.at[1], xr.at[1], send, recv, 8, "gx", -1)]

    def stagey(n, c):
        f, k = n // 5, lax.rem(n, 5)
        zs_hi = (48 * f + 35 + k) * 48 + 8
        zs_lo = (48 * f + 8 + k) * 48 + 8
        yr[0, f, k] = E[pl.ds(pl.multiple_of(zs_hi, 8), 32), :]
        yr[1, f, k] = E[pl.ds(pl.multiple_of(zs_lo, 8), 32), :]
        return c

    lax.fori_loop(0, 15, stagey, 0)
    yc = [remote(yr.at[0], yr.at[2], send, recv, 9, "gy", 1), remote(yr.at[1], yr.at[3], send, recv, 10, "gy", -1)]
    lane8 = lane // 8

    def packz(n, c):
        f, q, xo = n // 8, lax.rem(n // 4, 2), lax.rem(n, 4)
        top, bottom = None, None
        for i in range(16):
            v = E[pl.ds(pl.multiple_of((48 * f + 8 + 16 * q + i) * 48 + 8 + 8 * xo, 8), 8), :]
            hi = rot(v, (8 * i + 8) % 128)
            lo = rot(v, (8 * i) % 128) if i else v
            top = hi if i == 0 else jnp.where(lane8 == i, hi, top)
            bottom = lo if i == 0 else jnp.where(lane8 == i, lo, bottom)
        zs[0, f, q, pl.ds(pl.multiple_of(8 * xo, 8), 8), :] = top
        zs[1, f, q, pl.ds(pl.multiple_of(8 * xo, 8), 8), :] = bottom
        return c

    lax.fori_loop(0, 24, packz, 0)
    zc = [remote(zs.at[0], zr.at[0], send, recv, 11, "gz", 1), remote(zs.at[1], zr.at[1], send, recv, 12, "gz", -1)]
    for c in g1:
        c.wait()
    mine = ix * 4 + iy
    for h in range(4):
        gat[mine, h] = jnp.where(lane < 64, col[2 * h], rot(col[2 * h + 1], 64))
    g2 = [remote(gat.at[mine], gat.at[mine], send, recv, 12 + s, "gy", s) for s in range(1, 4)]

    my, py = edges("gy")
    mx, px = edges("gx")
    mz, pz = edges("gz")
    for c in yc:
        c.wait()
    cc = [remote(yr.at[pl.ds(2, 2), :, :, pl.ds(24, 8)], xc.at[0], send, recv, 16, "gx", 1),
          remote(yr.at[pl.ds(2, 2), :, :, pl.ds(0, 8)], xc.at[1], send, recv, 17, "gx", -1)]
    for c in g2:
        c.wait()
    plane = pl.ds(ix * 4, 4)
    g3 = [remote(gat.at[plane], gat.at[plane], send, recv, 17 + s, "gx", s) for s in range(1, 4)]

    def addy(n, c):
        f, k = n // 5, lax.rem(n, 5)
        E[pl.ds(pl.multiple_of((48 * f + 3 + k) * 48 + 8, 8), 32), :] = yr[2, f, k] * my
        E[pl.ds(pl.multiple_of((48 * f + 40 + k) * 48 + 8, 8), 32), :] = yr[3, f, k] * py
        return c

    lax.fori_loop(0, 15, addy, 0)
    for c in zc:
        c.wait()
    lane16 = lane // 16
    low = lax.rem(lane, 16) < 8

    def windows(n, c):
        f, xo = n // 4, lax.rem(n, 4)
        rows = pl.ds(pl.multiple_of(8 * xo, 8), 8)
        src = [[zr[d, f, q, rows, :] * m for q in range(2)] for d, m in ((0, mz), (1, pz))]
        for g in range(1, 6):
            acc = jnp.zeros((8, 128), jnp.float32)
            for pos in range(8):
                y = group_row(g, pos) - 8
                if y < 0 or y > 31:
                    continue
                a = rot(src[0][y // 16], (16 * pos - 8 * (y % 16)) % 128)
                b = rot(src[1][y // 16], (16 * pos + 8 - 8 * (y % 16)) % 128)
                acc = jnp.where(lane16 == pos, jnp.where(low, a, b), acc)
            G[f, g, pl.ds(pl.multiple_of(8 + 8 * xo, 8), 8), :] = acc
        return c

    lax.fori_loop(0, 12, windows, 0)
    wc = [remote(G.at[:, pl.ds(4, 2), pl.ds(8, 32)], yg.at[0], send, recv, 21, "gy", 1),
          remote(G.at[:, pl.ds(1, 2), pl.ds(8, 32)], yg.at[1], send, recv, 22, "gy", -1)]
    for c in xm:
        c.wait()

    def addx(n, c):
        f, k = n // 5, lax.rem(n, 5)
        for yo in range(4):
            E[pl.ds((48 * f + 8 + 8 * yo) * 48 + 3 + k, 8, stride=48), :] = xr[0, f, k, pl.ds(8 * yo, 8), :] * mx
            E[pl.ds((48 * f + 8 + 8 * yo) * 48 + 40 + k, 8, stride=48), :] = xr[1, f, k, pl.ds(8 * yo, 8), :] * px
        return c

    lax.fori_loop(0, 15, addx, 0)
    for c in wc:
        c.wait()
    inner = pl.ds(8, 32)
    for f in range(3):
        G[f, 0, inner, :] = yg[0, f, 0] * my
        G[f, 1, inner, :] += yg[0, f, 1] * my
        G[f, 5, inner, :] += yg[1, f, 0] * py
        G[f, 6, inner, :] = yg[1, f, 1] * py
    vc = [remote(G.at[:, :, pl.ds(32, 8)], xg.at[0], send, recv, 23, "gx", 1), remote(G.at[:, :, pl.ds(8, 8)], xg.at[1], send, recv, 24, "gx", -1)]
    for c in cc:
        c.wait()

    def addc(n, c):
        f, k = n // 5, lax.rem(n, 5)
        for d, y0, m in ((0, 3, my), (1, 40, py)):
            E[pl.ds(pl.multiple_of((48 * f + y0 + k) * 48, 8), 8), :] = xc[0, d, f, k] * (m * mx)
            E[pl.ds(pl.multiple_of((48 * f + y0 + k) * 48 + 40, 8), 8), :] = xc[1, d, f, k] * (m * px)
        return c

    lax.fori_loop(0, 15, addc, 0)
    for c in g3 + vc:
        c.wait()
    for f in range(3):
        for g in range(7):
            G[f, g, pl.ds(0, 8), :] = xg[0, f, g] * mx
            G[f, g, pl.ds(40, 8), :] = xg[1, f, g] * px


HALO = [("gy", 1), ("gy", -1), ("gx", 1), ("gx", -1), ("gz", 1), ("gz", -1)]


def split_rows(T, ey, rows):
    lane, _ = lanes_sub()
    t0 = rot(T[0, ey, rows, :], 124)
    t1 = rot(T[1, ey, rows, :], 4)
    a = jnp.where(lane < 124, t0, 0.0) + jnp.where(lane >= 4, t1, 0.0)
    m = jnp.where(lane >= 124, t0, jnp.where(lane < 4, t1, 0.0))
    return a, m


def merge_kernel(T, E, W, zs, zr, yr, yw, xs, xr, xws, xwr, send, recv):
    greet(HALO)
    lane, sub = lanes_sub()
    lane16 = lane // 16
    low = lax.rem(lane, 16) < 8
    E[3] = jnp.zeros((48, 128), jnp.float32)
    E[44] = jnp.zeros((48, 128), jnp.float32)

    def build(n, c):
        g, xo = 1 + n // 6, lax.rem(n, 6)
        rows = pl.ds(pl.multiple_of(8 * xo, 8), 8)
        nxt, prv, own = None, None, None
        for pos in range(8):
            ey = 8 * g - 4 + pos
            a, m = split_rows(T, ey, rows)
            E[ey, rows, :] = a
            ra = rot(a, (16 * pos + 8) % 128)
            rm = rot(m, (16 * pos + 8) % 128)
            s0, s1 = jnp.where(low, ra, rm), jnp.where(low, rm, ra)
            if pos == 0:
                nxt, prv, own = s0, s1, rm
            else:
                hit = lane16 == pos
                nxt, prv, own = jnp.where(hit, s0, nxt), jnp.where(hit, s1, prv), jnp.where(hit, rm, own)
        zs[0, g - 1, rows, :] = nxt
        zs[1, g - 1, rows, :] = prv
        W[0, g, rows, :] = own
        return c

    lax.fori_loop(0, 30, build, 0)
    yc = [remote(E.at[pl.ds(35, 9)], yr.at[0], send, recv, 0, "gy", 1), remote(E.at[pl.ds(4, 9)], yr.at[1], send, recv, 1, "gy", -1)]
    zc = [remote(zs.at[0], zr.at[0], send, recv, 2, "gz", 1), remote(zs.at[1], zr.at[1], send, recv, 3, "gz", -1)]
    my, py = edges("gy")
    mz, pz = edges("gz")
    mx, px = edges("gx")
    for c in yc:
        c.wait()
    def addy(k, c):
        E[3 + k] += yr[0, k] * my
        E[36 + k] += yr[1, k] * py
        return c
    lax.fori_loop(0, 9, addy, 0)
    def stage(y, c):
        xs[0, pl.ds(y * 9, 9), :] = E[3 + y, pl.ds(35, 9), :]
        xs[1, pl.ds(y * 9, 9), :] = E[3 + y, pl.ds(4, 9), :]
        return c
    lax.fori_loop(0, 42, stage, 0, unroll=6)
    xc = [remote(xs.at[0], xr.at[0], send, recv, 4, "gx", 1), remote(xs.at[1], xr.at[1], send, recv, 5, "gx", -1)]
    for c in zc:
        c.wait()
    def windows(n, c):
        g, xo = n // 6, lax.rem(n, 6)
        rows = pl.ds(pl.multiple_of(8 * xo, 8), 8)
        x, y = zr[0, g, rows, :] * mz, zr[1, g, rows, :] * pz
        W[0, g + 1, rows, :] += jnp.where(low, x, y)
        W[1, g + 1, rows, :] = jnp.where(low, y, x)
        return c
    lax.fori_loop(0, 30, windows, 0)
    wc = [remote(W.at[:, pl.ds(4, 2)], yw.at[0], send, recv, 6, "gy", 1), remote(W.at[:, pl.ds(1, 2)], yw.at[1], send, recv, 7, "gy", -1)]
    for c in wc:
        c.wait()
    for w in range(2):
        for k in range(2):
            a, b = yw[0, w, k] * my, yw[1, w, k] * py
            W[w, k] = a if k == 0 else W[w, k] + a
            W[w, 5 + k] = b if k == 1 else W[w, 5 + k] + b
    def stagew(n, c):
        w, g = n // 7, lax.rem(n, 7)
        xws[0, pl.ds(n * 9, 9), :] = W[w, g, pl.ds(35, 9), :]
        xws[1, pl.ds(n * 9, 9), :] = W[w, g, pl.ds(4, 9), :]
        return c
    lax.fori_loop(0, 14, stagew, 0, unroll=7)
    vc = [remote(xws.at[0], xwr.at[0], send, recv, 8, "gx", 1), remote(xws.at[1], xwr.at[1], send, recv, 9, "gx", -1)]
    for c in xc:
        c.wait()
    def unstage(y, c):
        E[3 + y, pl.ds(3, 9), :] += xr[0, pl.ds(y * 9, 9), :] * mx
        E[3 + y, pl.ds(36, 9), :] += xr[1, pl.ds(y * 9, 9), :] * px
        return c
    lax.fori_loop(0, 42, unstage, 0, unroll=6)
    for c in vc:
        c.wait()
    def unstagew(n, c):
        w, g = n // 7, lax.rem(n, 7)
        W[w, g, pl.ds(3, 9), :] += xwr[0, pl.ds(n * 9, 9), :] * mx
        W[w, g, pl.ds(36, 9), :] += xwr[1, pl.ds(n * 9, 9), :] * px
        return c
    lax.fori_loop(0, 14, unstagew, 0, unroll=7)


def fold_kernel(T, C, upd, E, zs, zr, yr, xs, xr, send, recv):
    greet(HALO)
    lane, sub = lanes_sub()
    lane8 = lane // 8

    def build(n, c):
        q, xo = n // 6, lax.rem(n, 6)
        rows = pl.ds(pl.multiple_of(8 * xo, 8), 8)
        nxt, prv = None, None
        for i in range(16):
            ey = 4 + 16 * q + i
            a, m = split_rows(T, ey, rows)
            E[ey, rows, :] = a
            hi = rot(m, (8 * i) % 128) if i else m
            lo = rot(m, (8 * i + 8) % 128)
            nxt = hi if i == 0 else jnp.where(lane8 == i, hi, nxt)
            prv = lo if i == 0 else jnp.where(lane8 == i, lo, prv)
        zs[0, q, rows, :] = nxt
        zs[1, q, rows, :] = prv
        return c

    lax.fori_loop(0, 18, build, 0)
    zc = [remote(zs.at[0], zr.at[0], send, recv, 0, "gz", 1), remote(zs.at[1], zr.at[1], send, recv, 1, "gz", -1)]
    my, py = edges("gy")
    mz, pz = edges("gz")
    mx, px = edges("gx")
    for c in zc:
        c.wait()
    def addz(n, c):
        q, xo = n // 6, lax.rem(n, 6)
        rows = pl.ds(pl.multiple_of(8 * xo, 8), 8)
        x, y = zr[0, q, rows, :] * mz, zr[1, q, rows, :] * pz
        for i in range(16):
            a = rot(x, (128 - 8 * i) % 128) if i else x
            b = rot(y, (120 - 8 * i) % 128)
            E[4 + 16 * q + i, rows, :] += jnp.where(lane < 8, a, jnp.where(lane >= 120, b, 0.0))
        return c
    lax.fori_loop(0, 18, addz, 0)
    yc = [remote(E.at[pl.ds(40, 4)], yr.at[0], send, recv, 2, "gy", 1), remote(E.at[pl.ds(4, 4)], yr.at[1], send, recv, 3, "gy", -1)]
    for c in yc:
        c.wait()
    for k in range(4):
        E[8 + k] += yr[0, k] * my
        E[36 + k] += yr[1, k] * py
    def stage(y, c):
        xs[0, pl.ds(y * 4, 4), :] = E[8 + y, pl.ds(40, 4), :]
        xs[1, pl.ds(y * 4, 4), :] = E[8 + y, pl.ds(4, 4), :]
        return c
    lax.fori_loop(0, 32, stage, 0, unroll=8)
    xc = [remote(xs.at[0], xr.at[0], send, recv, 4, "gx", 1), remote(xs.at[1], xr.at[1], send, recv, 5, "gx", -1)]
    for c in xc:
        c.wait()
    def finish(y, c):
        E[8 + y, pl.ds(8, 4), :] += xr[0, pl.ds(y * 4, 4), :] * mx
        E[8 + y, pl.ds(36, 4), :] += xr[1, pl.ds(y * 4, 4), :] * px
        for xo in range(4):
            upd[pl.ds(xo * 256 + y, 8, stride=32), :] = C[y, pl.ds(8 * xo, 8), :] + E[8 + y, pl.ds(8 + 8 * xo, 8), :]
        return c
    lax.fori_loop(0, 32, finish, 0, unroll=4)


def f32(*shape):
    return jax.ShapeDtypeStruct(shape, jnp.float32)


def vmem(*shape):
    return pltpu.VMEM(shape, jnp.float32)


def params(cid):
    return pltpu.CompilerParams(collective_id=cid, has_side_effects=True, vmem_limit_bytes=BIG)


def share(coef, forcing, base, labels, con, chw):
    return pl.pallas_call(
        share_kernel, out_shape=(f32(16, 4, 8, 128), f32(3 * 48 * 48, 128), f32(3, 7, 48, 128)),
        in_specs=[VM, VM, VM, VM, SM, SM], out_specs=(VM, VM, VM),
        scratch_shapes=[vmem(8, 128), vmem(8, 8, 128), vmem(2, 3, 2, 32, 128), vmem(2, 3, 2, 32, 128), vmem(4, 3, 5, 32, 128), vmem(2, 3, 2, 32, 128),
                        vmem(2, 3, 5, 32, 128), vmem(2, 3, 5, 32, 128), vmem(2, 2, 3, 5, 8, 128), vmem(2, 3, 7, 8, 128),
                        pltpu.SemaphoreType.DMA((25,)), pltpu.SemaphoreType.DMA((25,))],
        compiler_params=params(0), name="share")(coef, forcing, base, labels, con, chw)


def merge(T):
    return pl.pallas_call(
        merge_kernel, out_shape=(f32(48, 48, 128), f32(2, 7, 48, 128)), in_specs=[VM], out_specs=(VM, VM),
        scratch_shapes=[vmem(2, 5, 48, 128), vmem(2, 5, 48, 128), vmem(2, 9, 48, 128), vmem(2, 2, 2, 48, 128),
                        vmem(2, 384, 128), vmem(2, 384, 128), vmem(2, 128, 128), vmem(2, 128, 128),
                        pltpu.SemaphoreType.DMA((10,)), pltpu.SemaphoreType.DMA((10,))],
        compiler_params=params(1), name="merge")(T)


def fold(T, C):
    return pl.pallas_call(
        fold_kernel, out_shape=f32(1024, 128), in_specs=[VM, VM], out_specs=VM,
        scratch_shapes=[vmem(52, 48, 128), vmem(2, 3, 48, 128), vmem(2, 3, 48, 128), vmem(2, 4, 48, 128),
                        vmem(2, 128, 128), vmem(2, 128, 128),
                        pltpu.SemaphoreType.DMA((6,)), pltpu.SemaphoreType.DMA((6,))],
        compiler_params=params(2), name="fold")(T, C)


def prolong_kernel(live_ref, off, link, gat, basis, acc, buf, sems):
    live = jnp.clip(live_ref[0], 0, NP)

    def fetch(p):
        return pltpu.make_async_copy(basis.at[pl.ds(p * 256, 256)], buf.at[pl.ds(p * 256, 256)], sems.at[p])

    def start(p, c):
        fetch(p).start()
        return c

    lax.fori_loop(0, live, start, 0)
    acc[...] = jnp.zeros_like(acc)
    lane, sub = lanes_sub()
    ix, iy, iz = lax.axis_index("gx"), lax.axis_index("gy"), lax.axis_index("gz")

    def body(p, c):
        ox, oy, tile, lo = corner(off, p)
        jx, jy, jz = ix + link[0, p] - 1, iy + link[1, p] - 1, iz + link[2, p] - 1
        owner = jnp.clip((jx * 4 + jy) * 8 + jz, 0, 127)
        spot = jnp.clip(link[3, p], 0, ND - 1) + 64 * lax.rem(owner, 2)
        cell = rot(gat[owner // 8, lax.rem(owner // 2, 4)], lax.rem(128 - spot, 128))
        cell = jnp.broadcast_to(cell[:, 0:1], (8, 128))
        ck = [jnp.broadcast_to(cell[k : k + 1, :], (8, 128)) for k in range(NB)]
        fetch(p).wait()
        inwin = (lane >= lo) & (lane < lo + 16)
        for yh in range(2):
            for xo in range(2):
                v = None
                for k in range(NB):
                    t = ck[k] * buf[pl.ds(p * 256 + 128 * xo + 8 * yh + k, 8, stride=16), :]
                    v = t if v is None else v + t
                for yl in range(8):
                    r = rot(v, lax.rem(lo - 16 * yl + 128, 128))
                    acc[tile, oy + 4 + 8 * yh + yl, pl.ds(ox + 4 + 8 * xo, 8), :] += jnp.where(inwin, r, 0.0)
        return c

    lax.fori_loop(0, live, body, 0)


def residual_stage(E, G, Ec, Wc, R, K, W, gk, C, gc, inner):
    lane, sub = lanes_sub()
    near = (lane < 8) | (lane >= 120)

    def unpack(n, c):
        g, xo = n // 6, lax.rem(n, 6)
        rows = pl.ds(pl.multiple_of(8 * xo, 8), 8)
        gs, cs, ks = Wc[0, g, rows, :], Wc[1, g, rows, :], G[1, g, rows, :]
        for pos in range(8):
            ey = group_row(g, pos) + 4
            s = (120 - 16 * pos) % 128
            gc[ey, rows, :] = rot(gs, s)
            gk[ey, rows, :] = rot(ks, s)
            C[ey, rows, :] = Ec[jnp.clip(ey - 4, 0, 47), rows, :] + jnp.where(near, rot(cs, s), 0.0)
        return c

    lax.fori_loop(0, 42, unpack, 0)

    def pair(cv, kv, nc, nk):
        inside = nk > 0.0
        return jnp.where(inside, 0.5 * (kv + nk) * (cv - nc), kv * cv)

    def build(n, c):
        g, xo = 1 + n // 5, lax.rem(n, 5)
        x0 = 4 + 8 * xo
        rows = pl.ds(x0, 8)

        def row(f, cy, dx):
            return E[pl.ds((48 * f + cy - 4) * 48 + x0 + dx, 8), :]

        gf, gw = G[0, g, rows, :], G[2, g, rows, :]
        for pos in range(8):
            ey = group_row(g, pos) + 4
            s = (120 - 16 * pos) % 128
            cv, gv = C[ey, rows, :], gc[ey, rows, :]
            kv, hv = row(1, ey, 0), gk[ey, rows, :]
            cu, cd, gu, gd = rot(cv, 127), rot(cv, 1), rot(gv, 127), rot(gv, 1)
            ku, kd, hu, hd = rot(kv, 127), rot(kv, 1), rot(hv, 127), rot(hv, 1)
            last, first = lane == 127, lane == 0
            r = row(0, ey, 0)
            r = r - pair(cv, kv, jnp.where(last, gu, cu), jnp.where(last, hu, ku))
            r = r - pair(cv, kv, jnp.where(first, gd, cd), jnp.where(first, hd, kd))
            q = rot(gf, s)
            q = q - pair(gv, hv, jnp.where(last, cu, gu), jnp.where(last, ku, hu))
            q = q - pair(gv, hv, jnp.where(first, cd, gd), jnp.where(first, kd, hd))
            for dy, dx in ((-1, 0), (1, 0), (0, -1), (0, 1)):
                rr = pl.ds(x0 + dx, 8)
                r = r - pair(cv, kv, C[ey + dy, rr, :], row(1, ey + dy, dx))
                q = q - pair(gv, hv, gc[ey + dy, rr, :], gk[ey + dy, rr, :])
            head, tail = lane < 4, lane >= 124
            py, px = ey - 8, pl.ds(pl.multiple_of(8 * xo, 8), 8)
            wv, gwv = row(2, ey, 0), rot(gw, s)
            for F, inn, out in ((R, r, q), (K, kv, hv), (W, wv, gwv)):
                F[0, py, px, :] = rot(jnp.where(tail, out, inn), 4)
                F[1, py, px, :] = rot(jnp.where(head, out, inn), 124)
        return c

    lax.fori_loop(0, 25, build, 0)

    def keep(y, c):
        inner[y] = C[y + 12, pl.ds(8, 32), :]
        return c

    lax.fori_loop(0, 32, keep, 0)


def enrich_kernel(live_ref, off, E, G, Ec, Wc, out, corr, inner, R, K, W, gk, C, gc, cbuf, vbuf):
    residual_stage(E, G, Ec, Wc, R, K, W, gk, C, gc, inner)
    live = jnp.clip(live_ref[0], 0, NP)
    corr[...] = jnp.zeros_like(corr)
    lane, sub = lanes_sub()
    group = lane // 16
    zpos = lane % 16
    zw = zpos < 15
    zg = zpos > 0
    yup = lane < 112
    ydn = lane >= 16
    xup = sub < 7
    xdn = sub > 0
    fz = zpos.astype(jnp.float32)
    def tentf(t):
        return (t + 0.5) * (PIECE - t - 0.5) * (4.0 / (PIECE * PIECE))
    tents = {}
    for xp in range(2):
        for yp in range(2):
            tents[xp, yp] = tentf((2*sub + xp).astype(jnp.float32)) * tentf((2*group + yp).astype(jnp.float32)) * tentf(fz)
    par = [(0,0),(0,1),(1,0),(1,1)]

    def prep(p, slot):
        ox, oy, tile, lo = corner(off, p)
        active = jnp.where(p < live, 1.0, 0.0)
        got = []
        for F in (R, K, W):
            d = {}
            for xp, yp in par:
                a = None
                for yh in range(8):
                    row = F[tile, oy + 2*yh + yp, pl.ds(ox + xp, 8, stride=2), :]
                    r = rot(row, lax.rem(16*yh - lo + 128, 128))
                    a = r if a is None else jnp.where(group == yh, r, a)
                d[xp, yp] = a
            got.append(d)
        r, k, w = got
        for i, (xp, yp) in enumerate(par):
            kc = k[xp, yp]
            nbs = [
                (rot(kc, 127), zw), (rot(kc, 1), zg),
                (k[xp, 1-yp], None),
                (rot(k[xp, 1-yp], 16 if yp == 0 else 112), ydn if yp == 0 else yup),
                (k[1-xp, yp], None),
                (rot(k[1-xp, yp], 1 if xp == 0 else 7, 0), xdn if xp == 0 else xup),
            ]
            diag = None
            cs = []
            inside = kc > 0.0
            for nb, m in nbs:
                ok = nb > 0.0
                if m is not None:
                    ok = ok & m
                face = jnp.where(ok, 0.5 * (kc + nb), kc)
                cs.append(jnp.where(ok & inside, face, 0.0))
                diag = face if diag is None else diag + face
            inv = jnp.where(inside, OMEGA / jnp.where(inside, diag, 1.0), 0.0)
            for j, cj in enumerate(cs):
                cbuf[slot, pl.ds((i*6 + j)*8, 8), :] = cj * inv
            b1 = r[xp, yp] * inv * active
            vbuf[slot, pl.ds(i*8, 8), :] = b1
            vbuf[slot, pl.ds((4+i)*8, 8), :] = b1 * w[xp, yp]

    def sweep_piece(vs, slot):
        res = []
        for s in range(2):
            v = {par[i]: vs[s*4+i] for i in range(4)}
            for i, (xp, yp) in enumerate(par):
                c = [cbuf[slot, pl.ds((i*6 + j)*8, 8), :] for j in range(6)]
                vc = v[xp, yp]
                t0 = vbuf[slot, pl.ds((4*s+i)*8, 8), :] + (1.0 - OMEGA) * vc
                t1 = c[0] * rot(vc, 127) + c[1] * rot(vc, 1)
                t2 = c[2] * v[xp, 1-yp] + c[3] * rot(v[xp, 1-yp], 16 if yp == 0 else 112)
                t3 = c[4] * v[1-xp, yp] + c[5] * rot(v[1-xp, yp], 1 if xp == 0 else 7, 0)
                res.append((t0 + t1) + (t2 + t3))
        return res

    idxs = [16*(4*yh2 + group//2) + zpos for yh2 in range(2)]
    gpar = (group % 2) == 0

    def body(g, c):
        for slot in range(PAIR):
            prep(g*PAIR + slot, slot)
        init = tuple(vbuf[slot, pl.ds(n*8, 8), :] for slot in range(PAIR) for n in range(8))
        def sweep(_, vs):
            o = []
            for slot in range(PAIR):
                o += sweep_piece(vs[slot*8:slot*8+8], slot)
            return tuple(o)
        vs = lax.fori_loop(0, SWEEPS - 1, sweep, init)
        for slot in range(PAIR):
            p = g*PAIR + slot
            ox, oy, tile, lo = corner(off, p)
            inwin = (lane >= lo) & (lane < lo + 16)
            v = vs[slot*8:slot*8+8]
            for s in range(2):
                for xp in range(2):
                    for yh2 in range(2):
                        e = jnp.take_along_axis(v[s*4 + 2*xp], idxs[yh2], axis=1)
                        o = jnp.take_along_axis(v[s*4 + 2*xp + 1], idxs[yh2], axis=1)
                        out[pl.ds(p*64 + 4*xp + 2*yh2 + s, 8, stride=8), :] = jnp.where(gpar, e, o)
            for i, (xp, yp) in enumerate(par):
                sp = tents[xp, yp] * (v[i] + v[4+i])
                for yh in range(8):
                    rr = jnp.where(inwin, rot(sp, lax.rem(lo - 16*yh + 128, 128)), 0.0)
                    corr[tile, oy + 4 + 2*yh + yp, pl.ds(ox + 4 + xp, 8, stride=2), :] += rr
        return c
    ng = (live + PAIR - 1) // PAIR
    lax.fori_loop(0, ng, body, 0)
    def zero(p, c):
        out[pl.ds(p*64, 64), :] = jnp.zeros((64, 128), jnp.float32)
        return c
    lax.fori_loop(ng*PAIR, NP, zero, 0)


def prolong(live, off, link, gat, basis):
    return pl.pallas_call(
        prolong_kernel, out_shape=f32(2, 52, 48, 128), in_specs=[SM, SM, SM, VM, ANY], out_specs=VM,
        scratch_shapes=[vmem(NP * 256, 128), pltpu.SemaphoreType.DMA((NP,))],
        compiler_params=pltpu.CompilerParams(vmem_limit_bytes=BIG), name="prolong")(live, off, link, gat, basis)


def enrich(live, off, E, G, Ec, Wc):
    return pl.pallas_call(
        enrich_kernel, out_shape=(f32(NP * 64, 128), f32(2, 52, 48, 128), f32(32, 32, 128)),
        in_specs=[SM, SM, VM, VM, VM, VM], out_specs=(VM, VM, VM),
        scratch_shapes=[vmem(2, 40, 40, 128), vmem(2, 40, 40, 128), vmem(2, 40, 40, 128),
                        vmem(56, 48, 128), vmem(56, 48, 128), vmem(56, 48, 128), vmem(PAIR, 192, 128), vmem(PAIR, 64, 128)],
        compiler_params=pltpu.CompilerParams(vmem_limit_bytes=BIG), name="enrich")(live, off, E, G, Ec, Wc)


def basis_rows(rb):
    return rb.reshape(NP, NB, 32, 128).transpose(0, 2, 1, 3).reshape(NP * 256, 128)


def out_basis(o):
    return o.reshape(NP, 32, 2, 128).transpose(0, 2, 1, 3).reshape(1, 1, 1, NP, 2, 4096)


def local(forcing, kappa_base, labels, contrast, channel_weight, coarse_coef, source_link, offsets, live_pieces, resident_bases):
    live = live_pieces.reshape(1)
    off = offsets[0, 0].transpose(2, 0, 1)
    link = source_link[0, 0, 0].T
    gat, E, G = share(
        coarse_coef[0, 0, 0].T, forcing.reshape(1024, 128), kappa_base.reshape(1024, 128), labels.reshape(1024, 128),
        contrast, channel_weight)
    T = prolong(live, off, link, gat, basis_rows(resident_bases))
    Ec, Wc = merge(T)
    out, corr, inner = enrich(live, off, E, G, Ec, Wc)
    return fold(corr, inner).reshape(32, 32, 128), out_basis(out)


def solution(mesh):
    return jax.shard_map(
        local,
        mesh=mesh,
        in_specs=(
            P("gx", "gy", "gz"),
            P("gx", "gy", "gz"),
            P("gx", "gy", "gz"),
            P(),
            P(),
            P("gx", "gy", "gz", None, None),
            P("gx", "gy", "gz", None, None),
            P("gx", "gy", "gz", None, None),
            P("gx", "gy", "gz"),
            P("gx", "gy", "gz", None, None, None),
        ),
        out_specs=(P("gx", "gy", "gz"), P("gx", "gy", "gz", None, None, None)),
        check_vma=False,
    )
```

```python
import jax
import jax.numpy as jnp
from jax import lax
from jax.experimental import pallas as pl
from jax.experimental.pallas import tpu as pltpu
from jax.sharding import PartitionSpec as P

ND = 64
PIECE=16; NB=8; NP=40; SWEEPS=20
OMEGA = 2.0/3.0
PAIR = 8
FEW = 8
VM = pl.BlockSpec(memory_space=pltpu.VMEM)
SM = pl.BlockSpec(memory_space=pltpu.SMEM)
ANY = pl.BlockSpec(memory_space=pltpu.HBM)

def corner(off, p):
    ox = jnp.clip(off[0, 0, p], 0, 24)
    oy = jnp.clip(off[1, 0, p], 0, 24)
    oz = jnp.clip(off[2, 0, p], 0, 120)
    tile = (oz > 112).astype(jnp.int32)
    return ox, oy, tile, oz - 8 * tile

def rot(v, shift, axis=1):
    return pltpu.roll(v, shift, axis)

def lanes_sub():
    return lax.broadcasted_iota(jnp.int32, (8, 128), 1), lax.broadcasted_iota(jnp.int32, (8, 128), 0)

MESH = pl.DeviceIdType.MESH
SIZE = {"gx": 4, "gy": 4, "gz": 8}


def ring(axis, step):
    n = SIZE[axis]
    return lax.rem(lax.axis_index(axis) + (step + n), n)


def greet(pairs):
    barrier = pltpu.get_barrier_semaphore()
    for axis, step in pairs:
        pl.semaphore_signal(barrier, inc=1, device_id={axis: ring(axis, step)}, device_id_type=MESH)
    pl.semaphore_wait(barrier, len(pairs))


def remote(src, dst, send, recv, i, axis, step):
    copy = pltpu.make_async_remote_copy(
        src_ref=src, dst_ref=dst, send_sem=send.at[i], recv_sem=recv.at[i],
        device_id={axis: ring(axis, step)}, device_id_type=MESH,
    )
    copy.start()
    return copy


def edges(axis):
    i = lax.axis_index(axis)
    return (jnp.where(i > 0, 1.0, 0.0), jnp.where(i < SIZE[axis] - 1, 1.0, 0.0))


def group_row(g, pos):
    return 8 * g - 4 + pos


def share_kernel(coef, forcing, base, labels, con, chw, basis, gat, E, G, yk, held, bsem, tile, col, zs, zr, yr, xs, xr, send, recv):
    ix, iy, iz = lax.axis_index("gx"), lax.axis_index("gy"), lax.axis_index("gz")
    lane, sub = lanes_sub()
    tile[...] = jnp.zeros_like(tile)
    tile[0:8, 0:64] = coef[...]
    fetch = pltpu.make_async_copy(basis, held, bsem)
    fetch.start()
    greet([("gz", s) for s in range(1, 8)] + [("gy", s) for s in range(1, 4)] + [("gx", s) for s in range(1, 4)])
    g1 = [remote(tile, col.at[iz], send, recv, s - 1, "gz", s) for s in range(1, 8)]
    col[iz] = tile[...]

    def fill(x, c):
        for yo in range(4):
            rows = pl.ds(pl.multiple_of(x * 32 + 8 * yo, 8), 8)
            lab = labels[rows, :]
            kappa = jnp.zeros((8, 128), jnp.float32)
            weight = jnp.zeros((8, 128), jnp.float32)
            for ch in range(4):
                kappa = jnp.where(lab == ch, con[ch], kappa)
                weight = jnp.where(lab == ch, chw[ch], weight)
            for f, v in enumerate((forcing[rows, :], base[rows, :] * kappa, weight)):
                E[pl.ds((48 * f + 8 + 8 * yo) * 48 + 8 + x, 8, stride=48), :] = v
                @pl.when(x >= 27)
                def _():
                    xs[0, f, x - 27, pl.ds(8 * yo, 8), :] = v
                @pl.when(x < 5)
                def _():
                    xs[1, f, x, pl.ds(8 * yo, 8), :] = v
        return c

    lax.fori_loop(0, 32, fill, 0, unroll=2)
    xm = [remote(xs.at[0], xr.at[0], send, recv, 7, "gx", 1), remote(xs.at[1], xr.at[1], send, recv, 8, "gx", -1)]

    def stagey(n, c):
        f, k = n // 5, lax.rem(n, 5)
        zs_hi = (48 * f + 35 + k) * 48 + 8
        zs_lo = (48 * f + 8 + k) * 48 + 8
        yr[0, f, k] = E[pl.ds(pl.multiple_of(zs_hi, 8), 32), :]
        yr[1, f, k] = E[pl.ds(pl.multiple_of(zs_lo, 8), 32), :]
        return c

    lax.fori_loop(0, 15, stagey, 0)
    yc = [remote(yr.at[0], yr.at[2], send, recv, 9, "gy", 1), remote(yr.at[1], yr.at[3], send, recv, 10, "gy", -1)]
    lane8 = lane // 8

    def packz(n, c):
        f, q, xo = n // 8, lax.rem(n // 4, 2), lax.rem(n, 4)
        top, bottom = None, None
        for i in range(16):
            v = E[pl.ds(pl.multiple_of((48 * f + 8 + 16 * q + i) * 48 + 8 + 8 * xo, 8), 8), :]
            hi = rot(v, (8 * i + 8) % 128)
            lo = rot(v, (8 * i) % 128) if i else v
            top = hi if i == 0 else jnp.where(lane8 == i, hi, top)
            bottom = lo if i == 0 else jnp.where(lane8 == i, lo, bottom)
        zs[0, f, q, pl.ds(pl.multiple_of(8 * xo, 8), 8), :] = top
        zs[1, f, q, pl.ds(pl.multiple_of(8 * xo, 8), 8), :] = bottom
        return c

    lax.fori_loop(0, 24, packz, 0)
    zc = [remote(zs.at[0], zr.at[0], send, recv, 11, "gz", 1), remote(zs.at[1], zr.at[1], send, recv, 12, "gz", -1)]
    for c in g1:
        c.wait()
    mine = ix * 4 + iy
    for h in range(4):
        gat[mine, h] = jnp.where(lane < 64, col[2 * h], rot(col[2 * h + 1], 64))
    g2 = [remote(gat.at[mine], gat.at[mine], send, recv, 12 + s, "gy", s) for s in range(1, 4)]

    my, py = edges("gy")
    mx, px = edges("gx")
    mz, pz = edges("gz")
    for c in yc:
        c.wait()
    for c in g2:
        c.wait()
    plane = pl.ds(ix * 4, 4)
    g3 = [remote(gat.at[plane], gat.at[plane], send, recv, 15 + s, "gx", s) for s in range(1, 4)]

    def addy(n, c):
        f, k = n // 5, lax.rem(n, 5)
        for d, y0, m in ((0, 3, my), (1, 40, py)):
            v = yr[2 + d, f, k] * m
            E[pl.ds(pl.multiple_of((48 * f + y0 + k) * 48 + 8, 8), 32), :] = v
            yk[0, d, f, k] = v[24:32, :]
            yk[1, d, f, k] = v[0:8, :]
        return c

    lax.fori_loop(0, 15, addy, 0)
    for c in zc:
        c.wait()
    lane16 = lane // 16
    low = lax.rem(lane, 16) < 8

    def windows(n, c):
        f, xo = n // 4, lax.rem(n, 4)
        rows = pl.ds(pl.multiple_of(8 * xo, 8), 8)
        src = [[zr[d, f, q, rows, :] * m for q in range(2)] for d, m in ((0, mz), (1, pz))]
        for g in range(1, 6):
            acc = jnp.zeros((8, 128), jnp.float32)
            for pos in range(8):
                y = group_row(g, pos) - 8
                if y < 0 or y > 31:
                    continue
                a = rot(src[0][y // 16], (16 * pos - 8 * (y % 16)) % 128)
                b = rot(src[1][y // 16], (16 * pos + 8 - 8 * (y % 16)) % 128)
                acc = jnp.where(lane16 == pos, jnp.where(low, a, b), acc)
            G[f, g, pl.ds(pl.multiple_of(8 + 8 * xo, 8), 8), :] = acc
        return c

    lax.fori_loop(0, 12, windows, 0)
    for c in xm:
        c.wait()

    def addx(n, c):
        f, k = n // 5, lax.rem(n, 5)
        for yo in range(4):
            E[pl.ds((48 * f + 8 + 8 * yo) * 48 + 3 + k, 8, stride=48), :] = xr[0, f, k, pl.ds(8 * yo, 8), :] * mx
            E[pl.ds((48 * f + 8 + 8 * yo) * 48 + 40 + k, 8, stride=48), :] = xr[1, f, k, pl.ds(8 * yo, 8), :] * px
        return c

    lax.fori_loop(0, 15, addx, 0)
    for c in g3:
        c.wait()
    fetch.wait()


HALO = [("gy", 1), ("gy", -1), ("gx", 1), ("gx", -1), ("gz", 1), ("gz", -1)]


def split_rows(T, ey, rows):
    lane, _ = lanes_sub()
    t0 = rot(T[0, ey, rows, :], 124)
    t1 = rot(T[1, ey, rows, :], 4)
    a = jnp.where(lane < 124, t0, 0.0) + jnp.where(lane >= 4, t1, 0.0)
    m = jnp.where(lane >= 124, t0, jnp.where(lane < 4, t1, 0.0))
    return a, m


def merge_kernel(T, G0, yk, E, W, G, xk, yg, xg, kr, zs, zr, yr, yw, xs, xr, xws, xwr, send, recv):
    greet(HALO)
    cc = [remote(yk.at[0], kr.at[0], send, recv, 10, "gx", 1), remote(yk.at[1], kr.at[1], send, recv, 11, "gx", -1)]
    gc = [remote(G0.at[:, pl.ds(4, 2), pl.ds(8, 32)], yg.at[0], send, recv, 12, "gy", 1),
          remote(G0.at[:, pl.ds(1, 2), pl.ds(8, 32)], yg.at[1], send, recv, 13, "gy", -1)]
    lane, sub = lanes_sub()
    lane16 = lane // 16
    low = lax.rem(lane, 16) < 8
    E[3] = jnp.zeros((48, 128), jnp.float32)
    E[44] = jnp.zeros((48, 128), jnp.float32)

    def build(n, c):
        g, xo = 1 + n // 6, lax.rem(n, 6)
        rows = pl.ds(pl.multiple_of(8 * xo, 8), 8)
        nxt, prv, own = None, None, None
        for pos in range(8):
            ey = 8 * g - 4 + pos
            a, m = split_rows(T, ey, rows)
            E[ey, rows, :] = a
            ra = rot(a, (16 * pos + 8) % 128)
            rm = rot(m, (16 * pos + 8) % 128)
            s0, s1 = jnp.where(low, ra, rm), jnp.where(low, rm, ra)
            if pos == 0:
                nxt, prv, own = s0, s1, rm
            else:
                hit = lane16 == pos
                nxt, prv, own = jnp.where(hit, s0, nxt), jnp.where(hit, s1, prv), jnp.where(hit, rm, own)
        zs[0, g - 1, rows, :] = nxt
        zs[1, g - 1, rows, :] = prv
        W[0, g, rows, :] = own
        return c

    lax.fori_loop(0, 30, build, 0)
    zc = [remote(zs.at[0], zr.at[0], send, recv, 2, "gz", 1), remote(zs.at[1], zr.at[1], send, recv, 3, "gz", -1)]
    yc = [remote(E.at[pl.ds(35, 9)], yr.at[0], send, recv, 0, "gy", 1), remote(E.at[pl.ds(4, 9)], yr.at[1], send, recv, 1, "gy", -1)]
    my, py = edges("gy")
    mz, pz = edges("gz")
    mx, px = edges("gx")
    for c in gc:
        c.wait()
    inner = pl.ds(8, 32)
    for f in range(3):
        G[f, 0, inner, :] = yg[0, f, 0] * my
        G[f, 1, inner, :] = G0[f, 1, inner, :] + yg[0, f, 1] * my
        for g in (2, 3, 4):
            G[f, g, inner, :] = G0[f, g, inner, :]
        G[f, 5, inner, :] = G0[f, 5, inner, :] + yg[1, f, 0] * py
        G[f, 6, inner, :] = yg[1, f, 1] * py
    hc = [remote(G.at[:, :, pl.ds(32, 8)], xg.at[0], send, recv, 14, "gx", 1), remote(G.at[:, :, pl.ds(8, 8)], xg.at[1], send, recv, 15, "gx", -1)]
    for c in yc:
        c.wait()
    def addy(k, c):
        E[3 + k] += yr[0, k] * my
        E[36 + k] += yr[1, k] * py
        return c
    lax.fori_loop(0, 9, addy, 0)
    def stage(y, c):
        xs[0, pl.ds(y * 9, 9), :] = E[3 + y, pl.ds(35, 9), :]
        xs[1, pl.ds(y * 9, 9), :] = E[3 + y, pl.ds(4, 9), :]
        return c
    lax.fori_loop(0, 42, stage, 0, unroll=6)
    xc = [remote(xs.at[0], xr.at[0], send, recv, 4, "gx", 1), remote(xs.at[1], xr.at[1], send, recv, 5, "gx", -1)]
    for c in zc:
        c.wait()
    def windows(n, c):
        g, xo = n // 6, lax.rem(n, 6)
        rows = pl.ds(pl.multiple_of(8 * xo, 8), 8)
        x, y = zr[0, g, rows, :] * mz, zr[1, g, rows, :] * pz
        W[0, g + 1, rows, :] += jnp.where(low, x, y)
        W[1, g + 1, rows, :] = jnp.where(low, y, x)
        return c
    lax.fori_loop(0, 30, windows, 0)
    wc = [remote(W.at[:, pl.ds(4, 2)], yw.at[0], send, recv, 6, "gy", 1), remote(W.at[:, pl.ds(1, 2)], yw.at[1], send, recv, 7, "gy", -1)]
    for c in wc:
        c.wait()
    for w in range(2):
        for k in range(2):
            a, b = yw[0, w, k] * my, yw[1, w, k] * py
            W[w, k] = a if k == 0 else W[w, k] + a
            W[w, 5 + k] = b if k == 1 else W[w, 5 + k] + b
    def stagew(n, c):
        w, g = n // 7, lax.rem(n, 7)
        xws[0, pl.ds(n * 9, 9), :] = W[w, g, pl.ds(35, 9), :]
        xws[1, pl.ds(n * 9, 9), :] = W[w, g, pl.ds(4, 9), :]
        return c
    lax.fori_loop(0, 14, stagew, 0, unroll=7)
    vc = [remote(xws.at[0], xwr.at[0], send, recv, 8, "gx", 1), remote(xws.at[1], xwr.at[1], send, recv, 9, "gx", -1)]
    for c in cc + hc:
        c.wait()
    for d in range(2):
        for f in range(3):
            for k in range(5):
                xk[0, d, f, k] = kr[0, d, f, k] * mx
                xk[1, d, f, k] = kr[1, d, f, k] * px
    for f in range(3):
        for g in range(7):
            G[f, g, pl.ds(0, 8), :] = xg[0, f, g] * mx
            G[f, g, pl.ds(40, 8), :] = xg[1, f, g] * px
    for c in xc:
        c.wait()
    def unstage(y, c):
        E[3 + y, pl.ds(3, 9), :] += xr[0, pl.ds(y * 9, 9), :] * mx
        E[3 + y, pl.ds(36, 9), :] += xr[1, pl.ds(y * 9, 9), :] * px
        return c
    lax.fori_loop(0, 42, unstage, 0, unroll=6)
    for c in vc:
        c.wait()
    def unstagew(n, c):
        w, g = n // 7, lax.rem(n, 7)
        W[w, g, pl.ds(3, 9), :] += xwr[0, pl.ds(n * 9, 9), :] * mx
        W[w, g, pl.ds(36, 9), :] += xwr[1, pl.ds(n * 9, 9), :] * px
        return c
    lax.fori_loop(0, 14, unstagew, 0, unroll=7)


def fold_kernel(T, C, upd, E, zs, zr, yr, xs, xr, send, recv):
    greet(HALO)
    lane, sub = lanes_sub()
    lane8 = lane // 8

    def build(n, c):
        q, xo = n // 6, lax.rem(n, 6)
        rows = pl.ds(pl.multiple_of(8 * xo, 8), 8)
        nxt, prv = None, None
        for i in range(16):
            ey = 4 + 16 * q + i
            a, m = split_rows(T, ey, rows)
            E[ey, rows, :] = a
            hi = rot(m, (8 * i) % 128) if i else m
            lo = rot(m, (8 * i + 8) % 128)
            nxt = hi if i == 0 else jnp.where(lane8 == i, hi, nxt)
            prv = lo if i == 0 else jnp.where(lane8 == i, lo, prv)
        zs[0, q, rows, :] = nxt
        zs[1, q, rows, :] = prv
        return c

    lax.fori_loop(0, 18, build, 0)
    zc = [remote(zs.at[0], zr.at[0], send, recv, 0, "gz", 1), remote(zs.at[1], zr.at[1], send, recv, 1, "gz", -1)]
    my, py = edges("gy")
    mz, pz = edges("gz")
    mx, px = edges("gx")
    for c in zc:
        c.wait()
    def addz(n, c):
        q, xo = n // 6, lax.rem(n, 6)
        rows = pl.ds(pl.multiple_of(8 * xo, 8), 8)
        x, y = zr[0, q, rows, :] * mz, zr[1, q, rows, :] * pz
        for i in range(16):
            a = rot(x, (128 - 8 * i) % 128) if i else x
            b = rot(y, (120 - 8 * i) % 128)
            E[4 + 16 * q + i, rows, :] += jnp.where(lane < 8, a, jnp.where(lane >= 120, b, 0.0))
        return c
    lax.fori_loop(0, 18, addz, 0)
    yc = [remote(E.at[pl.ds(40, 4)], yr.at[0], send, recv, 2, "gy", 1), remote(E.at[pl.ds(4, 4)], yr.at[1], send, recv, 3, "gy", -1)]
    for c in yc:
        c.wait()
    for k in range(4):
        E[8 + k] += yr[0, k] * my
        E[36 + k] += yr[1, k] * py
    def stage(y, c):
        xs[0, pl.ds(y * 4, 4), :] = E[8 + y, pl.ds(40, 4), :]
        xs[1, pl.ds(y * 4, 4), :] = E[8 + y, pl.ds(4, 4), :]
        return c
    lax.fori_loop(0, 32, stage, 0, unroll=8)
    xc = [remote(xs.at[0], xr.at[0], send, recv, 4, "gx", 1), remote(xs.at[1], xr.at[1], send, recv, 5, "gx", -1)]
    for c in xc:
        c.wait()
    def finish(y, c):
        E[8 + y, pl.ds(8, 4), :] += xr[0, pl.ds(y * 4, 4), :] * mx
        E[8 + y, pl.ds(36, 4), :] += xr[1, pl.ds(y * 4, 4), :] * px
        for xo in range(4):
            upd[pl.ds(xo * 256 + y, 8, stride=32), :] = C[y, pl.ds(8 * xo, 8), :] + E[8 + y, pl.ds(8 + 8 * xo, 8), :]
        return c
    lax.fori_loop(0, 32, finish, 0, unroll=4)


def f32(*shape):
    return jax.ShapeDtypeStruct(shape, jnp.float32)


def vmem(*shape):
    return pltpu.VMEM(shape, jnp.float32)


def params(cid, mib):
    return pltpu.CompilerParams(collective_id=cid, has_side_effects=True, vmem_limit_bytes=mib << 20)


def share(coef, forcing, base, labels, con, chw, basis):
    return pl.pallas_call(
        share_kernel, out_shape=(f32(16, 4, 8, 128), f32(3 * 48 * 48, 128), f32(3, 7, 48, 128), f32(2, 2, 3, 5, 8, 128), f32(NP * 256, 128)),
        in_specs=[VM, VM, VM, VM, SM, SM, ANY], out_specs=(VM, VM, VM, VM, VM),
        scratch_shapes=[pltpu.SemaphoreType.DMA, vmem(8, 128), vmem(8, 8, 128), vmem(2, 3, 2, 32, 128), vmem(2, 3, 2, 32, 128), vmem(4, 3, 5, 32, 128),
                        vmem(2, 3, 5, 32, 128), vmem(2, 3, 5, 32, 128),
                        pltpu.SemaphoreType.DMA((19,)), pltpu.SemaphoreType.DMA((19,))],
        compiler_params=params(0, 20), name="share")(coef, forcing, base, labels, con, chw, basis)


def merge(T, G0, yk):
    return pl.pallas_call(
        merge_kernel, out_shape=(f32(48, 48, 128), f32(2, 7, 48, 128), f32(3, 7, 48, 128), f32(2, 2, 3, 5, 8, 128)),
        in_specs=[VM, VM, VM], out_specs=(VM, VM, VM, VM),
        scratch_shapes=[vmem(2, 3, 2, 32, 128), vmem(2, 3, 7, 8, 128), vmem(2, 2, 3, 5, 8, 128),
                        vmem(2, 5, 48, 128), vmem(2, 5, 48, 128), vmem(2, 9, 48, 128), vmem(2, 2, 2, 48, 128),
                        vmem(2, 384, 128), vmem(2, 384, 128), vmem(2, 128, 128), vmem(2, 128, 128),
                        pltpu.SemaphoreType.DMA((16,)), pltpu.SemaphoreType.DMA((16,))],
        compiler_params=params(1, 14), name="merge")(T, G0, yk)


def fold(T, C):
    return pl.pallas_call(
        fold_kernel, out_shape=f32(1024, 128), in_specs=[VM, VM], out_specs=VM,
        scratch_shapes=[vmem(52, 48, 128), vmem(2, 3, 48, 128), vmem(2, 3, 48, 128), vmem(2, 4, 48, 128),
                        vmem(2, 128, 128), vmem(2, 128, 128),
                        pltpu.SemaphoreType.DMA((6,)), pltpu.SemaphoreType.DMA((6,))],
        compiler_params=params(2, 12), name="fold")(T, C)


def prolong_kernel(live_ref, off, link, gat, buf, acc):
    live = jnp.clip(live_ref[0], 0, NP)
    acc[...] = jnp.zeros_like(acc)
    lane, sub = lanes_sub()
    ix, iy, iz = lax.axis_index("gx"), lax.axis_index("gy"), lax.axis_index("gz")

    def values(p):
        jx, jy, jz = ix + link[0, p] - 1, iy + link[1, p] - 1, iz + link[2, p] - 1
        owner = jnp.clip((jx * 4 + jy) * 8 + jz, 0, 127)
        spot = jnp.clip(link[3, p], 0, ND - 1) + 64 * lax.rem(owner, 2)
        cell = rot(gat[owner // 8, lax.rem(owner // 2, 4)], lax.rem(128 - spot, 128))
        cell = jnp.broadcast_to(cell[:, 0:1], (8, 128)) * jnp.where(p < live, 1.0, 0.0)
        ck = [jnp.broadcast_to(cell[k : k + 1, :], (8, 128)) for k in range(NB)]
        vs = {}
        for yh in range(2):
            for xo in range(2):
                t = [ck[k] * buf[pl.ds(p * 256 + 128 * xo + 8 * yh + k, 8, stride=16), :] for k in range(NB)]
                vs[yh, xo] = ((t[0] + t[1]) + (t[2] + t[3])) + ((t[4] + t[5]) + (t[6] + t[7]))
        return vs

    def body(g, c):
        pieces = [g * FEW + j for j in range(FEW)]
        every = [values(p) for p in pieces]
        for p, vs in zip(pieces, every):
            ox, oy, tile, lo = corner(off, p)
            inwin = (lane >= lo) & (lane < lo + 16)
            new = []
            for (yh, xo), v in vs.items():
                for yl in range(8):
                    r = rot(v, lax.rem(lo - 16 * yl + 128, 128))
                    spot = (tile, oy + 4 + 8 * yh + yl, pl.ds(ox + 4 + 8 * xo, 8), slice(None))
                    new.append((spot, acc[spot] + jnp.where(inwin, r, 0.0)))
            for spot, value in new:
                acc[spot] = value
        return c

    lax.fori_loop(0, (live + FEW - 1) // FEW, body, 0)


def residual_stage(E0, G, Ec, Wc, xk, E, R, K, W, gk, C, gc, inner, sem):
    lane, sub = lanes_sub()
    whole = pltpu.make_async_copy(E0, E, sem)
    whole.start()
    near = (lane < 8) | (lane >= 120)

    def unpack(n, c):
        g, xo = n // 6, lax.rem(n, 6)
        rows = pl.ds(pl.multiple_of(8 * xo, 8), 8)
        gs, cs, ks = Wc[0, g, rows, :], Wc[1, g, rows, :], G[1, g, rows, :]
        for pos in range(8):
            ey = group_row(g, pos) + 4
            s = (120 - 16 * pos) % 128
            gc[ey, rows, :] = rot(gs, s)
            gk[ey, rows, :] = rot(ks, s)
            C[ey, rows, :] = Ec[jnp.clip(ey - 4, 0, 47), rows, :] + jnp.where(near, rot(cs, s), 0.0)
        return c

    lax.fori_loop(0, 42, unpack, 0)

    whole.wait()
    for f in range(3):
        for k in range(5):
            for d, y0 in ((0, 3), (1, 40)):
                E[pl.ds((48 * f + y0 + k) * 48, 8), :] = xk[0, d, f, k]
                E[pl.ds((48 * f + y0 + k) * 48 + 40, 8), :] = xk[1, d, f, k]

    def pair(cv, kv, nc, nk):
        inside = nk > 0.0
        return jnp.where(inside, 0.5 * (kv + nk) * (cv - nc), kv * cv)

    def build(n, c):
        g, xo = 1 + n // 5, lax.rem(n, 5)
        x0 = 4 + 8 * xo
        rows = pl.ds(x0, 8)

        def row(f, cy, dx):
            return E[pl.ds((48 * f + cy - 4) * 48 + x0 + dx, 8), :]

        gf, gw = G[0, g, rows, :], G[2, g, rows, :]
        for pos in range(8):
            ey = group_row(g, pos) + 4
            s = (120 - 16 * pos) % 128
            cv, gv = C[ey, rows, :], gc[ey, rows, :]
            kv, hv = row(1, ey, 0), gk[ey, rows, :]
            cu, cd, gu, gd = rot(cv, 127), rot(cv, 1), rot(gv, 127), rot(gv, 1)
            ku, kd, hu, hd = rot(kv, 127), rot(kv, 1), rot(hv, 127), rot(hv, 1)
            last, first = lane == 127, lane == 0
            r = row(0, ey, 0)
            r = r - pair(cv, kv, jnp.where(last, gu, cu), jnp.where(last, hu, ku))
            r = r - pair(cv, kv, jnp.where(first, gd, cd), jnp.where(first, hd, kd))
            q = rot(gf, s)
            q = q - pair(gv, hv, jnp.where(last, cu, gu), jnp.where(last, ku, hu))
            q = q - pair(gv, hv, jnp.where(first, cd, gd), jnp.where(first, kd, hd))
            for dy, dx in ((-1, 0), (1, 0), (0, -1), (0, 1)):
                rr = pl.ds(x0 + dx, 8)
                r = r - pair(cv, kv, C[ey + dy, rr, :], row(1, ey + dy, dx))
                q = q - pair(gv, hv, gc[ey + dy, rr, :], gk[ey + dy, rr, :])
            head, tail = lane < 4, lane >= 124
            py, px = ey - 8, pl.ds(pl.multiple_of(8 * xo, 8), 8)
            wv, gwv = row(2, ey, 0), rot(gw, s)
            for F, inn, out in ((R, r, q), (K, kv, hv), (W, wv, gwv)):
                F[0, py, px, :] = rot(jnp.where(tail, out, inn), 4)
                F[1, py, px, :] = rot(jnp.where(head, out, inn), 124)
        return c

    lax.fori_loop(0, 25, build, 0)

    def keep(y, c):
        inner[y] = C[y + 12, pl.ds(8, 32), :]
        return c

    lax.fori_loop(0, 32, keep, 0)


def enrich_kernel(live_ref, off, E0, G, Ec, Wc, xk, out, corr, inner, E, R, K, W, gk, C, gc, cbuf, vbuf, sem):
    residual_stage(E0, G, Ec, Wc, xk, E, R, K, W, gk, C, gc, inner, sem)
    live = jnp.clip(live_ref[0], 0, NP)
    corr[...] = jnp.zeros_like(corr)
    lane, sub = lanes_sub()
    group = lane // 16
    zpos = lane % 16
    zw = zpos < 15
    zg = zpos > 0
    yup = lane < 112
    ydn = lane >= 16
    xup = sub < 7
    xdn = sub > 0
    fz = zpos.astype(jnp.float32)
    def tentf(t):
        return (t + 0.5) * (PIECE - t - 0.5) * (4.0 / (PIECE * PIECE))
    tents = {}
    for xp in range(2):
        for yp in range(2):
            tents[xp, yp] = tentf((2*sub + xp).astype(jnp.float32)) * tentf((2*group + yp).astype(jnp.float32)) * tentf(fz)
    par = [(0,0),(0,1),(1,0),(1,1)]

    def prep(p, slot):
        ox, oy, tile, lo = corner(off, p)
        active = jnp.where(p < live, 1.0, 0.0)
        got = []
        for F in (R, K, W):
            d = {}
            for xp, yp in par:
                a = None
                for yh in range(8):
                    row = F[tile, oy + 2*yh + yp, pl.ds(ox + xp, 8, stride=2), :]
                    r = rot(row, lax.rem(16*yh - lo + 128, 128))
                    a = r if a is None else jnp.where(group == yh, r, a)
                d[xp, yp] = a
            got.append(d)
        r, k, w = got
        for i, (xp, yp) in enumerate(par):
            kc = k[xp, yp]
            nbs = [
                (rot(kc, 127), zw), (rot(kc, 1), zg),
                (k[xp, 1-yp], None),
                (rot(k[xp, 1-yp], 16 if yp == 0 else 112), ydn if yp == 0 else yup),
                (k[1-xp, yp], None),
                (rot(k[1-xp, yp], 1 if xp == 0 else 7, 0), xdn if xp == 0 else xup),
            ]
            diag = None
            cs = []
            inside = kc > 0.0
            for nb, m in nbs:
                ok = nb > 0.0
                if m is not None:
                    ok = ok & m
                face = jnp.where(ok, 0.5 * (kc + nb), kc)
                cs.append(jnp.where(ok & inside, face, 0.0))
                diag = face if diag is None else diag + face
            inv = jnp.where(inside, OMEGA / jnp.where(inside, diag, 1.0), 0.0)
            for j, cj in enumerate(cs):
                cbuf[slot, pl.ds((i*6 + j)*8, 8), :] = cj * inv
            b1 = r[xp, yp] * inv * active
            vbuf[slot, pl.ds(i*8, 8), :] = b1
            vbuf[slot, pl.ds((4+i)*8, 8), :] = b1 * w[xp, yp]

    def sweep_piece(vs, slot):
        res = []
        for s in range(2):
            v = {par[i]: vs[s*4+i] for i in range(4)}
            for i, (xp, yp) in enumerate(par):
                c = [cbuf[slot, pl.ds((i*6 + j)*8, 8), :] for j in range(6)]
                vc = v[xp, yp]
                t0 = vbuf[slot, pl.ds((4*s+i)*8, 8), :] + (1.0 - OMEGA) * vc
                t1 = c[0] * rot(vc, 127) + c[1] * rot(vc, 1)
                t2 = c[2] * v[xp, 1-yp] + c[3] * rot(v[xp, 1-yp], 16 if yp == 0 else 112)
                t3 = c[4] * v[1-xp, yp] + c[5] * rot(v[1-xp, yp], 1 if xp == 0 else 7, 0)
                res.append((t0 + t1) + (t2 + t3))
        return res

    idxs = [16*(4*yh2 + group//2) + zpos for yh2 in range(2)]
    gpar = (group % 2) == 0

    def body(g, c):
        for slot in range(PAIR):
            prep(g*PAIR + slot, slot)
        init = tuple(vbuf[slot, pl.ds(n*8, 8), :] for slot in range(PAIR) for n in range(8))
        def sweep(_, vs):
            o = []
            for slot in range(PAIR):
                o += sweep_piece(vs[slot*8:slot*8+8], slot)
            return tuple(o)
        vs = lax.fori_loop(0, SWEEPS - 1, sweep, init)
        for slot in range(PAIR):
            p = g*PAIR + slot
            ox, oy, tile, lo = corner(off, p)
            inwin = (lane >= lo) & (lane < lo + 16)
            v = vs[slot*8:slot*8+8]
            for s in range(2):
                for xp in range(2):
                    for yh2 in range(2):
                        e = jnp.take_along_axis(v[s*4 + 2*xp], idxs[yh2], axis=1)
                        o = jnp.take_along_axis(v[s*4 + 2*xp + 1], idxs[yh2], axis=1)
                        out[pl.ds(p*64 + 4*xp + 2*yh2 + s, 8, stride=8), :] = jnp.where(gpar, e, o)
            for i, (xp, yp) in enumerate(par):
                sp = tents[xp, yp] * (v[i] + v[4+i])
                new = []
                for yh in range(8):
                    rr = jnp.where(inwin, rot(sp, lax.rem(lo - 16*yh + 128, 128)), 0.0)
                    spot = (tile, oy + 4 + 2*yh + yp, pl.ds(ox + 4 + xp, 8, stride=2), slice(None))
                    new.append((spot, corr[spot] + rr))
                for spot, value in new:
                    corr[spot] = value
        return c
    ng = (live + PAIR - 1) // PAIR
    lax.fori_loop(0, ng, body, 0)
    def zero(p, c):
        out[pl.ds(p*64, 64), :] = jnp.zeros((64, 128), jnp.float32)
        return c
    lax.fori_loop(ng*PAIR, NP, zero, 0)


def prolong(live, off, link, gat, basis):
    return pl.pallas_call(
        prolong_kernel, out_shape=f32(2, 52, 48, 128), in_specs=[SM, SM, SM, VM, VM], out_specs=VM,
        compiler_params=pltpu.CompilerParams(vmem_limit_bytes=14 << 20), name="prolong")(live, off, link, gat, basis)


def enrich(live, off, E, G, Ec, Wc, xk):
    return pl.pallas_call(
        enrich_kernel, out_shape=(f32(NP * 64, 128), f32(2, 52, 48, 128), f32(32, 32, 128)),
        in_specs=[SM, SM, pl.BlockSpec(memory_space=pl.ANY), VM, VM, VM, VM], out_specs=(VM, VM, VM),
        scratch_shapes=[vmem(3 * 48 * 48, 128), vmem(2, 40, 40, 128), vmem(2, 40, 40, 128), vmem(2, 40, 40, 128),
                        vmem(56, 48, 128), vmem(56, 48, 128), vmem(56, 48, 128), vmem(PAIR, 192, 128), vmem(PAIR, 64, 128), pltpu.SemaphoreType.DMA],
        compiler_params=pltpu.CompilerParams(vmem_limit_bytes=30 << 20), name="enrich")(live, off, E, G, Ec, Wc, xk)


def basis_rows(rb):
    return rb.reshape(NP, NB, 32, 128).transpose(0, 2, 1, 3).reshape(NP * 256, 128)


def out_basis(o):
    return o.reshape(NP, 32, 2, 128).transpose(0, 2, 1, 3).reshape(1, 1, 1, NP, 2, 4096)


def local(forcing, kappa_base, labels, contrast, channel_weight, coarse_coef, source_link, offsets, live_pieces, resident_bases):
    live = live_pieces.reshape(1)
    off = offsets[0, 0].transpose(2, 0, 1)
    link = source_link[0, 0, 0].T
    gat, E, G0, yk, held = share(
        coarse_coef[0, 0, 0].T, forcing.reshape(1024, 128), kappa_base.reshape(1024, 128), labels.reshape(1024, 128),
        contrast, channel_weight, basis_rows(resident_bases))
    T = prolong(live, off, link, gat, held)
    Ec, Wc, G, xk = merge(T, G0, yk)
    out, corr, inner = enrich(live, off, E, G, Ec, Wc, xk)
    return fold(corr, inner).reshape(32, 32, 128), out_basis(out)


def solution(mesh):
    return jax.shard_map(
        local,
        mesh=mesh,
        in_specs=(
            P("gx", "gy", "gz"),
            P("gx", "gy", "gz"),
            P("gx", "gy", "gz"),
            P(),
            P(),
            P("gx", "gy", "gz", None, None),
            P("gx", "gy", "gz", None, None),
            P("gx", "gy", "gz", None, None),
            P("gx", "gy", "gz"),
            P("gx", "gy", "gz", None, None, None),
        ),
        out_specs=(P("gx", "gy", "gz"), P("gx", "gy", "gz", None, None, None)),
        check_vma=False,
    )
```

```python
import jax
import jax.numpy as jnp
from jax import lax
from jax.experimental import pallas as pl
from jax.experimental.pallas import tpu as pltpu
from jax.sharding import PartitionSpec as P

ND = 64
PIECE=16; NB=8; NP=40; SWEEPS=20
OMEGA = 2.0/3.0
PAIR = 8
FEW = 8
VM = pl.BlockSpec(memory_space=pltpu.VMEM)
SM = pl.BlockSpec(memory_space=pltpu.SMEM)
ANY = pl.BlockSpec(memory_space=pltpu.HBM)

def corner(off, p):
    ox = jnp.clip(off[0, 0, p], 0, 24)
    oy = jnp.clip(off[1, 0, p], 0, 24)
    oz = jnp.clip(off[2, 0, p], 0, 120)
    tile = (oz > 112).astype(jnp.int32)
    return ox, oy, tile, oz - 8 * tile

def rot(v, shift, axis=1):
    return pltpu.roll(v, shift, axis)

def lanes_sub():
    return lax.broadcasted_iota(jnp.int32, (8, 128), 1), lax.broadcasted_iota(jnp.int32, (8, 128), 0)

MESH = pl.DeviceIdType.MESH
SIZE = {"gx": 4, "gy": 4, "gz": 8}


def ring(axis, step):
    n = SIZE[axis]
    return lax.rem(lax.axis_index(axis) + (step + n), n)


def greet(pairs):
    barrier = pltpu.get_barrier_semaphore()
    for axis, step in pairs:
        pl.semaphore_signal(barrier, inc=1, device_id={axis: ring(axis, step)}, device_id_type=MESH)
    pl.semaphore_wait(barrier, len(pairs))


def remote(src, dst, send, recv, i, axis, step):
    copy = pltpu.make_async_remote_copy(
        src_ref=src, dst_ref=dst, send_sem=send.at[i], recv_sem=recv.at[i],
        device_id={axis: ring(axis, step)}, device_id_type=MESH,
    )
    copy.start()
    return copy


def edges(axis):
    i = lax.axis_index(axis)
    return (jnp.where(i > 0, 1.0, 0.0), jnp.where(i < SIZE[axis] - 1, 1.0, 0.0))


def group_row(g, pos):
    return 8 * g - 4 + pos


def share_kernel(coef, forcing0, base0, labels0, con, chw, basis, gat, E, G, yk, held, bsem, forcing, base, labels, isem, tile, col, zs, zr, yr, xs, xr, send, recv):
    ix, iy, iz = lax.axis_index("gx"), lax.axis_index("gy"), lax.axis_index("gz")
    lane, sub = lanes_sub()
    tile[...] = jnp.zeros_like(tile)
    tile[0:8, 0:64] = coef[...]
    fields = [pltpu.make_async_copy(a, b, isem.at[i]) for i, (a, b) in enumerate(((forcing0, forcing), (base0, base), (labels0, labels)))]
    for c in fields:
        c.start()
    fetch = pltpu.make_async_copy(basis, held, bsem)
    fetch.start()
    greet([("gz", s) for s in range(1, 8)] + [("gy", s) for s in range(1, 4)] + [("gx", s) for s in range(1, 4)])
    g1 = [remote(tile, col.at[iz], send, recv, s - 1, "gz", s) for s in range(1, 8)]
    col[iz] = tile[...]

    for c in fields:
        c.wait()

    def fill(x, c):
        for yo in range(4):
            rows = pl.ds(pl.multiple_of(x * 32 + 8 * yo, 8), 8)
            lab = labels[rows, :]
            kappa = jnp.zeros((8, 128), jnp.float32)
            weight = jnp.zeros((8, 128), jnp.float32)
            for ch in range(4):
                kappa = jnp.where(lab == ch, con[ch], kappa)
                weight = jnp.where(lab == ch, chw[ch], weight)
            for f, v in enumerate((forcing[rows, :], base[rows, :] * kappa, weight)):
                E[pl.ds((48 * f + 8 + 8 * yo) * 48 + 8 + x, 8, stride=48), :] = v
                @pl.when(x >= 27)
                def _():
                    xs[0, f, x - 27, pl.ds(8 * yo, 8), :] = v
                @pl.when(x < 5)
                def _():
                    xs[1, f, x, pl.ds(8 * yo, 8), :] = v
        return c

    lax.fori_loop(0, 32, fill, 0, unroll=2)
    lane8 = lane // 8

    def packz(n, c):
        f, q, xo = n // 8, lax.rem(n // 4, 2), lax.rem(n, 4)
        top, bottom = None, None
        for i in range(16):
            v = E[pl.ds(pl.multiple_of((48 * f + 8 + 16 * q + i) * 48 + 8 + 8 * xo, 8), 8), :]
            hi = rot(v, (8 * i + 8) % 128)
            lo = rot(v, (8 * i) % 128) if i else v
            top = hi if i == 0 else jnp.where(lane8 == i, hi, top)
            bottom = lo if i == 0 else jnp.where(lane8 == i, lo, bottom)
        zs[0, f, q, pl.ds(pl.multiple_of(8 * xo, 8), 8), :] = top
        zs[1, f, q, pl.ds(pl.multiple_of(8 * xo, 8), 8), :] = bottom
        return c

    lax.fori_loop(0, 24, packz, 0)
    zc = [remote(zs.at[0], zr.at[0], send, recv, 11, "gz", 1), remote(zs.at[1], zr.at[1], send, recv, 12, "gz", -1)]
    xm = [remote(xs.at[0], xr.at[0], send, recv, 7, "gx", 1), remote(xs.at[1], xr.at[1], send, recv, 8, "gx", -1)]

    def stagey(n, c):
        f, k = n // 5, lax.rem(n, 5)
        zs_hi = (48 * f + 35 + k) * 48 + 8
        zs_lo = (48 * f + 8 + k) * 48 + 8
        yr[0, f, k] = E[pl.ds(pl.multiple_of(zs_hi, 8), 32), :]
        yr[1, f, k] = E[pl.ds(pl.multiple_of(zs_lo, 8), 32), :]
        return c

    lax.fori_loop(0, 15, stagey, 0)
    yc = [remote(yr.at[0], yr.at[2], send, recv, 9, "gy", 1), remote(yr.at[1], yr.at[3], send, recv, 10, "gy", -1)]
    for c in g1:
        c.wait()
    mine = ix * 4 + iy
    for h in range(4):
        gat[mine, h] = jnp.where(lane < 64, col[2 * h], rot(col[2 * h + 1], 64))
    g2 = [remote(gat.at[mine], gat.at[mine], send, recv, 12 + s, "gy", s) for s in range(1, 4)]

    my, py = edges("gy")
    mx, px = edges("gx")
    mz, pz = edges("gz")
    for c in yc:
        c.wait()
    for c in g2:
        c.wait()
    plane = pl.ds(ix * 4, 4)
    g3 = [remote(gat.at[plane], gat.at[plane], send, recv, 15 + s, "gx", s) for s in range(1, 4)]

    def addy(n, c):
        f, k = n // 5, lax.rem(n, 5)
        for d, y0, m in ((0, 3, my), (1, 40, py)):
            v = yr[2 + d, f, k] * m
            E[pl.ds(pl.multiple_of((48 * f + y0 + k) * 48 + 8, 8), 32), :] = v
            yk[0, d, f, k] = v[24:32, :]
            yk[1, d, f, k] = v[0:8, :]
        return c

    lax.fori_loop(0, 15, addy, 0)
    for c in xm:
        c.wait()

    def addx(n, c):
        f, k = n // 5, lax.rem(n, 5)
        for yo in range(4):
            E[pl.ds((48 * f + 8 + 8 * yo) * 48 + 3 + k, 8, stride=48), :] = xr[0, f, k, pl.ds(8 * yo, 8), :] * mx
            E[pl.ds((48 * f + 8 + 8 * yo) * 48 + 40 + k, 8, stride=48), :] = xr[1, f, k, pl.ds(8 * yo, 8), :] * px
        return c

    lax.fori_loop(0, 15, addx, 0)
    for c in zc:
        c.wait()
    lane16 = lane // 16
    low = lax.rem(lane, 16) < 8

    def windows(n, c):
        f, xo = n // 4, lax.rem(n, 4)
        rows = pl.ds(pl.multiple_of(8 * xo, 8), 8)
        src = [[zr[d, f, q, rows, :] * m for q in range(2)] for d, m in ((0, mz), (1, pz))]
        for g in range(1, 6):
            acc = jnp.zeros((8, 128), jnp.float32)
            for pos in range(8):
                y = group_row(g, pos) - 8
                if y < 0 or y > 31:
                    continue
                a = rot(src[0][y // 16], (16 * pos - 8 * (y % 16)) % 128)
                b = rot(src[1][y // 16], (16 * pos + 8 - 8 * (y % 16)) % 128)
                acc = jnp.where(lane16 == pos, jnp.where(low, a, b), acc)
            G[f, g, pl.ds(pl.multiple_of(8 + 8 * xo, 8), 8), :] = acc
        return c

    lax.fori_loop(0, 12, windows, 0)
    for c in g3:
        c.wait()
    fetch.wait()


HALO = [("gy", 1), ("gy", -1), ("gx", 1), ("gx", -1), ("gz", 1), ("gz", -1)]


def split_rows(T, ey, rows):
    lane, _ = lanes_sub()
    t0 = rot(T[0, ey, rows, :], 124)
    t1 = rot(T[1, ey, rows, :], 4)
    a = jnp.where(lane < 124, t0, 0.0) + jnp.where(lane >= 4, t1, 0.0)
    m = jnp.where(lane >= 124, t0, jnp.where(lane < 4, t1, 0.0))
    return a, m


def merge_kernel(T, G0, yk, E, W, G, xk, yg, xg, kr, zs, zr, yr, yw, xs, xr, xws, xwr, send, recv):
    greet(HALO)
    cc = [remote(yk.at[0], kr.at[0], send, recv, 10, "gx", 1), remote(yk.at[1], kr.at[1], send, recv, 11, "gx", -1)]
    gc = [remote(G0.at[:, pl.ds(4, 2), pl.ds(8, 32)], yg.at[0], send, recv, 12, "gy", 1),
          remote(G0.at[:, pl.ds(1, 2), pl.ds(8, 32)], yg.at[1], send, recv, 13, "gy", -1)]
    lane, sub = lanes_sub()
    lane16 = lane // 16
    low = lax.rem(lane, 16) < 8
    E[3] = jnp.zeros((48, 128), jnp.float32)
    E[44] = jnp.zeros((48, 128), jnp.float32)
    side = jnp.zeros((41, 8, 128), jnp.float32)
    E[pl.ds(4, 41), pl.ds(0, 8), :] = side
    E[pl.ds(4, 41), pl.ds(40, 8), :] = side
    W[:, :, pl.ds(0, 8), :] = jnp.zeros((2, 7, 8, 128), jnp.float32)
    W[:, :, pl.ds(40, 8), :] = jnp.zeros((2, 7, 8, 128), jnp.float32)

    def build(n, c):
        g, xo = 1 + n // 5, lax.rem(n, 5)
        rows, near = pl.ds(4 + 8 * xo, 8), pl.ds(pl.multiple_of(8 * xo, 8), 8)
        nxt, prv, own = None, None, None
        for pos in range(8):
            ey = 8 * g - 4 + pos
            a, m = split_rows(T, ey, rows)
            E[ey, rows, :] = a
            ra = rot(a, (16 * pos + 8) % 128)
            rm = rot(m, (16 * pos + 8) % 128)
            s0, s1 = jnp.where(low, ra, rm), jnp.where(low, rm, ra)
            if pos == 0:
                nxt, prv, own = s0, s1, rm
            else:
                hit = lane16 == pos
                nxt, prv, own = jnp.where(hit, s0, nxt), jnp.where(hit, s1, prv), jnp.where(hit, rm, own)
        zs[0, g - 1, near, :] = nxt
        zs[1, g - 1, near, :] = prv
        W[0, g, rows, :] = own
        return c

    lax.fori_loop(0, 25, build, 0)
    zc = [remote(zs.at[0], zr.at[0], send, recv, 2, "gz", 1), remote(zs.at[1], zr.at[1], send, recv, 3, "gz", -1)]
    yc = [remote(E.at[pl.ds(35, 9)], yr.at[0], send, recv, 0, "gy", 1), remote(E.at[pl.ds(4, 9)], yr.at[1], send, recv, 1, "gy", -1)]
    my, py = edges("gy")
    mz, pz = edges("gz")
    mx, px = edges("gx")
    for c in gc:
        c.wait()
    inner = pl.ds(8, 32)
    for f in range(3):
        G[f, 0, inner, :] = yg[0, f, 0] * my
        G[f, 1, inner, :] = G0[f, 1, inner, :] + yg[0, f, 1] * my
        for g in (2, 3, 4):
            G[f, g, inner, :] = G0[f, g, inner, :]
        G[f, 5, inner, :] = G0[f, 5, inner, :] + yg[1, f, 0] * py
        G[f, 6, inner, :] = yg[1, f, 1] * py
    hc = [remote(G.at[:, :, pl.ds(32, 8)], xg.at[0], send, recv, 14, "gx", 1), remote(G.at[:, :, pl.ds(8, 8)], xg.at[1], send, recv, 15, "gx", -1)]
    for c in yc:
        c.wait()
    def addy(k, c):
        E[3 + k] += yr[0, k] * my
        E[36 + k] += yr[1, k] * py
        return c
    lax.fori_loop(0, 9, addy, 0)
    def stage(y, c):
        xs[0, pl.ds(y * 9, 9), :] = E[3 + y, pl.ds(35, 9), :]
        xs[1, pl.ds(y * 9, 9), :] = E[3 + y, pl.ds(4, 9), :]
        return c
    lax.fori_loop(0, 42, stage, 0, unroll=6)
    xc = [remote(xs.at[0], xr.at[0], send, recv, 4, "gx", 1), remote(xs.at[1], xr.at[1], send, recv, 5, "gx", -1)]
    for c in zc:
        c.wait()
    def windows(n, c):
        g, xo = n // 5, lax.rem(n, 5)
        rows, near = pl.ds(4 + 8 * xo, 8), pl.ds(pl.multiple_of(8 * xo, 8), 8)
        x, y = zr[0, g, near, :] * mz, zr[1, g, near, :] * pz
        W[0, g + 1, rows, :] += jnp.where(low, x, y)
        W[1, g + 1, rows, :] = jnp.where(low, y, x)
        return c
    lax.fori_loop(0, 25, windows, 0, unroll=5)
    wc = [remote(W.at[:, pl.ds(4, 2)], yw.at[0], send, recv, 6, "gy", 1), remote(W.at[:, pl.ds(1, 2)], yw.at[1], send, recv, 7, "gy", -1)]
    for c in wc:
        c.wait()
    for w in range(2):
        for k in range(2):
            a, b = yw[0, w, k] * my, yw[1, w, k] * py
            W[w, k] = a if k == 0 else W[w, k] + a
            W[w, 5 + k] = b if k == 1 else W[w, 5 + k] + b
    def stagew(n, c):
        w, g = n // 7, lax.rem(n, 7)
        xws[0, pl.ds(n * 9, 9), :] = W[w, g, pl.ds(35, 9), :]
        xws[1, pl.ds(n * 9, 9), :] = W[w, g, pl.ds(4, 9), :]
        return c
    lax.fori_loop(0, 14, stagew, 0, unroll=7)
    vc = [remote(xws.at[0], xwr.at[0], send, recv, 8, "gx", 1), remote(xws.at[1], xwr.at[1], send, recv, 9, "gx", -1)]
    for c in cc + hc:
        c.wait()
    for d in range(2):
        for f in range(3):
            for k in range(5):
                xk[0, d, f, k] = kr[0, d, f, k] * mx
                xk[1, d, f, k] = kr[1, d, f, k] * px
    for f in range(3):
        for g in range(7):
            G[f, g, pl.ds(0, 8), :] = xg[0, f, g] * mx
            G[f, g, pl.ds(40, 8), :] = xg[1, f, g] * px
    for c in xc:
        c.wait()
    def unstage(y, c):
        E[3 + y, pl.ds(3, 9), :] += xr[0, pl.ds(y * 9, 9), :] * mx
        E[3 + y, pl.ds(36, 9), :] += xr[1, pl.ds(y * 9, 9), :] * px
        return c
    lax.fori_loop(0, 42, unstage, 0, unroll=6)
    for c in vc:
        c.wait()
    def unstagew(n, c):
        w, g = n // 7, lax.rem(n, 7)
        W[w, g, pl.ds(3, 9), :] += xwr[0, pl.ds(n * 9, 9), :] * mx
        W[w, g, pl.ds(36, 9), :] += xwr[1, pl.ds(n * 9, 9), :] * px
        return c
    lax.fori_loop(0, 14, unstagew, 0, unroll=7)


def fold_kernel(T, C, upd, E, zs, zr, yr, xs, xr, send, recv):
    greet(HALO)
    lane, sub = lanes_sub()
    lane8 = lane // 8

    def build(n, c):
        q, xo = n // 5, lax.rem(n, 5)
        rows, near = pl.ds(4 + 8 * xo, 8), pl.ds(pl.multiple_of(8 * xo, 8), 8)
        nxt, prv = None, None
        for i in range(16):
            ey = 4 + 16 * q + i
            a, m = split_rows(T, ey, rows)
            E[ey, rows, :] = a
            hi = rot(m, (8 * i) % 128) if i else m
            lo = rot(m, (8 * i + 8) % 128)
            nxt = hi if i == 0 else jnp.where(lane8 == i, hi, nxt)
            prv = lo if i == 0 else jnp.where(lane8 == i, lo, prv)
        zs[0, q, near, :] = nxt
        zs[1, q, near, :] = prv
        return c

    lax.fori_loop(0, 15, build, 0)
    zc = [remote(zs.at[0], zr.at[0], send, recv, 0, "gz", 1), remote(zs.at[1], zr.at[1], send, recv, 1, "gz", -1)]
    my, py = edges("gy")
    mz, pz = edges("gz")
    mx, px = edges("gx")
    for c in zc:
        c.wait()
    def addz(n, c):
        q, xo = n // 5, lax.rem(n, 5)
        rows, near = pl.ds(4 + 8 * xo, 8), pl.ds(pl.multiple_of(8 * xo, 8), 8)
        x, y = zr[0, q, near, :] * mz, zr[1, q, near, :] * pz
        for i in range(16):
            a = rot(x, (128 - 8 * i) % 128) if i else x
            b = rot(y, (120 - 8 * i) % 128)
            E[4 + 16 * q + i, rows, :] += jnp.where(lane < 8, a, jnp.where(lane >= 120, b, 0.0))
        return c
    lax.fori_loop(0, 15, addz, 0)
    yc = [remote(E.at[pl.ds(40, 4)], yr.at[0], send, recv, 2, "gy", 1), remote(E.at[pl.ds(4, 4)], yr.at[1], send, recv, 3, "gy", -1)]
    for c in yc:
        c.wait()
    for k in range(4):
        E[8 + k] += yr[0, k] * my
        E[36 + k] += yr[1, k] * py
    def stage(y, c):
        xs[0, pl.ds(y * 4, 4), :] = E[8 + y, pl.ds(40, 4), :]
        xs[1, pl.ds(y * 4, 4), :] = E[8 + y, pl.ds(4, 4), :]
        return c
    lax.fori_loop(0, 32, stage, 0, unroll=8)
    xc = [remote(xs.at[0], xr.at[0], send, recv, 4, "gx", 1), remote(xs.at[1], xr.at[1], send, recv, 5, "gx", -1)]
    for c in xc:
        c.wait()
    def finish(y, c):
        E[8 + y, pl.ds(8, 4), :] += xr[0, pl.ds(y * 4, 4), :] * mx
        E[8 + y, pl.ds(36, 4), :] += xr[1, pl.ds(y * 4, 4), :] * px
        for xo in range(4):
            upd[pl.ds(xo * 256 + y, 8, stride=32), :] = C[y, pl.ds(8 * xo, 8), :] + E[8 + y, pl.ds(8 + 8 * xo, 8), :]
        return c
    lax.fori_loop(0, 32, finish, 0, unroll=4)


def f32(*shape):
    return jax.ShapeDtypeStruct(shape, jnp.float32)


def vmem(*shape):
    return pltpu.VMEM(shape, jnp.float32)


def params(cid, mib):
    return pltpu.CompilerParams(collective_id=cid, has_side_effects=True, vmem_limit_bytes=mib << 20)


def share(coef, forcing, base, labels, con, chw, basis):
    return pl.pallas_call(
        share_kernel, out_shape=(f32(16, 4, 8, 128), f32(3 * 48 * 48, 128), f32(3, 7, 48, 128), f32(2, 2, 3, 5, 8, 128), f32(NP * 256, 128)),
        in_specs=[VM, ANY, ANY, ANY, SM, SM, ANY], out_specs=(VM, VM, VM, VM, VM),
        scratch_shapes=[pltpu.SemaphoreType.DMA, vmem(1024, 128), vmem(1024, 128), pltpu.VMEM((1024, 128), jnp.int32), pltpu.SemaphoreType.DMA((3,)),
                        vmem(8, 128), vmem(8, 8, 128), vmem(2, 3, 2, 32, 128), vmem(2, 3, 2, 32, 128), vmem(4, 3, 5, 32, 128),
                        vmem(2, 3, 5, 32, 128), vmem(2, 3, 5, 32, 128),
                        pltpu.SemaphoreType.DMA((19,)), pltpu.SemaphoreType.DMA((19,))],
        compiler_params=params(0, 41), name="share")(coef, forcing, base, labels, con, chw, basis)


def merge(T, G0, yk):
    return pl.pallas_call(
        merge_kernel, out_shape=(f32(48, 48, 128), f32(2, 7, 48, 128), f32(3, 7, 48, 128), f32(2, 2, 3, 5, 8, 128)),
        in_specs=[VM, VM, VM], out_specs=(VM, VM, VM, VM),
        scratch_shapes=[vmem(2, 3, 2, 32, 128), vmem(2, 3, 7, 8, 128), vmem(2, 2, 3, 5, 8, 128),
                        vmem(2, 5, 40, 128), vmem(2, 5, 40, 128), vmem(2, 9, 48, 128), vmem(2, 2, 2, 48, 128),
                        vmem(2, 384, 128), vmem(2, 384, 128), vmem(2, 128, 128), vmem(2, 128, 128),
                        pltpu.SemaphoreType.DMA((16,)), pltpu.SemaphoreType.DMA((16,))],
        compiler_params=params(1, 14), name="merge")(T, G0, yk)


def fold(T, C):
    return pl.pallas_call(
        fold_kernel, out_shape=f32(1024, 128), in_specs=[VM, VM], out_specs=VM,
        scratch_shapes=[vmem(52, 48, 128), vmem(2, 3, 40, 128), vmem(2, 3, 40, 128), vmem(2, 4, 48, 128),
                        vmem(2, 128, 128), vmem(2, 128, 128),
                        pltpu.SemaphoreType.DMA((6,)), pltpu.SemaphoreType.DMA((6,))],
        compiler_params=params(2, 12), name="fold")(T, C)


def prolong_kernel(live_ref, off, link, gat, buf, acc):
    live = jnp.clip(live_ref[0], 0, NP)
    acc[...] = jnp.zeros_like(acc)
    lane, sub = lanes_sub()
    ix, iy, iz = lax.axis_index("gx"), lax.axis_index("gy"), lax.axis_index("gz")

    def values(p):
        jx, jy, jz = ix + link[0, p] - 1, iy + link[1, p] - 1, iz + link[2, p] - 1
        owner = jnp.clip((jx * 4 + jy) * 8 + jz, 0, 127)
        spot = jnp.clip(link[3, p], 0, ND - 1) + 64 * lax.rem(owner, 2)
        cell = rot(gat[owner // 8, lax.rem(owner // 2, 4)], lax.rem(128 - spot, 128))
        cell = jnp.broadcast_to(cell[:, 0:1], (8, 128)) * jnp.where(p < live, 1.0, 0.0)
        ck = [jnp.broadcast_to(cell[k : k + 1, :], (8, 128)) for k in range(NB)]
        vs = {}
        for yh in range(2):
            for xo in range(2):
                t = [ck[k] * buf[pl.ds(p * 256 + 128 * xo + 8 * yh + k, 8, stride=16), :] for k in range(NB)]
                vs[yh, xo] = ((t[0] + t[1]) + (t[2] + t[3])) + ((t[4] + t[5]) + (t[6] + t[7]))
        return vs

    def body(g, c):
        pieces = [g * FEW + j for j in range(FEW)]
        every = [values(p) for p in pieces]
        for p, vs in zip(pieces, every):
            ox, oy, tile, lo = corner(off, p)
            inwin = (lane >= lo) & (lane < lo + 16)
            new = []
            for (yh, xo), v in vs.items():
                for yl in range(8):
                    r = rot(v, lax.rem(lo - 16 * yl + 128, 128))
                    spot = (tile, oy + 4 + 8 * yh + yl, pl.ds(ox + 4 + 8 * xo, 8), slice(None))
                    new.append((spot, acc[spot] + jnp.where(inwin, r, 0.0)))
            for spot, value in new:
                acc[spot] = value
        return c

    lax.fori_loop(0, (live + FEW - 1) // FEW, body, 0)


def residual_stage(E0, G, Ec, Wc, xk, E, R, K, W, gk, C, gc, inner, sem):
    lane, sub = lanes_sub()
    whole = pltpu.make_async_copy(E0, E, sem)
    whole.start()
    near = (lane < 8) | (lane >= 120)

    def unpack(n, c):
        g, xo = n // 6, lax.rem(n, 6)
        rows = pl.ds(pl.multiple_of(8 * xo, 8), 8)
        gs, cs, ks = Wc[0, g, rows, :], Wc[1, g, rows, :], G[1, g, rows, :]
        for pos in range(8):
            ey = group_row(g, pos) + 4
            s = (120 - 16 * pos) % 128
            gc[ey, rows, :] = rot(gs, s)
            gk[ey, rows, :] = rot(ks, s)
            C[ey, rows, :] = Ec[jnp.clip(ey - 4, 0, 47), rows, :] + jnp.where(near, rot(cs, s), 0.0)
        return c

    lax.fori_loop(0, 42, unpack, 0)

    whole.wait()
    for f in range(3):
        for k in range(5):
            for d, y0 in ((0, 3), (1, 40)):
                E[pl.ds((48 * f + y0 + k) * 48, 8), :] = xk[0, d, f, k]
                E[pl.ds((48 * f + y0 + k) * 48 + 40, 8), :] = xk[1, d, f, k]

    def pair(cv, kv, nc, nk):
        inside = nk > 0.0
        return jnp.where(inside, 0.5 * (kv + nk) * (cv - nc), kv * cv)

    def build(n, c):
        g, xo = 1 + n // 5, lax.rem(n, 5)
        x0 = 4 + 8 * xo
        rows = pl.ds(x0, 8)

        def row(f, cy, dx):
            return E[pl.ds((48 * f + cy - 4) * 48 + x0 + dx, 8), :]

        gf, gw = G[0, g, rows, :], G[2, g, rows, :]
        for pos in range(8):
            ey = group_row(g, pos) + 4
            s = (120 - 16 * pos) % 128
            cv, gv = C[ey, rows, :], gc[ey, rows, :]
            kv, hv = row(1, ey, 0), gk[ey, rows, :]
            cu, cd, gu, gd = rot(cv, 127), rot(cv, 1), rot(gv, 127), rot(gv, 1)
            ku, kd, hu, hd = rot(kv, 127), rot(kv, 1), rot(hv, 127), rot(hv, 1)
            last, first = lane == 127, lane == 0
            r = row(0, ey, 0)
            r = r - pair(cv, kv, jnp.where(last, gu, cu), jnp.where(last, hu, ku))
            r = r - pair(cv, kv, jnp.where(first, gd, cd), jnp.where(first, hd, kd))
            q = rot(gf, s)
            q = q - pair(gv, hv, jnp.where(last, cu, gu), jnp.where(last, ku, hu))
            q = q - pair(gv, hv, jnp.where(first, cd, gd), jnp.where(first, kd, hd))
            for dy, dx in ((-1, 0), (1, 0), (0, -1), (0, 1)):
                rr = pl.ds(x0 + dx, 8)
                r = r - pair(cv, kv, C[ey + dy, rr, :], row(1, ey + dy, dx))
                q = q - pair(gv, hv, gc[ey + dy, rr, :], gk[ey + dy, rr, :])
            head, tail = lane < 4, lane >= 124
            py, px = ey - 8, pl.ds(pl.multiple_of(8 * xo, 8), 8)
            wv, gwv = row(2, ey, 0), rot(gw, s)
            for F, inn, out in ((R, r, q), (K, kv, hv), (W, wv, gwv)):
                F[0, py, px, :] = rot(jnp.where(tail, out, inn), 4)
                F[1, py, px, :] = rot(jnp.where(head, out, inn), 124)
        return c

    lax.fori_loop(0, 25, build, 0)

    def keep(y, c):
        inner[y] = C[y + 12, pl.ds(8, 32), :]
        return c

    lax.fori_loop(0, 32, keep, 0)


def enrich_kernel(live_ref, off, E0, G, Ec, Wc, xk, out, corr, inner, E, R, K, W, gk, C, gc, cbuf, vbuf, sem):
    residual_stage(E0, G, Ec, Wc, xk, E, R, K, W, gk, C, gc, inner, sem)
    live = jnp.clip(live_ref[0], 0, NP)
    corr[...] = jnp.zeros_like(corr)
    lane, sub = lanes_sub()
    group = lane // 16
    zpos = lane % 16
    zw = zpos < 15
    zg = zpos > 0
    yup = lane < 112
    ydn = lane >= 16
    xup = sub < 7
    xdn = sub > 0
    fz = zpos.astype(jnp.float32)
    def tentf(t):
        return (t + 0.5) * (PIECE - t - 0.5) * (4.0 / (PIECE * PIECE))
    tents = {}
    for xp in range(2):
        for yp in range(2):
            tents[xp, yp] = tentf((2*sub + xp).astype(jnp.float32)) * tentf((2*group + yp).astype(jnp.float32)) * tentf(fz)
    par = [(0,0),(0,1),(1,0),(1,1)]

    def prep(p, slot):
        ox, oy, tile, lo = corner(off, p)
        active = jnp.where(p < live, 1.0, 0.0)
        got = []
        for F in (R, K, W):
            d = {}
            for xp, yp in par:
                a = None
                for yh in range(8):
                    row = F[tile, oy + 2*yh + yp, pl.ds(ox + xp, 8, stride=2), :]
                    r = rot(row, lax.rem(16*yh - lo + 128, 128))
                    a = r if a is None else jnp.where(group == yh, r, a)
                d[xp, yp] = a
            got.append(d)
        r, k, w = got
        for i, (xp, yp) in enumerate(par):
            kc = k[xp, yp]
            nbs = [
                (rot(kc, 127), zw), (rot(kc, 1), zg),
                (k[xp, 1-yp], None),
                (rot(k[xp, 1-yp], 16 if yp == 0 else 112), ydn if yp == 0 else yup),
                (k[1-xp, yp], None),
                (rot(k[1-xp, yp], 1 if xp == 0 else 7, 0), xdn if xp == 0 else xup),
            ]
            diag = None
            cs = []
            inside = kc > 0.0
            for nb, m in nbs:
                ok = nb > 0.0
                if m is not None:
                    ok = ok & m
                face = jnp.where(ok, 0.5 * (kc + nb), kc)
                cs.append(jnp.where(ok & inside, face, 0.0))
                diag = face if diag is None else diag + face
            inv = jnp.where(inside, OMEGA / jnp.where(inside, diag, 1.0), 0.0)
            for j, cj in enumerate(cs):
                cbuf[slot, pl.ds((i*6 + j)*8, 8), :] = cj * inv
            b1 = r[xp, yp] * inv * active
            vbuf[slot, pl.ds(i*8, 8), :] = b1
            vbuf[slot, pl.ds((4+i)*8, 8), :] = b1 * w[xp, yp]

    def sweep_piece(vs, slot):
        res = []
        for s in range(2):
            v = {par[i]: vs[s*4+i] for i in range(4)}
            for i, (xp, yp) in enumerate(par):
                c = [cbuf[slot, pl.ds((i*6 + j)*8, 8), :] for j in range(6)]
                vc = v[xp, yp]
                t0 = vbuf[slot, pl.ds((4*s+i)*8, 8), :] + (1.0 - OMEGA) * vc
                t1 = c[0] * rot(vc, 127) + c[1] * rot(vc, 1)
                t2 = c[2] * v[xp, 1-yp] + c[3] * rot(v[xp, 1-yp], 16 if yp == 0 else 112)
                t3 = c[4] * v[1-xp, yp] + c[5] * rot(v[1-xp, yp], 1 if xp == 0 else 7, 0)
                res.append((t0 + t1) + (t2 + t3))
        return res

    idxs = [16*(4*yh2 + group//2) + zpos for yh2 in range(2)]
    gpar = (group % 2) == 0

    def body(g, c):
        for slot in range(PAIR):
            prep(g*PAIR + slot, slot)
        init = tuple(vbuf[slot, pl.ds(n*8, 8), :] for slot in range(PAIR) for n in range(8))
        def sweep(_, vs):
            o = []
            for slot in range(PAIR):
                o += sweep_piece(vs[slot*8:slot*8+8], slot)
            return tuple(o)
        vs = lax.fori_loop(0, SWEEPS - 1, sweep, init)
        for slot in range(PAIR):
            p = g*PAIR + slot
            ox, oy, tile, lo = corner(off, p)
            inwin = (lane >= lo) & (lane < lo + 16)
            v = vs[slot*8:slot*8+8]
            for s in range(2):
                for xp in range(2):
                    for yh2 in range(2):
                        e = jnp.take_along_axis(v[s*4 + 2*xp], idxs[yh2], axis=1)
                        o = jnp.take_along_axis(v[s*4 + 2*xp + 1], idxs[yh2], axis=1)
                        out[pl.ds(p*64 + 4*xp + 2*yh2 + s, 8, stride=8), :] = jnp.where(gpar, e, o)
            for i, (xp, yp) in enumerate(par):
                sp = tents[xp, yp] * (v[i] + v[4+i])
                new = []
                for yh in range(8):
                    rr = jnp.where(inwin, rot(sp, lax.rem(lo - 16*yh + 128, 128)), 0.0)
                    spot = (tile, oy + 4 + 2*yh + yp, pl.ds(ox + 4 + xp, 8, stride=2), slice(None))
                    new.append((spot, corr[spot] + rr))
                for spot, value in new:
                    corr[spot] = value
        return c
    ng = (live + PAIR - 1) // PAIR
    lax.fori_loop(0, ng, body, 0)
    def zero(p, c):
        out[pl.ds(p*64, 64), :] = jnp.zeros((64, 128), jnp.float32)
        return c
    lax.fori_loop(ng*PAIR, NP, zero, 0)


def prolong(live, off, link, gat, basis):
    return pl.pallas_call(
        prolong_kernel, out_shape=f32(2, 52, 48, 128), in_specs=[SM, SM, SM, VM, VM], out_specs=VM,
        compiler_params=pltpu.CompilerParams(vmem_limit_bytes=14 << 20), name="prolong")(live, off, link, gat, basis)


def enrich(live, off, E, G, Ec, Wc, xk):
    return pl.pallas_call(
        enrich_kernel, out_shape=(f32(NP * 64, 128), f32(2, 52, 48, 128), f32(32, 32, 128)),
        in_specs=[SM, SM, pl.BlockSpec(memory_space=pl.ANY), VM, VM, VM, VM], out_specs=(VM, VM, VM),
        scratch_shapes=[vmem(3 * 48 * 48, 128), vmem(2, 40, 40, 128), vmem(2, 40, 40, 128), vmem(2, 40, 40, 128),
                        vmem(56, 48, 128), vmem(56, 48, 128), vmem(56, 48, 128), vmem(PAIR, 192, 128), vmem(PAIR, 64, 128), pltpu.SemaphoreType.DMA],
        compiler_params=pltpu.CompilerParams(vmem_limit_bytes=30 << 20), name="enrich")(live, off, E, G, Ec, Wc, xk)


def basis_rows(rb):
    return rb.reshape(NP, NB, 32, 128).transpose(0, 2, 1, 3).reshape(NP * 256, 128)


def out_basis(o):
    return o.reshape(NP, 32, 2, 128).transpose(0, 2, 1, 3).reshape(1, 1, 1, NP, 2, 4096)


def local(forcing, kappa_base, labels, contrast, channel_weight, coarse_coef, source_link, offsets, live_pieces, resident_bases):
    live = live_pieces.reshape(1)
    off = offsets[0, 0].transpose(2, 0, 1)
    link = source_link[0, 0, 0].T
    gat, E, G0, yk, held = share(*(pltpu.with_memory_space_constraint(v, pltpu.HBM) for v in (
        coarse_coef[0, 0, 0].T, forcing.reshape(1024, 128), kappa_base.reshape(1024, 128), labels.reshape(1024, 128),
        contrast, channel_weight, basis_rows(resident_bases))))
    T = prolong(live, off, link, gat, held)
    Ec, Wc, G, xk = merge(T, G0, yk)
    out, corr, inner = enrich(live, off, E, G, Ec, Wc, xk)
    return fold(corr, inner).reshape(32, 32, 128), out_basis(out)


def solution(mesh):
    return jax.shard_map(
        local,
        mesh=mesh,
        in_specs=(
            P("gx", "gy", "gz"),
            P("gx", "gy", "gz"),
            P("gx", "gy", "gz"),
            P(),
            P(),
            P("gx", "gy", "gz", None, None),
            P("gx", "gy", "gz", None, None),
            P("gx", "gy", "gz", None, None),
            P("gx", "gy", "gz"),
            P("gx", "gy", "gz", None, None, None),
        ),
        out_specs=(P("gx", "gy", "gz"), P("gx", "gy", "gz", None, None, None)),
        check_vma=False,
    )
```

```python
import jax
import jax.numpy as jnp
from jax import lax
from jax.experimental import pallas as pl
from jax.experimental.pallas import tpu as pltpu
from jax.sharding import PartitionSpec as P

ND = 64
PIECE=16; NB=8; NP=40; SWEEPS=20
OMEGA = 2.0/3.0
PAIR = 10
FEW = 8
VM = pl.BlockSpec(memory_space=pltpu.VMEM)
SM = pl.BlockSpec(memory_space=pltpu.SMEM)
ANY = pl.BlockSpec(memory_space=pltpu.HBM)

def corner(off, p):
    ox = jnp.clip(off[0, 0, p], 0, 24)
    oy = jnp.clip(off[1, 0, p], 0, 24)
    oz = jnp.clip(off[2, 0, p], 0, 120)
    tile = (oz > 112).astype(jnp.int32)
    return ox, oy, tile, oz - 8 * tile

def rot(v, shift, axis=1):
    return pltpu.roll(v, shift, axis)

def lanes_sub():
    return lax.broadcasted_iota(jnp.int32, (8, 128), 1), lax.broadcasted_iota(jnp.int32, (8, 128), 0)

MESH = pl.DeviceIdType.MESH
SIZE = {"gx": 4, "gy": 4, "gz": 8}


def ring(axis, step):
    n = SIZE[axis]
    return lax.rem(lax.axis_index(axis) + (step + n), n)


def greet(pairs):
    barrier = pltpu.get_barrier_semaphore()
    for axis, step in pairs:
        pl.semaphore_signal(barrier, inc=1, device_id={axis: ring(axis, step)}, device_id_type=MESH)
    pl.semaphore_wait(barrier, len(pairs))


def remote(src, dst, send, recv, i, axis, step):
    copy = pltpu.make_async_remote_copy(
        src_ref=src, dst_ref=dst, send_sem=send.at[i], recv_sem=recv.at[i],
        device_id={axis: ring(axis, step)}, device_id_type=MESH,
    )
    copy.start()
    return copy


def edges(axis):
    i = lax.axis_index(axis)
    return (jnp.where(i > 0, 1.0, 0.0), jnp.where(i < SIZE[axis] - 1, 1.0, 0.0))


def group_row(g, pos):
    return 8 * g - 4 + pos


def share_kernel(coef, forcing0, base0, labels0, con, chw, basis, gat, E, G, yk, held, bsem, forcing, base, labels, isem, tile, col, zs, zr, yr, xs, xr, send, recv):
    ix, iy, iz = lax.axis_index("gx"), lax.axis_index("gy"), lax.axis_index("gz")
    lane, sub = lanes_sub()
    tile[...] = jnp.zeros_like(tile)
    tile[0:8, 0:64] = coef[...]
    fields = [pltpu.make_async_copy(a, b, isem.at[i]) for i, (a, b) in enumerate(((forcing0, forcing), (base0, base), (labels0, labels)))]
    for c in fields:
        c.start()
    fetch = pltpu.make_async_copy(basis, held, bsem)
    fetch.start()
    greet([("gz", s) for s in range(1, 8)] + [("gy", s) for s in range(1, 4)] + [("gx", s) for s in range(1, 4)])
    g1 = [remote(tile, col.at[iz], send, recv, s - 1, "gz", s) for s in range(1, 8)]
    col[iz] = tile[...]

    for c in fields:
        c.wait()

    def fill(x, c):
        for yo in range(4):
            rows = pl.ds(pl.multiple_of(x * 32 + 8 * yo, 8), 8)
            lab = labels[rows, :]
            kappa = jnp.zeros((8, 128), jnp.float32)
            weight = jnp.zeros((8, 128), jnp.float32)
            for ch in range(4):
                kappa = jnp.where(lab == ch, con[ch], kappa)
                weight = jnp.where(lab == ch, chw[ch], weight)
            for f, v in enumerate((forcing[rows, :], base[rows, :] * kappa, weight)):
                E[pl.ds((48 * f + 8 + 8 * yo) * 48 + 8 + x, 8, stride=48), :] = v
                @pl.when(x >= 27)
                def _():
                    xs[0, f, x - 27, pl.ds(8 * yo, 8), :] = v
                @pl.when(x < 5)
                def _():
                    xs[1, f, x, pl.ds(8 * yo, 8), :] = v
        return c

    lax.fori_loop(0, 32, fill, 0, unroll=2)
    xm = [remote(xs.at[0], xr.at[0], send, recv, 7, "gx", 1), remote(xs.at[1], xr.at[1], send, recv, 8, "gx", -1)]

    def stagey(n, c):
        f, k = n // 5, lax.rem(n, 5)
        zs_hi = (48 * f + 35 + k) * 48 + 8
        zs_lo = (48 * f + 8 + k) * 48 + 8
        yr[0, f, k] = E[pl.ds(pl.multiple_of(zs_hi, 8), 32), :]
        yr[1, f, k] = E[pl.ds(pl.multiple_of(zs_lo, 8), 32), :]
        return c

    lax.fori_loop(0, 15, stagey, 0)
    yc = [remote(yr.at[0], yr.at[2], send, recv, 9, "gy", 1), remote(yr.at[1], yr.at[3], send, recv, 10, "gy", -1)]
    lane8 = lane // 8

    def packz(n, c):
        f, q, xo = n // 8, lax.rem(n // 4, 2), lax.rem(n, 4)
        top, bottom = None, None
        for i in range(16):
            v = E[pl.ds(pl.multiple_of((48 * f + 8 + 16 * q + i) * 48 + 8 + 8 * xo, 8), 8), :]
            hi = rot(v, (8 * i + 8) % 128)
            lo = rot(v, (8 * i) % 128) if i else v
            top = hi if i == 0 else jnp.where(lane8 == i, hi, top)
            bottom = lo if i == 0 else jnp.where(lane8 == i, lo, bottom)
        zs[0, f, q, pl.ds(pl.multiple_of(8 * xo, 8), 8), :] = top
        zs[1, f, q, pl.ds(pl.multiple_of(8 * xo, 8), 8), :] = bottom
        return c

    lax.fori_loop(0, 24, packz, 0)
    zc = [remote(zs.at[0], zr.at[0], send, recv, 11, "gz", 1), remote(zs.at[1], zr.at[1], send, recv, 12, "gz", -1)]
    for c in g1:
        c.wait()
    mine = ix * 4 + iy
    for h in range(4):
        gat[mine, h] = jnp.where(lane < 64, col[2 * h], rot(col[2 * h + 1], 64))
    g2 = [remote(gat.at[mine], gat.at[mine], send, recv, 12 + s, "gy", s) for s in range(1, 4)]

    my, py = edges("gy")
    mx, px = edges("gx")
    mz, pz = edges("gz")
    for c in yc:
        c.wait()
    for c in g2:
        c.wait()
    plane = pl.ds(ix * 4, 4)
    g3 = [remote(gat.at[plane], gat.at[plane], send, recv, 15 + s, "gx", s) for s in range(1, 4)]

    def addy(n, c):
        f, k = n // 5, lax.rem(n, 5)
        for d, y0, m in ((0, 3, my), (1, 40, py)):
            v = yr[2 + d, f, k] * m
            E[pl.ds(pl.multiple_of((48 * f + y0 + k) * 48 + 8, 8), 32), :] = v
            yk[0, d, f, k] = v[24:32, :]
            yk[1, d, f, k] = v[0:8, :]
        return c

    lax.fori_loop(0, 15, addy, 0)
    for c in xm:
        c.wait()

    def addx(n, c):
        f, k = n // 5, lax.rem(n, 5)
        for yo in range(4):
            E[pl.ds((48 * f + 8 + 8 * yo) * 48 + 3 + k, 8, stride=48), :] = xr[0, f, k, pl.ds(8 * yo, 8), :] * mx
            E[pl.ds((48 * f + 8 + 8 * yo) * 48 + 40 + k, 8, stride=48), :] = xr[1, f, k, pl.ds(8 * yo, 8), :] * px
        return c

    lax.fori_loop(0, 15, addx, 0)
    for c in zc:
        c.wait()
    lane16 = lane // 16
    low = lax.rem(lane, 16) < 8

    def windows(n, c):
        f, xo = n // 4, lax.rem(n, 4)
        rows = pl.ds(pl.multiple_of(8 * xo, 8), 8)
        src = [[zr[d, f, q, rows, :] * m for q in range(2)] for d, m in ((0, mz), (1, pz))]
        for g in range(1, 6):
            acc = jnp.zeros((8, 128), jnp.float32)
            for pos in range(8):
                y = group_row(g, pos) - 8
                if y < 0 or y > 31:
                    continue
                a = rot(src[0][y // 16], (16 * pos - 8 * (y % 16)) % 128)
                b = rot(src[1][y // 16], (16 * pos + 8 - 8 * (y % 16)) % 128)
                acc = jnp.where(lane16 == pos, jnp.where(low, a, b), acc)
            G[f, g, pl.ds(pl.multiple_of(8 + 8 * xo, 8), 8), :] = acc
        return c

    lax.fori_loop(0, 12, windows, 0)
    for c in g3:
        c.wait()
    fetch.wait()


HALO = [("gy", 1), ("gy", -1), ("gx", 1), ("gx", -1), ("gz", 1), ("gz", -1)]


def split_rows(T, ey, rows):
    lane, _ = lanes_sub()
    t0 = rot(T[0, ey, rows, :], 124)
    t1 = rot(T[1, ey, rows, :], 4)
    a = jnp.where(lane < 124, t0, 0.0) + jnp.where(lane >= 4, t1, 0.0)
    m = jnp.where(lane >= 124, t0, jnp.where(lane < 4, t1, 0.0))
    return a, m


def merge_kernel(T, G0, yk, E, W, G, xk, yg, xg, kr, zs, zr, yr, yw, xs, xr, xws, xwr, send, recv):
    greet(HALO)
    cc = [remote(yk.at[0], kr.at[0], send, recv, 10, "gx", 1), remote(yk.at[1], kr.at[1], send, recv, 11, "gx", -1)]
    gc = [remote(G0.at[:, pl.ds(4, 2), pl.ds(8, 32)], yg.at[0], send, recv, 12, "gy", 1),
          remote(G0.at[:, pl.ds(1, 2), pl.ds(8, 32)], yg.at[1], send, recv, 13, "gy", -1)]
    lane, sub = lanes_sub()
    lane16 = lane // 16
    low = lax.rem(lane, 16) < 8
    E[3] = jnp.zeros((48, 128), jnp.float32)
    E[44] = jnp.zeros((48, 128), jnp.float32)
    side = jnp.zeros((41, 8, 128), jnp.float32)
    E[pl.ds(4, 41), pl.ds(0, 8), :] = side
    E[pl.ds(4, 41), pl.ds(40, 8), :] = side
    W[:, :, pl.ds(0, 8), :] = jnp.zeros((2, 7, 8, 128), jnp.float32)
    W[:, :, pl.ds(40, 8), :] = jnp.zeros((2, 7, 8, 128), jnp.float32)

    def build(n, c):
        g, xo = 1 + n // 5, lax.rem(n, 5)
        rows, near = pl.ds(4 + 8 * xo, 8), pl.ds(pl.multiple_of(8 * xo, 8), 8)
        nxt, prv, own = None, None, None
        for pos in range(8):
            ey = 8 * g - 4 + pos
            a, m = split_rows(T, ey, rows)
            E[ey, rows, :] = a
            ra = rot(a, (16 * pos + 8) % 128)
            rm = rot(m, (16 * pos + 8) % 128)
            s0, s1 = jnp.where(low, ra, rm), jnp.where(low, rm, ra)
            if pos == 0:
                nxt, prv, own = s0, s1, rm
            else:
                hit = lane16 == pos
                nxt, prv, own = jnp.where(hit, s0, nxt), jnp.where(hit, s1, prv), jnp.where(hit, rm, own)
        zs[0, g - 1, near, :] = nxt
        zs[1, g - 1, near, :] = prv
        W[0, g, rows, :] = own
        return c

    lax.fori_loop(0, 25, build, 0)
    zc = [remote(zs.at[0], zr.at[0], send, recv, 2, "gz", 1), remote(zs.at[1], zr.at[1], send, recv, 3, "gz", -1)]
    yc = [remote(E.at[pl.ds(35, 9)], yr.at[0], send, recv, 0, "gy", 1), remote(E.at[pl.ds(4, 9)], yr.at[1], send, recv, 1, "gy", -1)]
    my, py = edges("gy")
    mz, pz = edges("gz")
    mx, px = edges("gx")
    for c in gc:
        c.wait()
    inner = pl.ds(8, 32)
    for f in range(3):
        G[f, 0, inner, :] = yg[0, f, 0] * my
        G[f, 1, inner, :] = G0[f, 1, inner, :] + yg[0, f, 1] * my
        for g in (2, 3, 4):
            G[f, g, inner, :] = G0[f, g, inner, :]
        G[f, 5, inner, :] = G0[f, 5, inner, :] + yg[1, f, 0] * py
        G[f, 6, inner, :] = yg[1, f, 1] * py
    hc = [remote(G.at[:, :, pl.ds(32, 8)], xg.at[0], send, recv, 14, "gx", 1), remote(G.at[:, :, pl.ds(8, 8)], xg.at[1], send, recv, 15, "gx", -1)]
    for c in yc:
        c.wait()
    def addy(k, c):
        E[3 + k] += yr[0, k] * my
        E[36 + k] += yr[1, k] * py
        return c
    lax.fori_loop(0, 9, addy, 0)
    def stage(y, c):
        xs[0, pl.ds(y * 9, 9), :] = E[3 + y, pl.ds(35, 9), :]
        xs[1, pl.ds(y * 9, 9), :] = E[3 + y, pl.ds(4, 9), :]
        return c
    lax.fori_loop(0, 42, stage, 0, unroll=6)
    xc = [remote(xs.at[0], xr.at[0], send, recv, 4, "gx", 1), remote(xs.at[1], xr.at[1], send, recv, 5, "gx", -1)]
    for c in zc:
        c.wait()
    def windows(n, c):
        g, xo = n // 5, lax.rem(n, 5)
        rows, near = pl.ds(4 + 8 * xo, 8), pl.ds(pl.multiple_of(8 * xo, 8), 8)
        x, y = zr[0, g, near, :] * mz, zr[1, g, near, :] * pz
        W[0, g + 1, rows, :] += jnp.where(low, x, y)
        W[1, g + 1, rows, :] = jnp.where(low, y, x)
        return c
    lax.fori_loop(0, 25, windows, 0, unroll=5)
    wc = [remote(W.at[:, pl.ds(4, 2)], yw.at[0], send, recv, 6, "gy", 1), remote(W.at[:, pl.ds(1, 2)], yw.at[1], send, recv, 7, "gy", -1)]
    for c in wc:
        c.wait()
    for w in range(2):
        for k in range(2):
            a, b = yw[0, w, k] * my, yw[1, w, k] * py
            W[w, k] = a if k == 0 else W[w, k] + a
            W[w, 5 + k] = b if k == 1 else W[w, 5 + k] + b
    def stagew(n, c):
        w, g = n // 7, lax.rem(n, 7)
        xws[0, pl.ds(n * 9, 9), :] = W[w, g, pl.ds(35, 9), :]
        xws[1, pl.ds(n * 9, 9), :] = W[w, g, pl.ds(4, 9), :]
        return c
    lax.fori_loop(0, 14, stagew, 0, unroll=7)
    vc = [remote(xws.at[0], xwr.at[0], send, recv, 8, "gx", 1), remote(xws.at[1], xwr.at[1], send, recv, 9, "gx", -1)]
    for c in cc + hc:
        c.wait()
    for d in range(2):
        for f in range(3):
            for k in range(5):
                xk[0, d, f, k] = kr[0, d, f, k] * mx
                xk[1, d, f, k] = kr[1, d, f, k] * px
    for f in range(3):
        for g in range(7):
            G[f, g, pl.ds(0, 8), :] = xg[0, f, g] * mx
            G[f, g, pl.ds(40, 8), :] = xg[1, f, g] * px
    for c in xc:
        c.wait()
    def unstage(y, c):
        E[3 + y, pl.ds(3, 9), :] += xr[0, pl.ds(y * 9, 9), :] * mx
        E[3 + y, pl.ds(36, 9), :] += xr[1, pl.ds(y * 9, 9), :] * px
        return c
    lax.fori_loop(0, 42, unstage, 0, unroll=6)
    for c in vc:
        c.wait()
    def unstagew(n, c):
        w, g = n // 7, lax.rem(n, 7)
        W[w, g, pl.ds(3, 9), :] += xwr[0, pl.ds(n * 9, 9), :] * mx
        W[w, g, pl.ds(36, 9), :] += xwr[1, pl.ds(n * 9, 9), :] * px
        return c
    lax.fori_loop(0, 14, unstagew, 0, unroll=7)


def fold_kernel(T, C, upd, E, zs, zr, yr, xs, xr, send, recv):
    greet(HALO)
    lane, sub = lanes_sub()
    lane8 = lane // 8

    def build(n, c):
        q, xo = n // 5, lax.rem(n, 5)
        rows, near = pl.ds(4 + 8 * xo, 8), pl.ds(pl.multiple_of(8 * xo, 8), 8)
        nxt, prv = None, None
        for i in range(16):
            ey = 4 + 16 * q + i
            a, m = split_rows(T, ey, rows)
            E[ey, rows, :] = a
            hi = rot(m, (8 * i) % 128) if i else m
            lo = rot(m, (8 * i + 8) % 128)
            nxt = hi if i == 0 else jnp.where(lane8 == i, hi, nxt)
            prv = lo if i == 0 else jnp.where(lane8 == i, lo, prv)
        zs[0, q, near, :] = nxt
        zs[1, q, near, :] = prv
        return c

    lax.fori_loop(0, 15, build, 0)
    zc = [remote(zs.at[0], zr.at[0], send, recv, 0, "gz", 1), remote(zs.at[1], zr.at[1], send, recv, 1, "gz", -1)]
    my, py = edges("gy")
    mz, pz = edges("gz")
    mx, px = edges("gx")
    for c in zc:
        c.wait()
    def addz(n, c):
        q, xo = n // 5, lax.rem(n, 5)
        rows, near = pl.ds(4 + 8 * xo, 8), pl.ds(pl.multiple_of(8 * xo, 8), 8)
        x, y = zr[0, q, near, :] * mz, zr[1, q, near, :] * pz
        for i in range(16):
            a = rot(x, (128 - 8 * i) % 128) if i else x
            b = rot(y, (120 - 8 * i) % 128)
            E[4 + 16 * q + i, rows, :] += jnp.where(lane < 8, a, jnp.where(lane >= 120, b, 0.0))
        return c
    lax.fori_loop(0, 15, addz, 0)
    yc = [remote(E.at[pl.ds(40, 4)], yr.at[0], send, recv, 2, "gy", 1), remote(E.at[pl.ds(4, 4)], yr.at[1], send, recv, 3, "gy", -1)]
    for c in yc:
        c.wait()
    for k in range(4):
        E[8 + k] += yr[0, k] * my
        E[36 + k] += yr[1, k] * py
    def stage(y, c):
        xs[0, pl.ds(y * 4, 4), :] = E[8 + y, pl.ds(40, 4), :]
        xs[1, pl.ds(y * 4, 4), :] = E[8 + y, pl.ds(4, 4), :]
        return c
    lax.fori_loop(0, 32, stage, 0, unroll=8)
    xc = [remote(xs.at[0], xr.at[0], send, recv, 4, "gx", 1), remote(xs.at[1], xr.at[1], send, recv, 5, "gx", -1)]
    for c in xc:
        c.wait()
    def finish(y, c):
        E[8 + y, pl.ds(8, 4), :] += xr[0, pl.ds(y * 4, 4), :] * mx
        E[8 + y, pl.ds(36, 4), :] += xr[1, pl.ds(y * 4, 4), :] * px
        for xo in range(4):
            upd[pl.ds(xo * 256 + y, 8, stride=32), :] = C[y, pl.ds(8 * xo, 8), :] + E[8 + y, pl.ds(8 + 8 * xo, 8), :]
        return c
    lax.fori_loop(0, 32, finish, 0, unroll=4)


def f32(*shape):
    return jax.ShapeDtypeStruct(shape, jnp.float32)


def vmem(*shape):
    return pltpu.VMEM(shape, jnp.float32)


def params(cid, mib):
    return pltpu.CompilerParams(collective_id=cid, has_side_effects=True, vmem_limit_bytes=mib << 20)


def share(coef, forcing, base, labels, con, chw, basis):
    return pl.pallas_call(
        share_kernel, out_shape=(f32(16, 4, 8, 128), f32(3 * 48 * 48, 128), f32(3, 7, 48, 128), f32(2, 2, 3, 5, 8, 128), f32(NP * 256, 128)),
        in_specs=[VM, ANY, ANY, ANY, SM, SM, ANY], out_specs=(VM, VM, VM, VM, VM),
        scratch_shapes=[pltpu.SemaphoreType.DMA, vmem(1024, 128), vmem(1024, 128), pltpu.VMEM((1024, 128), jnp.int32), pltpu.SemaphoreType.DMA((3,)),
                        vmem(8, 128), vmem(8, 8, 128), vmem(2, 3, 2, 32, 128), vmem(2, 3, 2, 32, 128), vmem(4, 3, 5, 32, 128),
                        vmem(2, 3, 5, 32, 128), vmem(2, 3, 5, 32, 128),
                        pltpu.SemaphoreType.DMA((19,)), pltpu.SemaphoreType.DMA((19,))],
        compiler_params=params(0, 41), name="share")(coef, forcing, base, labels, con, chw, basis)


def merge(T, G0, yk):
    return pl.pallas_call(
        merge_kernel, out_shape=(f32(48, 48, 128), f32(2, 7, 48, 128), f32(3, 7, 48, 128), f32(2, 2, 3, 5, 8, 128)),
        in_specs=[VM, VM, VM], out_specs=(VM, VM, VM, VM),
        scratch_shapes=[vmem(2, 3, 2, 32, 128), vmem(2, 3, 7, 8, 128), vmem(2, 2, 3, 5, 8, 128),
                        vmem(2, 5, 40, 128), vmem(2, 5, 40, 128), vmem(2, 9, 48, 128), vmem(2, 2, 2, 48, 128),
                        vmem(2, 384, 128), vmem(2, 384, 128), vmem(2, 128, 128), vmem(2, 128, 128),
                        pltpu.SemaphoreType.DMA((16,)), pltpu.SemaphoreType.DMA((16,))],
        compiler_params=params(1, 14), name="merge")(T, G0, yk)


def fold(T, C):
    return pl.pallas_call(
        fold_kernel, out_shape=f32(1024, 128), in_specs=[VM, VM], out_specs=VM,
        scratch_shapes=[vmem(52, 48, 128), vmem(2, 3, 40, 128), vmem(2, 3, 40, 128), vmem(2, 4, 48, 128),
                        vmem(2, 128, 128), vmem(2, 128, 128),
                        pltpu.SemaphoreType.DMA((6,)), pltpu.SemaphoreType.DMA((6,))],
        compiler_params=params(2, 12), name="fold")(T, C)


def prolong_kernel(live_ref, off, link, gat, buf, acc):
    live = jnp.clip(live_ref[0], 0, NP)
    acc[...] = jnp.zeros_like(acc)
    lane, sub = lanes_sub()
    ix, iy, iz = lax.axis_index("gx"), lax.axis_index("gy"), lax.axis_index("gz")

    def values(p):
        jx, jy, jz = ix + link[0, p] - 1, iy + link[1, p] - 1, iz + link[2, p] - 1
        owner = jnp.clip((jx * 4 + jy) * 8 + jz, 0, 127)
        spot = jnp.clip(link[3, p], 0, ND - 1) + 64 * lax.rem(owner, 2)
        cell = rot(gat[owner // 8, lax.rem(owner // 2, 4)], lax.rem(128 - spot, 128))
        cell = jnp.broadcast_to(cell[:, 0:1], (8, 128)) * jnp.where(p < live, 1.0, 0.0)
        ck = [jnp.broadcast_to(cell[k : k + 1, :], (8, 128)) for k in range(NB)]
        vs = {}
        for yh in range(2):
            for xo in range(2):
                t = [ck[k] * buf[pl.ds(p * 256 + 128 * xo + 8 * yh + k, 8, stride=16), :] for k in range(NB)]
                vs[yh, xo] = ((t[0] + t[1]) + (t[2] + t[3])) + ((t[4] + t[5]) + (t[6] + t[7]))
        return vs

    def body(g, c):
        pieces = [g * FEW + j for j in range(FEW)]
        every = [values(p) for p in pieces]
        for p, vs in zip(pieces, every):
            ox, oy, tile, lo = corner(off, p)
            inwin = (lane >= lo) & (lane < lo + 16)
            new = []
            for (yh, xo), v in vs.items():
                for yl in range(8):
                    r = rot(v, lax.rem(lo - 16 * yl + 128, 128))
                    spot = (tile, oy + 4 + 8 * yh + yl, pl.ds(ox + 4 + 8 * xo, 8), slice(None))
                    new.append((spot, acc[spot] + jnp.where(inwin, r, 0.0)))
            for spot, value in new:
                acc[spot] = value
        return c

    lax.fori_loop(0, (live + FEW - 1) // FEW, body, 0)


def residual_stage(E, G, Ec, Wc, xk, R, K, W, gk, C, gc, inner):
    lane, sub = lanes_sub()
    near = (lane < 8) | (lane >= 120)

    def unpack(n, c):
        g, xo = n // 6, lax.rem(n, 6)
        rows = pl.ds(pl.multiple_of(8 * xo, 8), 8)
        gs, cs, ks = Wc[0, g, rows, :], Wc[1, g, rows, :], G[1, g, rows, :]
        for pos in range(8):
            ey = group_row(g, pos) + 4
            s = (120 - 16 * pos) % 128
            gc[ey, rows, :] = rot(gs, s)
            gk[ey, rows, :] = rot(ks, s)
            C[ey, rows, :] = Ec[jnp.clip(ey - 4, 0, 47), rows, :] + jnp.where(near, rot(cs, s), 0.0)
        return c

    lax.fori_loop(0, 42, unpack, 0)

    for f in range(3):
        for k in range(5):
            for d, y0 in ((0, 3), (1, 40)):
                E[pl.ds((48 * f + y0 + k) * 48, 8), :] = xk[0, d, f, k]
                E[pl.ds((48 * f + y0 + k) * 48 + 40, 8), :] = xk[1, d, f, k]

    def pair(cv, kv, nc, nk):
        inside = nk > 0.0
        return jnp.where(inside, 0.5 * (kv + nk) * (cv - nc), kv * cv)

    def build(n, c):
        g, xo = 1 + n // 5, lax.rem(n, 5)
        x0 = 4 + 8 * xo
        rows = pl.ds(x0, 8)

        def row(f, cy, dx):
            return E[pl.ds((48 * f + cy - 4) * 48 + x0 + dx, 8), :]

        gf, gw = G[0, g, rows, :], G[2, g, rows, :]
        for pos in range(8):
            ey = group_row(g, pos) + 4
            s = (120 - 16 * pos) % 128
            cv, gv = C[ey, rows, :], gc[ey, rows, :]
            kv, hv = row(1, ey, 0), gk[ey, rows, :]
            cu, cd, gu, gd = rot(cv, 127), rot(cv, 1), rot(gv, 127), rot(gv, 1)
            ku, kd, hu, hd = rot(kv, 127), rot(kv, 1), rot(hv, 127), rot(hv, 1)
            last, first = lane == 127, lane == 0
            r = row(0, ey, 0)
            r = r - pair(cv, kv, jnp.where(last, gu, cu), jnp.where(last, hu, ku))
            r = r - pair(cv, kv, jnp.where(first, gd, cd), jnp.where(first, hd, kd))
            q = rot(gf, s)
            q = q - pair(gv, hv, jnp.where(last, cu, gu), jnp.where(last, ku, hu))
            q = q - pair(gv, hv, jnp.where(first, cd, gd), jnp.where(first, kd, hd))
            for dy, dx in ((-1, 0), (1, 0), (0, -1), (0, 1)):
                rr = pl.ds(x0 + dx, 8)
                r = r - pair(cv, kv, C[ey + dy, rr, :], row(1, ey + dy, dx))
                q = q - pair(gv, hv, gc[ey + dy, rr, :], gk[ey + dy, rr, :])
            head, tail = lane < 4, lane >= 124
            py, px = ey - 8, pl.ds(pl.multiple_of(8 * xo, 8), 8)
            wv, gwv = row(2, ey, 0), rot(gw, s)
            for F, inn, out in ((R, r, q), (K, kv, hv), (W, wv, gwv)):
                F[0, py, px, :] = rot(jnp.where(tail, out, inn), 4)
                F[1, py, px, :] = rot(jnp.where(head, out, inn), 124)
        return c

    lax.fori_loop(0, 25, build, 0)

    def keep(y, c):
        inner[y] = C[y + 12, pl.ds(8, 32), :]
        return c

    lax.fori_loop(0, 32, keep, 0)


def enrich_kernel(live_ref, off, E, G, Ec, Wc, xk, out, corr, inner, R, K, W, gk, C, gc, cbuf, vbuf):
    residual_stage(E, G, Ec, Wc, xk, R, K, W, gk, C, gc, inner)
    live = jnp.clip(live_ref[0], 0, NP)
    corr[...] = jnp.zeros_like(corr)
    lane, sub = lanes_sub()
    group = lane // 16
    zpos = lane % 16
    zw = zpos < 15
    zg = zpos > 0
    yup = lane < 112
    ydn = lane >= 16
    xup = sub < 7
    xdn = sub > 0
    fz = zpos.astype(jnp.float32)
    def tentf(t):
        return (t + 0.5) * (PIECE - t - 0.5) * (4.0 / (PIECE * PIECE))
    tents = {}
    for xp in range(2):
        for yp in range(2):
            tents[xp, yp] = tentf((2*sub + xp).astype(jnp.float32)) * tentf((2*group + yp).astype(jnp.float32)) * tentf(fz)
    par = [(0,0),(0,1),(1,0),(1,1)]

    def prep(p, slot):
        ox, oy, tile, lo = corner(off, p)
        active = jnp.where(p < live, 1.0, 0.0)
        got = []
        for F in (R, K, W):
            d = {}
            for xp, yp in par:
                a = None
                for yh in range(8):
                    row = F[tile, oy + 2*yh + yp, pl.ds(ox + xp, 8, stride=2), :]
                    r = rot(row, lax.rem(16*yh - lo + 128, 128))
                    a = r if a is None else jnp.where(group == yh, r, a)
                d[xp, yp] = a
            got.append(d)
        r, k, w = got
        for i, (xp, yp) in enumerate(par):
            kc = k[xp, yp]
            nbs = [
                (rot(kc, 127), zw), (rot(kc, 1), zg),
                (k[xp, 1-yp], None),
                (rot(k[xp, 1-yp], 16 if yp == 0 else 112), ydn if yp == 0 else yup),
                (k[1-xp, yp], None),
                (rot(k[1-xp, yp], 1 if xp == 0 else 7, 0), xdn if xp == 0 else xup),
            ]
            diag = None
            cs = []
            inside = kc > 0.0
            for nb, m in nbs:
                ok = nb > 0.0
                if m is not None:
                    ok = ok & m
                face = jnp.where(ok, 0.5 * (kc + nb), kc)
                cs.append(jnp.where(ok & inside, face, 0.0))
                diag = face if diag is None else diag + face
            inv = jnp.where(inside, OMEGA / jnp.where(inside, diag, 1.0), 0.0)
            for j, cj in enumerate(cs):
                cbuf[slot, pl.ds((i*6 + j)*8, 8), :] = cj * inv
            b1 = r[xp, yp] * inv * active
            vbuf[slot, pl.ds(i*8, 8), :] = b1
            vbuf[slot, pl.ds((4+i)*8, 8), :] = b1 * w[xp, yp]

    def sweep_piece(vs, slot):
        res = []
        for s in range(2):
            v = {par[i]: vs[s*4+i] for i in range(4)}
            for i, (xp, yp) in enumerate(par):
                c = [cbuf[slot, pl.ds((i*6 + j)*8, 8), :] for j in range(6)]
                vc = v[xp, yp]
                t0 = vbuf[slot, pl.ds((4*s+i)*8, 8), :] + (1.0 - OMEGA) * vc
                t1 = c[0] * rot(vc, 127) + c[1] * rot(vc, 1)
                t2 = c[2] * v[xp, 1-yp] + c[3] * rot(v[xp, 1-yp], 16 if yp == 0 else 112)
                t3 = c[4] * v[1-xp, yp] + c[5] * rot(v[1-xp, yp], 1 if xp == 0 else 7, 0)
                res.append((t0 + t1) + (t2 + t3))
        return res

    idxs = [16*(4*yh2 + group//2) + zpos for yh2 in range(2)]
    gpar = (group % 2) == 0

    def body(g, c):
        for slot in range(PAIR):
            prep(g*PAIR + slot, slot)
        init = tuple(vbuf[slot, pl.ds(n*8, 8), :] for slot in range(PAIR) for n in range(8))
        def sweep(_, vs):
            o = []
            for slot in range(PAIR):
                o += sweep_piece(vs[slot*8:slot*8+8], slot)
            return tuple(o)
        vs = lax.fori_loop(0, SWEEPS - 1, sweep, init)
        for slot in range(PAIR):
            p = g*PAIR + slot
            ox, oy, tile, lo = corner(off, p)
            inwin = (lane >= lo) & (lane < lo + 16)
            v = vs[slot*8:slot*8+8]
            for s in range(2):
                for xp in range(2):
                    for yh2 in range(2):
                        e = jnp.take_along_axis(v[s*4 + 2*xp], idxs[yh2], axis=1)
                        o = jnp.take_along_axis(v[s*4 + 2*xp + 1], idxs[yh2], axis=1)
                        out[pl.ds(p*64 + 4*xp + 2*yh2 + s, 8, stride=8), :] = jnp.where(gpar, e, o)
            for i, (xp, yp) in enumerate(par):
                sp = tents[xp, yp] * (v[i] + v[4+i])
                new = []
                for yh in range(8):
                    rr = jnp.where(inwin, rot(sp, lax.rem(lo - 16*yh + 128, 128)), 0.0)
                    spot = (tile, oy + 4 + 2*yh + yp, pl.ds(ox + 4 + xp, 8, stride=2), slice(None))
                    new.append((spot, corr[spot] + rr))
                for spot, value in new:
                    corr[spot] = value
        return c
    ng = (live + PAIR - 1) // PAIR
    lax.fori_loop(0, ng, body, 0)
    def zero(p, c):
        out[pl.ds(p*64, 64), :] = jnp.zeros((64, 128), jnp.float32)
        return c
    lax.fori_loop(ng*PAIR, NP, zero, 0)


def prolong(live, off, link, gat, basis):
    return pl.pallas_call(
        prolong_kernel, out_shape=f32(2, 52, 48, 128), in_specs=[SM, SM, SM, VM, VM], out_specs=VM,
        compiler_params=pltpu.CompilerParams(vmem_limit_bytes=14 << 20), name="prolong")(live, off, link, gat, basis)


def enrich(live, off, E, G, Ec, Wc, xk):
    return pl.pallas_call(
        enrich_kernel, out_shape=(f32(NP * 64, 128), f32(2, 52, 48, 128), f32(32, 32, 128)),
        in_specs=[SM, SM, VM, VM, VM, VM, VM], out_specs=(VM, VM, VM),
        scratch_shapes=[vmem(2, 40, 40, 128), vmem(2, 40, 40, 128), vmem(2, 40, 40, 128),
                        vmem(56, 48, 128), vmem(56, 48, 128), vmem(56, 48, 128), vmem(PAIR, 192, 128), vmem(PAIR, 64, 128)],
        compiler_params=pltpu.CompilerParams(vmem_limit_bytes=30 << 20), name="enrich")(live, off, E, G, Ec, Wc, xk)


def basis_rows(rb):
    return rb.reshape(NP, NB, 32, 128).transpose(0, 2, 1, 3).reshape(NP * 256, 128)


def out_basis(o):
    return o.reshape(NP, 32, 2, 128).transpose(0, 2, 1, 3).reshape(1, 1, 1, NP, 2, 4096)


def local(forcing, kappa_base, labels, contrast, channel_weight, coarse_coef, source_link, offsets, live_pieces, resident_bases):
    live = live_pieces.reshape(1)
    off = offsets[0, 0].transpose(2, 0, 1)
    link = source_link[0, 0, 0].T
    gat, E, G0, yk, held = share(*(pltpu.with_memory_space_constraint(v, pltpu.HBM) for v in (
        coarse_coef[0, 0, 0].T, forcing.reshape(1024, 128), kappa_base.reshape(1024, 128), labels.reshape(1024, 128),
        contrast, channel_weight, basis_rows(resident_bases))))
    T = prolong(live, off, link, gat, held)
    Ec, Wc, G, xk = merge(T, G0, yk)
    out, corr, inner = enrich(live, off, E, G, Ec, Wc, xk)
    return fold(corr, inner).reshape(32, 32, 128), out_basis(out)


def solution(mesh):
    return jax.shard_map(
        local,
        mesh=mesh,
        in_specs=(
            P("gx", "gy", "gz"),
            P("gx", "gy", "gz"),
            P("gx", "gy", "gz"),
            P(),
            P(),
            P("gx", "gy", "gz", None, None),
            P("gx", "gy", "gz", None, None),
            P("gx", "gy", "gz", None, None),
            P("gx", "gy", "gz"),
            P("gx", "gy", "gz", None, None, None),
        ),
        out_specs=(P("gx", "gy", "gz"), P("gx", "gy", "gz", None, None, None)),
        check_vma=False,
    )
```
